32 devices in a mesh: seq: 8 (over z, x), tp: 4 (over y, core).
Axes of the slice: x: 2, y: 2, z: 4, core: 2. Of those that a mesh axis runs over, the one named last changes fastest.
Arguments:
- inputs: bfloat16 [2, 3584, 1024], P(None, 'seq'), may hold values from -6 to 6
- memory: bfloat16 [2, 3584, 1024], P(None, 'seq'), may hold values from -6 to 6
- compressed: bfloat16 [2, 3584, 1024], P(None, 'seq'), may hold values from -6 to 6
- boundary: int32 [2, 7], replicated, may hold values from 0 to 512
- links: int32 [2, 7], replicated, may hold values 0 or 1
- gains: float32 [2, 1024], replicated, may hold values from 0.5 to 1.5
- shifts: float32 [2, 1024], replicated, may hold values from -3 to 3
- slopes: float32 [8], P('tp'), may hold values from 0.05 to 1.5
- w_query: bfloat16 [1024, 1024], P(None, 'tp'), may hold values from -0.1875 to 0.1875
- w_key: bfloat16 [1024, 1024], P(None, 'tp'), may hold values from -0.1875 to 0.1875
- w_value: bfloat16 [1024, 1024], P(None, 'tp'), may hold values from -0.1875 to 0.1875
- w_out: bfloat16 [1024, 1024], P('tp'), may hold values from -1 to 1
- w_in: bfloat16 [1024, 4096], P(None, 'tp'), may hold values from -0.1875 to 0.1875
- w_down: bfloat16 [4096, 1024], P('tp'), may hold values from -0.09375 to 0.09375
- w_comp: bfloat16 [3, 1024, 1024], P(None, None, 'tp'), may hold values from -0.109375 to 0.109375
- cot_out: bfloat16 [2, 3584, 1024], P(None, 'seq'), may hold values from -6 to 6
- cot_new: bfloat16 [2, 1232, 1024], P(None, 'seq', 'tp'), may hold values from -6 to 6
Outputs:
- out: bfloat16 [2, 3584, 1024], P(None, 'seq')
- d_input: float32 [2, 3584, 1024], P(None, 'seq')
- d_memory: float32 [2, 3584, 1024], P(None, 'seq')
- d_compressed: float32 [2, 3584, 1024], P(None, 'seq')
- new_compressed: float32 [2, 1232, 1024], P(None, 'seq', 'tp')
- g_gains: float32 [2, 1024], P(None, 'seq')
- g_shifts: float32 [2, 1024], P(None, 'seq')
- g_slopes: float32 [8], P('tp')
- g_query: float32 [1024, 1024], P('seq', 'tp')
- g_key: float32 [1024, 1024], P('seq', 'tp')
- g_value: float32 [1024, 1024], P('seq', 'tp')
- g_out: float32 [1024, 1024], P('tp', 'seq')
- g_in: float32 [1024, 4096], P('seq', 'tp')
- g_down: float32 [4096, 1024], P('tp', 'seq')
- g_comp: float32 [3, 1024, 1024], P(None, 'seq', 'tp')
The draws below stay inside these ranges and needn't reach their ends.
Inputs may be any that keep to these rules, and one draw needn't show every extreme that they name: boundary[m, s] is the place in segment s of micro-batch m where a new document begins; 512 means none begins in it. links[m, s] is 1 where segment s of micro-batch m continues the document of its memories, else 0.
All inputs are finite; a program needn't handle non-finite values.
Results may differ from the reference program's by a relative error of at most 0.013.
The reference program's roundings to bfloat16 on the way count: a program that leaves them out, or rounds other values in their place, can miss the bound.
Values may be sent and summed in bfloat16 or wider, within the bound.
A program may use at most 192 MiB of HBM per device.

```python
import math
import jax
import jax.numpy as jnp
from jax import lax

D = 1024
HEADS = 8
HEAD = 128
FF = 4096
SEG = 512
MICRO = 2
SEGM = 7
ROWS_MB = 3584
CSEG = 176
SLOTS = 1232


def plant(entries, stream_key, low, largest):
    longest = entries.shape.index(max(entries.shape))
    spots = []
    for shift in (0, 1):
        where = [jax.random.randint(jax.random.fold_in(stream_key, axis), (), 0, length) for axis, length in enumerate(entries.shape)]
        where[longest] = (where[longest] + shift) % entries.shape[longest]
        spots.append(tuple(where))
    return entries.at[spots[0]].set(low).at[spots[1]].set(largest)


def shard_levels(rng, dims, pieces, low, top_value):
    loudness = 1.0
    for dim, parts in pieces:
        steps = jax.random.uniform(jax.random.fold_in(jax.random.fold_in(rng, 6), dim), (parts,), jnp.float32, low / len(pieces), top_value / len(pieces))
        loudness = loudness * jnp.repeat(jnp.exp(steps), dims[dim] // parts).reshape((-1,) + (1,) * (len(dims) - 1 - dim))
    return loudness


def centred(rng, extent, width, bound, shards=(), kind=jnp.bfloat16):
    factor_of = shard_levels(rng, extent, shards, -0.22, 0.18) if shards else 1.0
    drawn = jax.random.normal(rng, extent, jnp.float32) * width * factor_of
    return jnp.minimum(jnp.maximum(drawn, -bound), bound).astype(kind)


def setup_inputs(seed: int = 0) -> dict:
    splits = jax.random.split(jax.random.key(seed), 18)
    inputs = centred(splits[0], (MICRO, ROWS_MB, D), 1.0, 6.0, ((1, 8),))
    memory = centred(splits[1], (MICRO, ROWS_MB, D), 1.0, 6.0, ((1, 8),))
    compressed = centred(splits[2], (MICRO, ROWS_MB, D), 1.0, 6.0, ((1, 8),))
    boundary = plant(jax.random.randint(splits[3], (MICRO, SEGM), 0, SEG + 1), jax.random.fold_in(splits[3], 1), 0, SEG).astype(jnp.int32)
    links = plant((jax.random.randint(splits[4], (MICRO, SEGM), 0, 2) < 1).astype(jnp.int32), jax.random.fold_in(splits[4], 1), 0, 1)
    gains = jnp.clip(1.0 + 0.1 * jax.random.normal(splits[5], (2, D), jnp.float32), 0.5, 1.5)
    shifts = centred(splits[6], (2, D), 0.5, 3.0, (), jnp.float32)
    slopes = jnp.clip(jnp.exp(math.log(1.5) - 3.4011974 * jax.random.uniform(splits[7], (HEADS,), jnp.float32) ** shard_levels(splits[7], (HEADS,), ((0, 4),), -0.2, 0.2)), 0.05, 1.5)
    w_query = centred(splits[8], (D, HEADS * HEAD), D ** -0.5, 0.1875, ((1, 4),))
    w_key = centred(splits[9], (D, HEADS * HEAD), D ** -0.5, 0.1875, ((1, 4),))
    w_value = centred(splits[10], (D, HEADS * HEAD), D ** -0.5, 0.1875, ((1, 4),))
    w_out = centred(splits[11], (HEADS * HEAD, D), (D // 32) ** -0.5, 1.0, ((0, 4),))
    w_in = centred(splits[12], (D, FF), D ** -0.5, 0.1875, ((1, 4),))
    w_down = centred(splits[13], (FF, D), FF ** -0.5, 0.09375, ((0, 4),))
    w_comp = centred(splits[14], (3, D, D), (3 * D) ** -0.5, 0.109375, ((2, 4),))
    cot_out = centred(splits[15], (MICRO, ROWS_MB, D), 1.0, 6.0, ((1, 8),))
    cot_new = centred(splits[16], (MICRO, SLOTS, D), 1.0, 6.0, ((1, 8), (2, 4)))
    return {"inputs": inputs, "memory": memory, "compressed": compressed, "boundary": boundary, "links": links, "gains": gains, "shifts": shifts, "slopes": slopes, "w_query": w_query, "w_key": w_key, "w_value": w_value, "w_out": w_out, "w_in": w_in, "w_down": w_down, "w_comp": w_comp, "cot_out": cot_out, "cot_new": cot_new}


@jax.custom_vjp
def low(v):
    return lax.optimization_barrier(v.astype(jnp.bfloat16)).astype(jnp.float32)

@jax.custom_vjp
def low_back(v):
    return v

def low_keep(v):
    return (low(v), None)

def low_pass(kept, grad):
    return (grad,)

def back_keep(v):
    return (v, None)

def back_low(kept, grad):
    return (low(grad),)
low.defvjp(low_keep, low_pass)
low_back.defvjp(back_keep, back_low)
norm_eps = 1e-05

def high_dot(matrix_a, matrix_b):
    return jnp.dot(matrix_a, matrix_b, precision=lax.Precision.HIGHEST, preferred_element_type=jnp.float32)

def layer_norm(rows_in, gain_row, shift_row):
    center = rows_in - lax.optimization_barrier(jnp.mean(rows_in, axis=-1, keepdims=True))
    inverse = lax.rsqrt(lax.optimization_barrier(jnp.mean(center * center, axis=-1, keepdims=True)) + norm_eps)
    return center * inverse * gain_row + shift_row

def segment_attend(queries, keys, values, bound_at, link_flag, slopes):
    position = jnp.arange(SEG, dtype=jnp.int32)
    key_place = jnp.concatenate([position, position, position])
    key_kind = jnp.concatenate([jnp.full((SEG,), 2, jnp.int32), jnp.full((SEG,), 1, jnp.int32), jnp.zeros((SEG,), jnp.int32)])
    distance = position[:, None] - key_place[None, :] + key_kind[None, :] * SEG
    earlier = key_place[None, :] <= position[:, None]
    same_doc = (key_place[None, :] >= bound_at) | (position[:, None] < bound_at)
    sees_memory = (position[:, None] < bound_at) & (link_flag == 1)
    visible = jnp.where(key_kind[None, :] == 0, earlier & same_doc, sees_memory)
    reach_term = -distance.astype(jnp.float32) / SEG
    scores = jnp.einsum('qhd,khd->hqk', queries, keys, precision=lax.Precision.HIGHEST) * HEAD ** (-0.5)
    scores = low_back(scores + slopes[:, None, None] * reach_term[None])
    masked = jnp.where(visible[None], scores, -1e+30)
    row_top = lax.optimization_barrier(jnp.max(masked, axis=-1, keepdims=True))
    exponent = jnp.exp(masked - row_top)
    probability = low(exponent / lax.optimization_barrier(jnp.sum(exponent, axis=-1, keepdims=True)))
    return jnp.einsum('hqk,khd->qhd', probability, values, precision=lax.Precision.HIGHEST)

def micro_forward(params, rows_in, rows_mem, rows_comp, bound_row, link_row):
    gains, shifts, slopes, w_query, w_key, w_value, w_out, w_in, w_down, w_comp = params
    normed_x = low(layer_norm(rows_in, gains[0], shifts[0]))
    normed_mem = low(layer_norm(rows_mem, gains[0], shifts[0]))
    normed_comp = low(layer_norm(rows_comp, gains[0], shifts[0]))
    queries = low(low_back(high_dot(normed_x, w_query)))
    keys_x = low(low_back(high_dot(normed_x, w_key)))
    keys_mem = low(low_back(high_dot(normed_mem, w_key)))
    keys_comp = low(low_back(high_dot(normed_comp, w_key)))
    values_x = low(low_back(high_dot(normed_x, w_value)))
    values_mem = low(low_back(high_dot(normed_mem, w_value)))
    values_comp = low(low_back(high_dot(normed_comp, w_value)))
    seg_count = rows_in.shape[0] // SEG

    def heads_view(matrix):
        return matrix.reshape(seg_count, SEG, HEADS, HEAD)
    keys_all = jnp.concatenate([heads_view(keys_comp), heads_view(keys_mem), heads_view(keys_x)], axis=1)
    values_all = jnp.concatenate([heads_view(values_comp), heads_view(values_mem), heads_view(values_x)], axis=1)

    def attend_one(bundle):
        return segment_attend(bundle[0], bundle[1], bundle[2], bundle[3], bundle[4], slopes)
    context = lax.map(jax.checkpoint(attend_one), (heads_view(queries), keys_all, values_all, bound_row, link_row))
    context = low(low_back(context.reshape(-1, HEADS * HEAD)))
    attended = low_back(high_dot(context, w_out))
    hidden = rows_in + attended
    normed_h = low(layer_norm(hidden, gains[1], shifts[1]))
    upper = low_back(high_dot(normed_h, w_in))
    active = low(jax.nn.gelu(upper, approximate=True))
    output = hidden + high_dot(active, w_down)
    mem_segments = rows_mem.reshape(seg_count, SEG, D)
    padded = jnp.concatenate([mem_segments, jnp.zeros((seg_count, 3 * CSEG - SEG, D), jnp.float32)], axis=1)
    fresh_comp = high_dot(padded.reshape(seg_count * CSEG, 3 * D), w_comp.reshape(3 * D, D))
    return (output, fresh_comp)

def reference(inputs, memory, compressed, boundary, links, gains, shifts, slopes, w_query, w_key, w_value, w_out, w_in, w_down, w_comp, cot_out, cot_new):
    params = (gains, shifts, slopes) + tuple((weight.astype(jnp.float32) for weight in (w_query, w_key, w_value, w_out, w_in, w_down, w_comp)))
    totals = jax.tree.map(jnp.zeros_like, params)
    outputs, grads_in, grads_mem, grads_comp, fresh_list = ([], [], [], [], [])
    for batch_index in range(MICRO):
        bound_row = boundary[batch_index]
        link_row = links[batch_index]

        def forward(weights_now, rows_in, rows_mem, rows_comp):
            return micro_forward(weights_now, rows_in, rows_mem, rows_comp, bound_row, link_row)
        (output, fresh_comp), pullback = jax.vjp(forward, params, inputs[batch_index].astype(jnp.float32), memory[batch_index].astype(jnp.float32), compressed[batch_index].astype(jnp.float32))
        grads_param, grad_in, grad_mem, grad_comp = pullback((cot_out[batch_index].astype(jnp.float32), cot_new[batch_index].astype(jnp.float32)))
        totals = jax.tree.map(lambda running, adding: running + adding, totals, grads_param)
        outputs.append(output)
        grads_in.append(grad_in)
        grads_mem.append(grad_mem)
        grads_comp.append(grad_comp)
        fresh_list.append(fresh_comp)
    return (jnp.stack(outputs).astype(jnp.bfloat16), jnp.stack(grads_in), jnp.stack(grads_mem), jnp.stack(grads_comp), jnp.stack(fresh_list), totals[0], totals[1], totals[2], totals[3], totals[4], totals[5], totals[6], totals[7], totals[8], totals[9])
```

```python
import functools

import jax
import jax.numpy as jnp
from jax import lax
from jax.experimental import pallas as pl
from jax.experimental.pallas import tpu as pltpu
from jax.sharding import PartitionSpec as P

HEAD = 128
SEG = 512
CSEG = 176
REACH = 19


norm_eps = 1e-05


def shifted(block, axis, distance):
    devices = range(lax.axis_size(axis))
    route = [(i - distance, i) for i in devices if i - distance in devices]
    return lax.ppermute(block, axis, route)


def dot_plain(matrix_a, matrix_b):
    return jnp.dot(matrix_a, matrix_b, preferred_element_type=jnp.float32)


def dot_first_t(matrix_a, matrix_b):
    return lax.dot_general(
        matrix_a, matrix_b, (((0,), (0,)), ((), ())), preferred_element_type=jnp.float32
    )


def dot_second_t(matrix_a, matrix_b):
    return lax.dot_general(
        matrix_a, matrix_b, (((1,), (1,)), ((), ())), preferred_element_type=jnp.float32
    )


def normalize(rows_in, gain_row, shift_row):
    center = rows_in - jnp.mean(rows_in, axis=-1, keepdims=True)
    inverse = lax.rsqrt(jnp.mean(center * center, axis=-1, keepdims=True) + norm_eps)
    scaled = center * inverse
    return (scaled * gain_row + shift_row, scaled, inverse)


def normalize_back(grad_rows, scaled, inverse, gain_row):
    weighted = grad_rows * gain_row
    first_mean = jnp.mean(weighted, axis=-1, keepdims=True)
    second_mean = jnp.mean(weighted * scaled, axis=-1, keepdims=True)
    grad_input = inverse * (weighted - first_mean - scaled * second_mean)
    return (grad_input, jnp.sum(grad_rows * scaled, axis=0), jnp.sum(grad_rows, axis=0))


MESH = pl.DeviceIdType.MESH


def bit_view(array, count):
    bits = count.bit_length() - 1
    return array.reshape((2,) * bits + (array.shape[0] // count, array.shape[1]))


def halving_kernel(count, width, grads, total, landed, kept, send_sem, recv_sem):
    bits = count.bit_length() - 1
    me = lax.axis_index("seq")
    tp_me = lax.axis_index("tp")
    mine = [lax.rem(lax.div(me, 1 << b), 2) for b in range(bits)]
    chunks = grads.shape[-1] // width

    def partner(bit):
        return (me + (1 - 2 * mine[bit]) * (1 << bit), tp_me)

    barrier = pltpu.get_barrier_semaphore()
    for bit in range(bits):
        pl.semaphore_signal(barrier, inc=1, device_id=partner(bit), device_id_type=MESH)
    pl.semaphore_wait(barrier, bits)

    def order(chunk):
        return [(i + chunk % 2) % bits for i in range(bits)]

    def where(left, bit, own):
        return tuple(
            (mine[b] if own else 1 - mine[b]) if b == bit else slice(None) for b in left
        )

    def cols(chunk):
        return pl.ds(chunk * width, width)

    def source(chunk, step):
        return grads if step == 0 else kept[step - 1]

    def copy(chunk, step):
        plan = order(chunk)
        left = [b for b in reversed(range(bits)) if b not in plan[:step]]
        index = where(left, plan[step], False) + (slice(None), cols(chunk))
        return pltpu.make_async_remote_copy(
            src_ref=source(chunk, step).at[index],
            dst_ref=landed[step].at[(slice(None),) * (bits - step) + (cols(chunk),)],
            send_sem=send_sem.at[step, chunk],
            recv_sem=recv_sem.at[step, chunk],
            device_id=partner(plan[step]),
            device_id_type=MESH,
        )

    def finish(chunk, step):
        copy(chunk, step).wait()
        plan = order(chunk)
        left = [b for b in reversed(range(bits)) if b not in plan[:step]]
        index = where(left, plan[step], True) + (slice(None), cols(chunk))
        mine_part = source(chunk, step)[index].astype(jnp.float32)
        came = landed[step][(slice(None),) * (bits - step) + (cols(chunk),)]
        added = mine_part + came.astype(jnp.float32)
        if step == bits - 1:
            total[:, cols(chunk)] = added
        else:
            kept[step][(slice(None),) * (bits - step) + (cols(chunk),)] = added.astype(jnp.bfloat16)
            copy(chunk, step + 1).start()

    group = 2
    for turn in range(chunks // group + bits):
        for step in reversed(range(bits)):
            for at in range(group):
                chunk = (turn - step - 1) * group + at
                if 0 <= chunk < chunks:
                    finish(chunk, step)
        for at in range(group):
            chunk = turn * group + at
            if chunk < chunks:
                copy(chunk, 0).start()


def reduce_over_seq(grads):
    count = lax.axis_size("seq")
    bits = count.bit_length() - 1
    rows, columns = grads.shape[0] // count, grads.shape[1]
    width = 256
    chunks = columns // width
    return pl.pallas_call(
        functools.partial(halving_kernel, count, width),
        out_shape=jax.ShapeDtypeStruct((rows, columns), jnp.float32),
        in_specs=[pl.BlockSpec(memory_space=pltpu.VMEM)],
        out_specs=pl.BlockSpec(memory_space=pltpu.VMEM),
        scratch_shapes=[
            [pltpu.VMEM((2,) * (bits - 1 - i) + (rows, columns), jnp.bfloat16) for i in range(bits)],
            [pltpu.VMEM((2,) * (bits - 1 - i) + (rows, columns), jnp.bfloat16) for i in range(bits - 1)],
            pltpu.SemaphoreType.DMA((bits, chunks)),
            pltpu.SemaphoreType.DMA((bits, chunks)),
        ],
        compiler_params=pltpu.CompilerParams(
            collective_id=1, has_side_effects=True, vmem_limit_bytes=50 << 20
        ),
    )(bit_view(grads, count))


def per_device(
    inputs,
    memory,
    compressed,
    boundary,
    links,
    gains,
    shifts,
    slopes,
    w_query,
    w_key,
    w_value,
    w_out,
    w_in,
    w_down,
    w_comp,
    cot_out,
    cot_new,
):
    rows = inputs.shape[1]
    slot_count = cot_new.shape[1]
    local_dim = w_comp.shape[2]
    heads_local = w_query.shape[1] // HEAD
    seq_index = lax.axis_index("seq")
    scale = HEAD ** (-0.5)
    row_ids = jnp.arange(rows, dtype=jnp.int32)
    query_pos = seq_index * rows + row_ids
    prev_pos = (seq_index - 1) * rows + row_ids
    next_pos = (seq_index + 1) * rows + row_ids
    beside_all = jnp.concatenate([prev_pos, query_pos, next_pos])
    key_pos = jnp.concatenate([prev_pos, query_pos, beside_all, beside_all])
    key_kind = jnp.concatenate(
        [
            jnp.zeros((2 * rows,), jnp.int32),
            jnp.ones((3 * rows,), jnp.int32),
            jnp.full((3 * rows,), 2, jnp.int32),
        ]
    )
    query_seg = query_pos // SEG
    query_at = query_pos - query_seg * SEG
    key_seg = key_pos // SEG
    key_at = key_pos - key_seg * SEG
    distance = query_at[:, None] - key_at[None, :] + key_kind[None, :] * SEG
    reach_term = -distance.astype(jnp.float32) / SEG
    earlier = key_at[None, :] <= query_at[:, None]
    same_seg = key_seg[None, :] == query_seg[:, None]
    seg_ids = jnp.arange(boundary.shape[1], dtype=jnp.int32)
    own_segment = query_seg[:, None] == seg_ids[None, :]
    slot_ids = seq_index * slot_count + jnp.arange(slot_count, dtype=jnp.int32)
    slot_seg = slot_ids // CSEG
    slot_at = slot_ids - slot_seg * CSEG
    tap_place = 3 * slot_at[:, None] + jnp.arange(3, dtype=jnp.int32)[None, :]
    local_row = slot_seg[:, None] * SEG + tap_place - seq_index * rows
    gather_at = jnp.where(tap_place < SEG, local_row, rows + REACH).reshape(-1)
    comp_flat = w_comp.reshape(-1, local_dim)
    shapes = [
        w_query.shape,
        w_key.shape,
        w_value.shape,
        w_out.shape,
        w_in.shape,
        w_down.shape,
        w_comp.shape,
        gains.shape,
        shifts.shape,
    ]

    def piece(matrix, index_at):
        return matrix[index_at * rows : (index_at + 1) * rows]

    def micro_step(carry, slices):
        totals, slope_total = carry
        rows_in, rows_mem, rows_comp, bound_row, link_row, cot_rows, cot_slots = slices
        bound_at = jnp.sum(jnp.where(own_segment, bound_row[None, :], 0), axis=1)
        link_at = jnp.sum(jnp.where(own_segment, link_row[None, :], 0), axis=1)
        same_doc = (key_at[None, :] >= bound_at[:, None]) | (query_at[:, None] < bound_at[:, None])
        sees_memory = (query_at < bound_at) & (link_at == 1)
        visible = same_seg & jnp.where(
            key_kind[None, :] == 0, earlier & same_doc, sees_memory[:, None]
        )
        stacked = jnp.concatenate([rows_in, rows_mem, rows_comp], axis=0).astype(jnp.float32)
        normed_f, scaled_one, inverse_one = normalize(stacked, gains[0], shifts[0])
        normed = normed_f.astype(jnp.bfloat16)
        normed_x = normed[:rows]
        queries = dot_plain(normed_x, w_query).astype(jnp.bfloat16)
        keys_own = dot_plain(normed, w_key).astype(jnp.bfloat16)
        values_own = dot_plain(normed, w_value).astype(jnp.bfloat16)
        before = shifted((keys_own, values_own), "seq", 1)
        after = shifted((keys_own[rows:], values_own[rows:], rows_mem[:REACH]), "seq", -1)

        def assemble(own_part, prev_part, next_part):
            return jnp.concatenate(
                [
                    piece(prev_part, 0),
                    piece(own_part, 0),
                    piece(prev_part, 1),
                    piece(own_part, 1),
                    piece(next_part, 0),
                    piece(prev_part, 2),
                    piece(own_part, 2),
                    piece(next_part, 1),
                ],
                axis=0,
            )

        key_heads = assemble(keys_own, before[0], after[0]).reshape(8 * rows, heads_local, HEAD)
        value_heads = assemble(values_own, before[1], after[1]).reshape(8 * rows, heads_local, HEAD)
        query_heads = queries.reshape(rows, heads_local, HEAD)

        def masked_scores():
            raw_scores = (
                jnp.einsum(
                    "qhd,khd->hqk", query_heads, key_heads, preferred_element_type=jnp.float32
                )
                * scale
            )
            raw_scores = raw_scores + slopes[:, None, None] * reach_term[None]
            return jnp.where(visible[None], raw_scores, -1e30)

        masked = masked_scores()
        row_top = jnp.max(masked, axis=-1, keepdims=True)
        log_total = row_top + jnp.log(jnp.sum(jnp.exp(masked - row_top), axis=-1, keepdims=True))
        probability = jnp.exp(masked - log_total).astype(jnp.bfloat16)
        context = (
            jnp.einsum("hqk,khd->qhd", probability, value_heads, preferred_element_type=jnp.float32)
            .reshape(rows, -1)
            .astype(jnp.bfloat16)
        )
        attended = lax.psum(dot_plain(context, w_out), "tp")
        hidden = rows_in.astype(jnp.float32) + attended
        normed_hf, scaled_two, inverse_two = normalize(hidden, gains[1], shifts[1])
        normed_h = normed_hf.astype(jnp.bfloat16)
        upper = dot_plain(normed_h, w_in)
        active_f, gelu_back = jax.vjp(
            lambda upper_in: jax.nn.gelu(upper_in, approximate=True), upper
        )
        active = active_f.astype(jnp.bfloat16)
        output = hidden + lax.psum(dot_plain(active, w_down).astype(jnp.bfloat16), "tp").astype(
            jnp.float32
        )
        extended = jnp.concatenate(
            [rows_mem, after[2], jnp.zeros((1, rows_mem.shape[1]), jnp.bfloat16)], axis=0
        )
        windows = jnp.take(extended, gather_at, axis=0).reshape(slot_count, -1)
        fresh = dot_plain(windows, comp_flat)
        grad_comp = dot_first_t(windows, cot_slots).reshape(3, -1, local_dim)
        d_windows = dot_second_t(cot_slots, comp_flat).reshape(3 * slot_count, -1)
        d_extended = (
            jnp.zeros((rows + REACH + 1, d_windows.shape[1]), jnp.float32)
            .at[gather_at]
            .add(d_windows)
        )
        grad_down = dot_first_t(active, cot_rows)
        d_upper = gelu_back(dot_second_t(cot_rows, w_down))[0].astype(jnp.bfloat16)
        grad_in = dot_first_t(normed_h, d_upper)
        d_normed_h = lax.psum(dot_second_t(d_upper, w_in), "tp")
        d_hidden_ln, gain_two, shift_two = normalize_back(
            d_normed_h, scaled_two, inverse_two, gains[1]
        )
        d_hidden = cot_rows.astype(jnp.float32) + d_hidden_ln
        d_attended = d_hidden.astype(jnp.bfloat16)
        grad_out = dot_first_t(context, d_attended)
        d_context = dot_second_t(d_attended, w_out).astype(jnp.bfloat16)
        d_context_heads = d_context.reshape(rows, heads_local, HEAD)
        masked = masked_scores()
        soft = jnp.exp(masked - log_total)
        d_soft = jnp.einsum(
            "qhd,khd->hqk", d_context_heads, value_heads, preferred_element_type=jnp.float32
        )
        d_scores = (soft * (d_soft - jnp.sum(soft * d_soft, axis=-1, keepdims=True))).astype(
            jnp.bfloat16
        )
        grad_slope = jnp.sum(d_scores.astype(jnp.float32) * reach_term[None], axis=(1, 2))
        d_queries = (
            (
                jnp.einsum("hqk,khd->qhd", d_scores, key_heads, preferred_element_type=jnp.float32)
                * scale
            )
            .reshape(rows, -1)
            .astype(jnp.bfloat16)
        )
        d_keys_all = (
            jnp.einsum(
                "hqk,qhd->khd", d_scores, query_heads, preferred_element_type=jnp.float32
            ).reshape(8 * rows, -1)
            * scale
        )
        d_values_all = jnp.einsum(
            "hqk,qhd->khd",
            soft.astype(jnp.bfloat16),
            d_context_heads,
            preferred_element_type=jnp.float32,
        ).reshape(8 * rows, -1)
        from_next = shifted(
            (
                piece(d_keys_all, 0),
                piece(d_values_all, 0),
                piece(d_keys_all, 2),
                piece(d_values_all, 2),
                piece(d_keys_all, 5),
                piece(d_values_all, 5),
            ),
            "seq",
            -1,
        )
        from_prev = (
            shifted(piece(d_keys_all, 4).astype(jnp.bfloat16), "seq", 1).astype(jnp.float32),
            shifted(piece(d_values_all, 4).astype(jnp.bfloat16), "seq", 1).astype(jnp.float32),
            shifted(piece(d_keys_all, 7).astype(jnp.bfloat16), "seq", 1).astype(jnp.float32),
            shifted(piece(d_values_all, 7).astype(jnp.bfloat16), "seq", 1).astype(jnp.float32),
            shifted(d_extended[rows : rows + REACH].astype(jnp.bfloat16), "seq", 1).astype(
                jnp.float32
            ),
        )
        d_keys = jnp.concatenate(
            [
                piece(d_keys_all, 1) + from_next[0],
                piece(d_keys_all, 3) + from_next[2] + from_prev[0],
                piece(d_keys_all, 6) + from_next[4] + from_prev[2],
            ],
            axis=0,
        ).astype(jnp.bfloat16)
        d_values = jnp.concatenate(
            [
                piece(d_values_all, 1) + from_next[1],
                piece(d_values_all, 3) + from_next[3] + from_prev[1],
                piece(d_values_all, 6) + from_next[5] + from_prev[3],
            ],
            axis=0,
        ).astype(jnp.bfloat16)
        grad_query = dot_first_t(normed_x, d_queries)
        grad_key = dot_first_t(normed, d_keys)
        grad_value = dot_first_t(normed, d_values)
        d_normed = dot_second_t(d_keys, w_key) + dot_second_t(d_values, w_value)
        d_normed = jnp.concatenate(
            [d_normed[:rows] + dot_second_t(d_queries, w_query), d_normed[rows:]], axis=0
        )
        window_part = jnp.concatenate(
            [d_extended[:REACH] + from_prev[4], d_extended[REACH:rows]], axis=0
        )
        d_normed_sum, window_sum = lax.psum((d_normed, window_part), "tp")
        d_stacked, gain_one, shift_one = normalize_back(
            d_normed_sum, scaled_one, inverse_one, gains[0]
        )
        d_input = d_hidden + d_stacked[:rows]
        d_memory = d_stacked[rows : 2 * rows] + window_sum
        d_compressed = d_stacked[2 * rows :]
        local = (
            grad_query,
            grad_key,
            grad_value,
            grad_out,
            grad_in,
            grad_down,
            grad_comp,
            jnp.stack([gain_one, gain_two]),
            jnp.stack([shift_one, shift_two]),
        )
        new_totals = tuple((running + adding for running, adding in zip(totals, local)))
        return (
            (new_totals, slope_total + grad_slope),
            (output.astype(jnp.bfloat16), d_input, d_memory, d_compressed, fresh),
        )

    start = (
        tuple((jnp.zeros(shape_one, jnp.float32) for shape_one in shapes)),
        jnp.zeros(slopes.shape, jnp.float32),
    )
    (totals, slope_total), results = lax.scan(
        micro_step, start, (inputs, memory, compressed, boundary, links, cot_out, cot_new)
    )
    pieces = [
        totals[0],
        totals[1],
        totals[2],
        totals[3].T,
        totals[4],
        totals[5].T,
        totals[6][0],
        totals[6][1],
        totals[6][2],
        jnp.pad(jnp.concatenate([totals[7], totals[8]], axis=0).T, ((0, 0), (0, 252))),
    ]
    mixed = reduce_over_seq(
        jnp.concatenate([matrix.astype(jnp.bfloat16) for matrix in pieces], axis=1)
    )
    out_rows = []
    at = 0
    for matrix in pieces:
        out_rows.append(mixed[:, at : at + matrix.shape[1]])
        at += matrix.shape[1]
    vectors = out_rows[9][:, :4].T
    summed = (
        out_rows[0],
        out_rows[1],
        out_rows[2],
        out_rows[3].T,
        out_rows[4],
        out_rows[5].T,
        jnp.stack(out_rows[6:9]),
        vectors[:2],
        vectors[2:],
    )
    grad_slopes = lax.psum(slope_total, "seq")
    return (
        results[0],
        results[1],
        results[2],
        results[3],
        results[4],
        summed[7],
        summed[8],
        grad_slopes,
        summed[0],
        summed[1],
        summed[2],
        summed[3],
        summed[4],
        summed[5],
        summed[6],
    )


def solution(mesh):
    in_specs = (
        P(None, "seq", None),
        P(None, "seq", None),
        P(None, "seq", None),
        P(),
        P(),
        P(),
        P(),
        P("tp"),
        P(None, "tp"),
        P(None, "tp"),
        P(None, "tp"),
        P("tp", None),
        P(None, "tp"),
        P("tp", None),
        P(None, None, "tp"),
        P(None, "seq", None),
        P(None, "seq", "tp"),
    )
    out_specs = (
        P(None, "seq", None),
        P(None, "seq", None),
        P(None, "seq", None),
        P(None, "seq", None),
        P(None, "seq", "tp"),
        P(None, "seq"),
        P(None, "seq"),
        P("tp"),
        P("seq", "tp"),
        P("seq", "tp"),
        P("seq", "tp"),
        P("tp", "seq"),
        P("seq", "tp"),
        P("tp", "seq"),
        P(None, "seq", "tp"),
    )
    return jax.shard_map(
        per_device, mesh=mesh, in_specs=in_specs, out_specs=out_specs, check_vma=False
    )
```

```python
import functools
import math

import jax
import jax.numpy as jnp
from jax import lax
from jax.experimental import pallas as pl
from jax.experimental.pallas import tpu as pltpu
from jax.sharding import PartitionSpec as P

HEAD = 128
SEG = 512
CSEG = 176
REACH = 32
LEAD = 16
CHUNK = 64
PART = 16
KINDS = 3
NORM_EPS = 1e-05
MESH = pl.DeviceIdType.MESH
BF = jnp.bfloat16
F32 = jnp.float32
GELU_IN = math.sqrt(2.0 / math.pi)
PER_SEG = SEG // CHUNK
PER_DEV = PER_SEG - 1
QUERY_BLOCK = 128


def dot_plain(a, b):
    return jnp.dot(a, b, preferred_element_type=F32)


def dot_first_t(a, b):
    return lax.dot_general(a, b, (((0,), (0,)), ((), ())), preferred_element_type=F32)


def dot_second_t(a, b):
    return lax.dot_general(a, b, (((1,), (1,)), ((), ())), preferred_element_type=F32)


def home_of(segment, micro):
    middle = PER_DEV // 2
    home = jnp.where(
        segment < middle, segment, jnp.where(segment == middle, middle + micro, segment + 1)
    )
    slot = jnp.where(segment == middle, 0, micro)
    return home, slot


def units_of(place, slot):
    middle = PER_DEV // 2
    segment = jnp.where(place <= middle, place, place - 1)
    is_middle = segment == middle
    micro = jnp.where(is_middle, place - middle, slot)
    return segment, micro, jnp.logical_or(jnp.logical_not(is_middle), slot == 0)


class Place:
    def __init__(self):
        self.seq = lax.axis_index("seq")
        self.tp = lax.axis_index("tp")
        self.column = lax.rem(self.seq, PER_SEG)
        self.low = lax.rem(self.tp, 2)
        self.high = lax.div(self.tp, 2)
        self.count = lax.axis_size("seq")

    def mate(self):
        return (self.seq, self.tp + 1 - 2 * self.low)

    def across(self):
        return (self.seq, self.tp + 2 - 4 * self.high)

    def beside(self, by):
        return (self.seq + by, self.tp)


def remote(src, dst, send, recv, device):
    return pltpu.make_async_remote_copy(
        src_ref=src,
        dst_ref=dst,
        send_sem=send,
        recv_sem=recv,
        device_id=device,
        device_id_type=MESH,
    )


class TpReduce:
    def __init__(self, me, part, first, second, sems, index):
        self.me, self.part, self.first, self.second = me, part, first, second
        send, recv = sems
        self.one = remote(
            part.at[:, :, 1 - me.low], first, send.at[index, 0], recv.at[index, 0], me.mate()
        )
        self.two = remote(
            part.at[:, 1 - me.high, me.low],
            second,
            send.at[index, 1],
            recv.at[index, 1],
            me.across(),
        )

    def start(self):
        self.one.start()

    def middle(self):
        self.one.wait()
        part, first, low = self.part, self.first, self.me.low

        @pl.loop(0, part.shape[0])
        def _(k):
            added = part[k, :, low].astype(F32) + first[k].astype(F32)
            part[k, :, low] = added.astype(BF)

        self.two.start()

    def end(self):
        self.two.wait()

    def total(self, k):
        me = self.me
        return self.part[k, me.high, me.low].astype(F32) + self.second[k].astype(F32)


class TpGather:
    def __init__(self, me, whole, sems, index):
        send, recv = sems
        mine = whole.at[:, me.high, me.low]
        self.one = remote(mine, mine, send.at[index, 0], recv.at[index, 0], me.across())
        both = whole.at[:, :, me.low]
        self.two = remote(both, both, send.at[index, 1], recv.at[index, 1], me.mate())

    def start(self):
        self.one.start()

    def middle(self):
        self.one.wait()
        self.two.start()

    def end(self):
        self.two.wait()


def meet(me, with_bits):
    barrier = pltpu.get_barrier_semaphore()
    friends = [me.mate(), me.across()]
    count = me.count
    if with_bits:
        for bit in range(count.bit_length() - 1):
            mine = lax.rem(lax.div(me.seq, 1 << bit), 2)
            friends.append(me.beside((1 - 2 * mine) * (1 << bit)))
    friends.append((lax.rem(me.seq + 1, count), me.tp))
    friends.append((lax.rem(me.seq + count - 1, count), me.tp))
    for friend in friends:
        pl.semaphore_signal(barrier, inc=1, device_id=friend, device_id_type=MESH)
    pl.semaphore_wait(barrier, len(friends))


def center_of(rows):
    center = rows - jnp.mean(rows, axis=-1, keepdims=True)
    inverse = lax.rsqrt(jnp.mean(center * center, axis=-1, keepdims=True) + NORM_EPS)
    return center * inverse, inverse


def norm_back(grad, scaled, inverse, gain):
    weighted = grad * gain
    first = jnp.mean(weighted, axis=-1, keepdims=True)
    second = jnp.mean(weighted * scaled, axis=-1, keepdims=True)
    return inverse * (weighted - first - scaled * second)


def eights(rows):
    return rows[: PART // 2] + rows[PART // 2 :]


def forward_kernel(
    rows_hbm,
    cot_hbm,
    bound,
    link,
    slopes,
    gains,
    shifts,
    w_query,
    w_key,
    w_value,
    w_out,
    w_in,
    w_down,
    normed_hbm,
    own_hbm,
    q_hbm,
    k_hbm,
    v_hbm,
    prob_hbm,
    ctx_hbm,
    out_hbm,
    dhid_hbm,
    datt_hbm,
    gffn_hbm,
    vec_hbm,
    x_ref,
    cot_ref,
    own_ref,
    q_ref,
    k_ref,
    v_ref,
    prob_ref,
    ctx_ref,
    wqkv_ref,
    wo_ref,
    wi_ref,
    wd_ref,
    parts,
    firsts,
    seconds,
    nh_ref,
    datt_ref,
    act_ref,
    du_ref,
    hid_ref,
    dhid_ref,
    out_ref,
    gffn_ref,
    vec_ref,
    load_sem,
    save_sem,
    prob_sem,
    place_sem,
    move_send,
    move_recv,
    pass_send,
    pass_recv,
    rs_send,
    rs_recv,
    ag_send,
    ag_recv,
):
    me = Place()
    d = x_ref.shape[-1]
    half = d // 2
    heads = q_ref.shape[1]
    my_cols = pl.ds(pl.multiple_of(me.low * half, half), half)
    their_cols = pl.ds(pl.multiple_of((1 - me.low) * half, half), half)
    width = w_query.shape[1]

    loads = [
        pltpu.make_async_copy(w_query, wqkv_ref.at[:, pl.ds(2 * width, width)], load_sem.at[0]),
        pltpu.make_async_copy(w_key, wqkv_ref.at[:, pl.ds(0, width)], load_sem.at[1]),
        pltpu.make_async_copy(w_value, wqkv_ref.at[:, pl.ds(width, width)], load_sem.at[2]),
        pltpu.make_async_copy(w_out, wo_ref, load_sem.at[3]),
        pltpu.make_async_copy(w_in, wi_ref, load_sem.at[4]),
        pltpu.make_async_copy(w_down, wd_ref, load_sem.at[5]),
    ]
    for load in loads:
        load.start()

    meet(me, False)

    sources = [rows_hbm[0], rows_hbm[1], rows_hbm[2], cot_hbm]

    def landing(kind, slot, chunk):
        if kind == KINDS:
            return cot_ref.at[slot, chunk]
        return x_ref.at[slot, kind, chunk]

    def send_out(kinds, micro):
        @pl.loop(0, PER_DEV)
        def _(q):
            segment = jnp.where(q < me.column, me.column - 1, me.column)
            home, slot = home_of(segment, micro)
            chunk = PER_DEV * me.column + q - PER_SEG * segment
            for kind in kinds:
                src = sources[kind].at[micro, q]
                dst = landing(kind, slot, chunk)

                @pl.when(home == me.column)
                def _():
                    pltpu.make_async_copy(src, dst, place_sem.at[kind, slot, chunk]).start()

                @pl.when(home != me.column)
                def _():
                    remote(
                        src.at[:, :, my_cols],
                        dst.at[:, :, my_cols],
                        move_send.at[kind, micro, q],
                        move_recv.at[kind, slot, chunk],
                        me.beside(home - me.column),
                    ).start()

    def sent(kinds, micro):
        @pl.loop(0, PER_DEV)
        def _(q):
            segment = jnp.where(q < me.column, me.column - 1, me.column)
            home, slot = home_of(segment, micro)
            chunk = PER_DEV * me.column + q - PER_SEG * segment
            for kind in kinds:

                @pl.when(home != me.column)
                def _():
                    remote(
                        sources[kind].at[micro, q, :, :, my_cols],
                        landing(kind, slot, chunk).at[:, :, my_cols],
                        move_send.at[kind, micro, q],
                        move_recv.at[kind, slot, chunk],
                        me.beside(home - me.column),
                    ).wait_send()

    def handing(kind, slot, chunk):
        dst = landing(kind, slot, chunk).at[:, :, my_cols]
        return remote(
            dst,
            dst,
            pass_send.at[kind, slot, chunk],
            pass_recv.at[kind, slot, chunk],
            me.mate(),
        )

    def pass_on(kinds, slot):
        segment, micro, there = units_of(me.column, slot)

        @pl.loop(0, PER_SEG)
        def _(chunk):
            place = PER_SEG * segment + chunk
            source = lax.div(place, PER_DEV)
            for kind in kinds:
                dst = landing(kind, slot, chunk)

                @pl.when(jnp.logical_and(there, source == me.column))
                def _():
                    pltpu.make_async_copy(dst, dst, place_sem.at[kind, slot, chunk]).wait()

                @pl.when(jnp.logical_and(there, source != me.column))
                def _():
                    came = dst.at[:, :, my_cols]
                    remote(
                        came,
                        came,
                        move_send.at[kind, 0, 0],
                        move_recv.at[kind, slot, chunk],
                        me.mate(),
                    ).wait_recv()
                    handing(kind, slot, chunk).start()

                @pl.when(jnp.logical_not(there))
                def _():
                    dst[...] = jnp.zeros(dst.shape, BF)

    def arrived(kinds, slot):
        segment, micro, there = units_of(me.column, slot)

        @pl.loop(0, PER_SEG)
        def _(chunk):
            place = PER_SEG * segment + chunk
            source = lax.div(place, PER_DEV)
            for kind in kinds:

                @pl.when(jnp.logical_and(there, source != me.column))
                def _():
                    dst = landing(kind, slot, chunk).at[:, :, their_cols]
                    handing(kind, slot, chunk).wait_send()
                    remote(
                        dst,
                        dst,
                        pass_send.at[kind, slot, chunk],
                        pass_recv.at[kind, slot, chunk],
                        me.mate(),
                    ).wait_recv()

    kinds = list(range(KINDS))
    for micro in range(2):
        send_out(kinds, micro)
    for micro in range(2):
        send_out([KINDS], micro)

    gain_0, shift_0 = gains[0:1], shifts[0:1]
    gain_1, shift_1 = gains[1:2], shifts[1:2]
    vec_ref[...] = jnp.zeros(vec_ref.shape, F32)

    def project(u):
        for kind in range(KINDS):

            @pl.loop(0, PER_SEG)
            def _(k):
                raw = x_ref[u, kind, k]
                own_ref[u, kind, k] = x_ref[u, kind, k, me.tp]
                scaled, _ = center_of(raw.reshape(CHUNK, d).astype(F32))
                normed = (scaled * gain_0 + shift_0).astype(BF)
                x_ref[u, kind, k] = normed.reshape(CHUNK // PART, PART, d)

            normed = x_ref[u, kind].reshape(SEG, d)
            span = pl.ds(kind * SEG, SEG)
            keys = dot_plain(normed, wqkv_ref[:, :width]).astype(BF)
            values = dot_plain(normed, wqkv_ref[:, width : 2 * width]).astype(BF)
            for h in range(heads):
                cols = slice(h * HEAD, (h + 1) * HEAD)
                k_ref[u, h, span] = keys[:, cols]
                v_ref[u, h, span] = values[:, cols]
            if kind == 0:
                queries = dot_plain(normed, wqkv_ref[:, 2 * width :]).astype(BF)
                for h in range(heads):
                    q_ref[u, h] = queries[:, h * HEAD : (h + 1) * HEAD]

    def prob_save(u, h):
        return pltpu.make_async_copy(
            prob_ref.at[h % 2], prob_hbm.at[u, h], prob_sem.at[u, h]
        )

    def attend(u, h):
        scale = HEAD ** (-0.5)
        slope = slopes[h]
        edge = bound[u]
        linked = link[u]
        key_at = lax.broadcasted_iota(jnp.int32, (1, KINDS * SEG), 1)
        kind_at = lax.div(key_at, SEG)
        bias = (key_at - 2 * SEG * kind_at).astype(F32) * (slope / SEG)
        key_x = lax.broadcasted_iota(jnp.int32, (QUERY_BLOCK, SEG), 1)

        @pl.loop(0, SEG // QUERY_BLOCK)
        def _(b):
            rows = pl.ds(pl.multiple_of(b * QUERY_BLOCK, QUERY_BLOCK), QUERY_BLOCK)
            raw = dot_second_t(q_ref[u, h, rows], k_ref[u, h]) * scale + bias
            at = b * QUERY_BLOCK + lax.broadcasted_iota(jnp.int32, (QUERY_BLOCK, SEG), 0)
            seen = jnp.logical_and(key_x <= at, jnp.logical_or(key_x >= edge, at < edge))
            near = jnp.where(seen, raw[:, :SEG], -1e30)
            open_row = jnp.logical_and(at[:, :1] < edge, linked == 1)
            far = jnp.where(open_row, raw[:, SEG:], -1e30)
            top = jnp.maximum(
                jnp.max(near, axis=-1, keepdims=True), jnp.max(far, axis=-1, keepdims=True)
            )
            near = jnp.exp(near - top)
            far = jnp.exp(far - top)
            whole = jnp.sum(near, axis=-1, keepdims=True) + jnp.sum(far, axis=-1, keepdims=True)
            share = 1.0 / whole
            near = (near * share).astype(BF)
            far = (far * share).astype(BF)
            prob_ref[h % 2, rows, :SEG] = near
            prob_ref[h % 2, rows, SEG:] = far
            context = dot_plain(near, v_ref[u, h, :SEG]) + dot_plain(far, v_ref[u, h, SEG:])
            ctx_ref[u, h, rows] = context.astype(BF)

    def store_part(part, cols, tile):
        part[:, :, :, :, cols] = tile.astype(BF).reshape(PER_SEG, 2, 2, PART, tile.shape[1])

    def out_project(u, part):
        @pl.loop(0, d // 256)
        def _(n):
            cols = pl.ds(pl.multiple_of(n * 256, 256), 256)
            tile = dot_plain(ctx_ref[u, 0], wo_ref[:HEAD, cols])
            for h in range(1, heads):
                tile += dot_plain(ctx_ref[u, h], wo_ref[h * HEAD : (h + 1) * HEAD, cols])
            store_part(part, cols, tile)

    rs = (rs_send, rs_recv)
    ag = (ag_send, ag_recv)

    def reduce_task(index):
        return TpReduce(me, parts[index], firsts[index], seconds[index], rs, index)

    def hidden_norm(u, task):
        task.end()

        @pl.loop(0, PER_SEG)
        def _(k):
            hidden = own_ref[u, 0, k].astype(F32) + task.total(k)
            hid_ref[u, k] = hidden
            scaled, _ = center_of(hidden)
            nh_ref[u, k, me.high, me.low] = (scaled * gain_1 + shift_1).astype(BF)

    def ffn_up(u):
        ff = wi_ref.shape[1]

        @pl.loop(0, ff // 256)
        def _(n):
            cols = pl.ds(pl.multiple_of(n * 256, 256), 256)
            for r in range(2):
                chunks = slice(r * PER_SEG // 2, (r + 1) * PER_SEG // 2)
                rows = slice(r * SEG // 2, (r + 1) * SEG // 2)
                upper = dot_plain(nh_ref[u, chunks].reshape(SEG // 2, d), wi_ref[:, cols])
                d_act = dot_second_t(cot_ref[u, chunks].reshape(SEG // 2, d), wd_ref[cols])
                square = upper * upper
                inner = GELU_IN * upper * (1.0 + 0.044715 * square)
                bend = jnp.tanh(inner)
                grown = 0.5 * (1.0 + bend)
                act_ref[u, rows, cols] = (upper * grown).astype(BF)
                slope = grown + 0.5 * upper * (1.0 - bend * bend) * (
                    GELU_IN * (1.0 + 3.0 * 0.044715 * square)
                )
                du_ref[u, rows, cols] = (d_act * slope).astype(BF)

    def ffn_out(u, part):
        @pl.loop(0, d // 256)
        def _(n):
            cols = pl.ds(pl.multiple_of(n * 256, 256), 256)
            store_part(part, cols, dot_plain(act_ref[u], wd_ref[:, cols]))

    def ffn_back(u, part):
        @pl.loop(0, d // 256)
        def _(n):
            cols = pl.ds(pl.multiple_of(n * 256, 256), 256)
            store_part(part, cols, dot_second_t(du_ref[u], wi_ref[cols]))

    def hidden_back(u, task):
        task.end()

        @pl.loop(0, PER_SEG)
        def _(k):
            scaled, inverse = center_of(hid_ref[u, k])
            grad = task.total(k)
            cot = cot_ref[u, k, me.tp].astype(F32)
            d_hidden = cot + norm_back(grad, scaled, inverse, gain_1)
            vec_ref[0] += eights(grad * scaled)
            vec_ref[1] += eights(grad)
            dhid_ref[u, k] = d_hidden
            datt_ref[u, k, me.high, me.low] = d_hidden.astype(BF)

    def out_end(u, task):
        task.end()

        @pl.loop(0, PER_SEG)
        def _(k):
            out_ref[u, k] = (hid_ref[u, k] + task.total(k)).astype(BF)

    def weight_grads(cols_from, left, right):
        @pl.loop(0, d // 256)
        def _(n):
            cols = pl.ds(pl.multiple_of(n * 256, 256), 256)
            tile = dot_first_t(left(0, cols), right(0)) + dot_first_t(left(1, cols), right(1))
            gffn_ref[cols, pl.ds(cols_from, tile.shape[1])] = tile.astype(BF)

    pass_on(kinds, 0)
    arrived(kinds, 0)
    for load in loads[:3]:
        load.wait()
    project(0)
    attend(0, 0)
    prob_save(0, 0).start()
    pass_on(kinds, 1)
    attend(0, 1)
    prob_save(0, 1).start()
    loads[3].wait()
    out_project(0, parts[0])
    att_0 = reduce_task(0)
    att_0.start()
    arrived(kinds, 1)
    project(1)
    att_0.middle()
    prob_save(0, 0).wait()
    attend(1, 0)
    prob_save(1, 0).start()
    hidden_norm(0, att_0)
    nh_0 = TpGather(me, nh_ref.at[0], ag, 0)
    nh_0.start()
    prob_save(0, 1).wait()
    attend(1, 1)
    prob_save(1, 1).start()
    nh_0.middle()
    out_project(1, parts[1])
    att_1 = reduce_task(1)
    att_1.start()
    pass_on([KINDS], 0)
    arrived([KINDS], 0)
    loads[4].wait()
    loads[5].wait()
    nh_0.end()
    att_1.middle()
    ffn_up(0)
    pass_on([KINDS], 1)
    hidden_norm(1, att_1)
    nh_1 = TpGather(me, nh_ref.at[1], ag, 1)
    nh_1.start()
    ffn_back(0, parts[2])
    back_0 = reduce_task(2)
    back_0.start()
    ffn_out(0, parts[3])
    nh_1.middle()
    back_0.middle()
    outs_0 = reduce_task(3)
    outs_0.start()
    arrived([KINDS], 1)
    nh_1.end()
    ffn_up(1)
    outs_0.middle()
    hidden_back(0, back_0)
    datt_0 = TpGather(me, datt_ref.at[0], ag, 2)
    datt_0.start()
    ffn_back(1, parts[4])
    back_1 = reduce_task(4)
    back_1.start()
    ffn_out(1, parts[5])
    back_1.middle()
    datt_0.middle()
    outs_1 = reduce_task(5)
    outs_1.start()
    weight_grads(
        0,
        lambda u, cols: nh_ref[u, :, :, :, :, cols].reshape(SEG, 256),
        lambda u: du_ref[u],
    )
    outs_1.middle()
    hidden_back(1, back_1)
    datt_1 = TpGather(me, datt_ref.at[1], ag, 3)
    datt_1.start()
    weight_grads(
        wi_ref.shape[1],
        lambda u, cols: cot_ref[u, :, :, :, cols].reshape(SEG, 256),
        lambda u: act_ref[u],
    )
    out_end(0, outs_0)
    out_end(1, outs_1)
    datt_0.end()
    datt_1.middle()
    prob_save(1, 0).wait()
    prob_save(1, 1).wait()
    datt_1.end()
    pairs = [
        (x_ref, normed_hbm),
        (own_ref, own_hbm),
        (q_ref, q_hbm),
        (k_ref, k_hbm),
        (v_ref, v_hbm),
        (ctx_ref, ctx_hbm),
        (out_ref, out_hbm),
        (dhid_ref, dhid_hbm),
        (datt_ref, datt_hbm),
        (gffn_ref, gffn_hbm),
        (vec_ref, vec_hbm),
    ]
    saves = [
        pltpu.make_async_copy(src, dst, save_sem.at[i]) for i, (src, dst) in enumerate(pairs)
    ]
    for save in saves:
        save.start()
    for micro in range(2):
        sent(kinds + [KINDS], micro)
    for save in saves:
        save.wait()


def forward_call(rows, cot, bound, link, slopes, gains, shifts, weights):
    d = cot.shape[-1]
    heads = weights[0].shape[1] // HEAD
    ff = weights[4].shape[1]
    unit = (PER_SEG, 4, PART, d)
    own = (PER_SEG, PART, d)
    keys = KINDS * SEG
    any_space = pl.BlockSpec(memory_space=pl.ANY)
    smem = pl.BlockSpec(memory_space=pltpu.SMEM)
    vmem = pl.BlockSpec(memory_space=pltpu.VMEM)
    shapes = [
        ((2, KINDS) + unit, BF),
        ((2, KINDS) + own, BF),
        ((2, heads, SEG, HEAD), BF),
        ((2, heads, keys, HEAD), BF),
        ((2, heads, keys, HEAD), BF),
        ((2, heads, SEG, keys), BF),
        ((2, heads, SEG, HEAD), BF),
        ((2,) + own, BF),
        ((2,) + own, F32),
        ((2, PER_SEG, 2, 2, PART, d), BF),
        ((d, 2 * ff), BF),
        ((2, 8, d), F32),
    ]
    dma = pltpu.SemaphoreType.DMA
    split = (PER_SEG, 2, 2, PART, d)
    scratch = [
        pltpu.VMEM((2, KINDS) + unit, BF),
        pltpu.VMEM((2,) + unit, BF),
        pltpu.VMEM((2, KINDS) + own, BF),
        pltpu.VMEM((2, heads, SEG, HEAD), BF),
        pltpu.VMEM((2, heads, keys, HEAD), BF),
        pltpu.VMEM((2, heads, keys, HEAD), BF),
        pltpu.VMEM((2, SEG, keys), BF),
        pltpu.VMEM((2, heads, SEG, HEAD), BF),
        pltpu.VMEM((d, 3 * heads * HEAD), BF),
        pltpu.VMEM((heads * HEAD, d), BF),
        pltpu.VMEM((d, ff), BF),
        pltpu.VMEM((ff, d), BF),
        [pltpu.VMEM(split, BF) for _ in range(6)],
        [pltpu.VMEM((PER_SEG, 2, PART, d), BF) for _ in range(6)],
        [pltpu.VMEM(own, BF) for _ in range(6)],
        pltpu.VMEM((2,) + split, BF),
        pltpu.VMEM((2,) + split, BF),
        pltpu.VMEM((2, SEG, ff), BF),
        pltpu.VMEM((2, SEG, ff), BF),
        pltpu.VMEM((2,) + own, F32),
        pltpu.VMEM((2,) + own, F32),
        pltpu.VMEM((2,) + own, BF),
        pltpu.VMEM((d, 2 * ff), BF),
        pltpu.VMEM((2, 8, d), F32),
        dma((6,)),
        dma((11,)),
        dma((2, heads)),
        dma((KINDS + 1, 2, PER_SEG)),
        dma((KINDS + 1, 2, PER_DEV)),
        dma((KINDS + 1, 2, PER_SEG)),
        dma((KINDS + 1, 2, PER_SEG)),
        dma((KINDS + 1, 2, PER_SEG)),
        dma((6, 2)),
        dma((6, 2)),
        dma((4, 2)),
        dma((4, 2)),
    ]
    return pl.pallas_call(
        forward_kernel,
        out_shape=[jax.ShapeDtypeStruct(shape, kind) for shape, kind in shapes],
        in_specs=[[any_space] * KINDS, any_space, smem, smem, smem, vmem, vmem] + [any_space] * 6,
        out_specs=[any_space] * len(shapes),
        scratch_shapes=scratch,
        compiler_params=pltpu.CompilerParams(
            collective_id=1, has_side_effects=True, vmem_limit_bytes=62 << 20
        ),
    )(rows, cot, bound, link, slopes, gains, shifts, *weights)


class SeqReduce:
    def __init__(self, me, grads, total, landed, sems, groups, width):
        self.me, self.grads, self.total, self.landed = me, grads, total, landed
        self.send, self.recv = sems
        self.groups, self.width = groups, width
        self.bits = me.count.bit_length() - 1
        self.mine = [lax.rem(lax.div(me.seq, 1 << b), 2) for b in range(self.bits)]
        self.turn_at = 0

    def cols(self, chunk):
        return pl.ds(chunk * self.width, self.width)

    def plan(self, chunk):
        return [(i + chunk % 2) % self.bits for i in range(self.bits)]

    def index(self, chunk, step, own):
        plan = self.plan(chunk)
        out = []
        for b in reversed(range(self.bits)):
            if b in plan[:step] or (b == plan[step] and own):
                out.append(self.mine[b])
            elif b == plan[step]:
                out.append(1 - self.mine[b])
            else:
                out.append(slice(None))
        return tuple(out) + (slice(None), self.cols(chunk))

    def spot(self, chunk, step):
        return (slice(None),) * (self.bits - step) + (self.cols(chunk),)

    def copy(self, chunk, step):
        bit = self.plan(chunk)[step]
        return remote(
            self.grads.at[self.index(chunk, step, False)],
            self.landed[step].at[self.spot(chunk, step)],
            self.send.at[step, chunk],
            self.recv.at[step, chunk],
            self.me.beside((1 - 2 * self.mine[bit]) * (1 << bit)),
        )

    def finish(self, chunk, step):
        self.copy(chunk, step).wait()
        here = self.index(chunk, step, True)
        added = self.grads[here].astype(F32) + self.landed[step][self.spot(chunk, step)].astype(F32)
        if step == self.bits - 1:
            self.total[:, self.cols(chunk)] = added
        else:
            self.grads[here] = added.astype(BF)
            self.copy(chunk, step + 1).start()

    def turn(self):
        at = self.turn_at
        self.turn_at += 1
        for step in reversed(range(self.bits)):
            group = at - step - 1
            if 0 <= group < len(self.groups):
                for chunk in self.groups[group]:
                    self.finish(chunk, step)
        if at < len(self.groups):
            for chunk in self.groups[at]:
                self.copy(chunk, 0).start()

    def drain(self):
        while self.turn_at < len(self.groups) + self.bits:
            self.turn()


FINALS = 4


def backward_kernel(
    normed_hbm,
    own_hbm,
    q_hbm,
    k_hbm,
    v_hbm,
    prob_hbm,
    ctx_hbm,
    out_hbm,
    dhid_hbm,
    datt_hbm,
    gffn_hbm,
    gcomp_hbm,
    win_hbm,
    gains,
    w_query,
    w_key,
    w_value,
    w_out,
    finals,
    total_hbm,
    vec_hbm,
    aux_hbm,
    normed_ref,
    own_ref,
    q_ref,
    kx_ref,
    v_ref,
    prob_ref,
    ctx_ref,
    dhid_ref,
    datt_ref,
    wqkv_ref,
    wo_ref,
    dctx_ref,
    ds_ref,
    dqkv_ref,
    parts,
    firsts,
    seconds,
    win_part,
    win_first,
    win_second,
    home_ref,
    owner_ref,
    grads_ref,
    total_ref,
    landed,
    vec_ref,
    aux_ref,
    load_sem,
    save_sem,
    rs_send,
    rs_recv,
    ag_send,
    ag_recv,
    ag_here,
    move_send,
    move_recv,
    seq_send,
    seq_recv,
):
    me = Place()
    d = normed_ref.shape[-1]
    heads = q_ref.shape[1]
    width = heads * HEAD
    bits = me.count.bit_length() - 1
    lead = (slice(None),) * (bits + 1)
    ffn_cols, comp_cols = gffn_hbm.shape[-1], gcomp_hbm.shape[-1]
    late = ffn_cols + comp_cols

    load_pairs = [
        (datt_hbm, datt_ref),
        (w_out, wo_ref),
        (v_hbm, v_ref),
        (ctx_hbm, ctx_ref),
        (prob_hbm.at[0], prob_ref.at[0]),
        (k_hbm, kx_ref.at[:, :, :, pl.ds(0, HEAD)]),
        (q_hbm, q_ref),
        (win_hbm, win_part),
        (gffn_hbm, grads_ref.at[lead + (pl.ds(0, ffn_cols),)]),
        (gcomp_hbm, grads_ref.at[lead + (pl.ds(ffn_cols, comp_cols),)]),
        (w_key, wqkv_ref.at[:, pl.ds(0, width)]),
        (w_value, wqkv_ref.at[:, pl.ds(width, width)]),
        (w_query, wqkv_ref.at[:, pl.ds(2 * width, width)]),
        (prob_hbm.at[1], prob_ref.at[1]),
        (own_hbm, own_ref),
        (dhid_hbm, dhid_ref),
        (normed_hbm, normed_ref),
    ]
    loads = [
        pltpu.make_async_copy(src, dst, load_sem.at[i]) for i, (src, dst) in enumerate(load_pairs)
    ]
    for load in loads:
        load.start()

    meet(me, True)

    gain_0 = gains[0:1]
    vec_ref[...] = jnp.zeros(vec_ref.shape, F32)
    aux_ref[...] = jnp.zeros(aux_ref.shape, F32)
    key_at = lax.broadcasted_iota(jnp.int32, (KINDS * SEG, HEAD), 0)
    lane = lax.broadcasted_iota(jnp.int32, (KINDS * SEG, HEAD), 1)
    kind_at = lax.div(key_at, SEG)
    in_kind = key_at - SEG * kind_at
    odd = lax.rem(in_kind, 2)
    marks = jnp.where(
        lane == 0,
        in_kind - odd,
        jnp.where(lane == 1, odd, jnp.where(lane == 2, kind_at, jnp.where(lane == 3, 1, 0))),
    )
    marks = marks.astype(F32).astype(BF)
    for u in range(2):
        for h in range(heads):
            kx_ref[u, h, :, HEAD:] = marks

    rs = (rs_send, rs_recv)
    win = TpReduce(me, win_part, win_first, win_second, rs, 2 * KINDS)
    groups = [[0, 1], [2, 3], [4, 5], [6, 7], [8, 9], [10], [11, 12], [13, 14]]
    seq = SeqReduce(me, grads_ref, total_ref, landed, (seq_send, seq_recv), groups, 256)


    def to_owner(kind, slot):
        segment, micro, there = units_of(me.column, slot)

        @pl.loop(0, PER_SEG)
        def _(chunk):
            place = PER_SEG * segment + chunk
            holder = lax.div(place, PER_DEV)
            q = lax.rem(place, PER_DEV)
            src = out_hbm.at[slot, chunk] if kind == KINDS else home_ref.at[kind, slot, chunk]
            dst = owner_ref.at[kind, micro, q]

            @pl.when(jnp.logical_and(there, holder == me.column))
            def _():
                pltpu.make_async_copy(src, dst, move_recv.at[kind, micro, q]).start()

            @pl.when(jnp.logical_and(there, holder != me.column))
            def _():
                remote(
                    src,
                    dst,
                    move_send.at[kind, slot, chunk],
                    move_recv.at[kind, micro, q],
                    me.beside(holder - me.column),
                ).start()

    def sent(kind, slot):
        segment, micro, there = units_of(me.column, slot)

        @pl.loop(0, PER_SEG)
        def _(chunk):
            holder = lax.div(PER_SEG * segment + chunk, PER_DEV)

            @pl.when(jnp.logical_and(there, holder != me.column))
            def _():
                src = home_ref.at[0, slot, chunk]
                remote(
                    src,
                    src,
                    move_send.at[kind, slot, chunk],
                    move_recv.at[kind, 0, 0],
                    me.mate(),
                ).wait_send()

    def collect(kind, micro):
        @pl.loop(0, PER_DEV)
        def _(q):
            segment = jnp.where(q < me.column, me.column - 1, me.column)
            home, slot = home_of(segment, micro)
            dst = owner_ref.at[kind, micro, q]

            @pl.when(home == me.column)
            def _():
                pltpu.make_async_copy(dst, dst, move_recv.at[kind, micro, q]).wait()

            @pl.when(home != me.column)
            def _():
                remote(
                    dst,
                    dst,
                    move_send.at[kind, 0, 0],
                    move_recv.at[kind, micro, q],
                    me.mate(),
                ).wait_recv()

    class Final:
        def __init__(self, kind, micro):
            self.own = owner_ref.at[kind, micro]
            whole = finals[kind].at[micro]
            self.mine = whole.at[:, me.high, me.low]
            self.here = pltpu.make_async_copy(self.own, self.mine, ag_here.at[kind, micro])
            self.one = remote(
                self.own,
                self.mine,
                ag_send.at[kind, micro, 0],
                ag_recv.at[kind, micro, 0],
                me.across(),
            )
            both = whole.at[:, :, me.low]
            self.two = remote(
                both, both, ag_send.at[kind, micro, 1], ag_recv.at[kind, micro, 1], me.mate()
            )

        def start(self):
            self.here.start()
            self.one.start()

        def middle(self):
            self.here.wait()
            self.one.wait()
            self.two.start()

        def end(self):
            self.two.wait()

    def context_back(u):
        datt = datt_ref[u].reshape(SEG, d)
        for h in range(heads):
            rows = slice(h * HEAD, (h + 1) * HEAD)
            dctx_ref[u, h] = dot_second_t(datt, wo_ref[rows]).astype(BF)

    def attend_back(u, h):
        scale = HEAD ** (-0.5)

        @pl.loop(0, SEG // QUERY_BLOCK)
        def _(b):
            rows = pl.ds(pl.multiple_of(b * QUERY_BLOCK, QUERY_BLOCK), QUERY_BLOCK)
            d_ctx = dctx_ref[u, h, rows]
            d_prob = dot_second_t(d_ctx, v_ref[u, h])
            prob = prob_ref[u, h, rows].astype(F32)
            mean = jnp.sum(prob * d_prob, axis=-1, keepdims=True) / jnp.sum(
                prob, axis=-1, keepdims=True
            )
            d_scores = (prob * (d_prob - mean)).astype(BF)
            ds_ref[rows] = d_scores
            both = dot_plain(d_scores, kx_ref[u, h])
            dqkv_ref[u, 0, rows, 2 * width + h * HEAD : 2 * width + (h + 1) * HEAD] = (
                both[:, :HEAD] * scale
            ).astype(BF)
            marked = both[:, HEAD:]
            at = (b * QUERY_BLOCK + lax.broadcasted_iota(jnp.int32, (QUERY_BLOCK, HEAD), 0)).astype(F32)
            aux_ref[h, 0:1] += jnp.sum(marked, axis=0, keepdims=True)
            aux_ref[h, 1:2] += jnp.sum(marked * at, axis=0, keepdims=True)

        for kind in range(KINDS):
            for part in range(2):
                span = SEG // 2
                keys = slice(kind * SEG + part * span, kind * SEG + (part + 1) * span)
                rows = slice(part * span, (part + 1) * span)
                d_key = dot_first_t(ds_ref[:, keys], q_ref[u, h]) * scale
                d_value = dot_first_t(prob_ref[u, h, :, keys], dctx_ref[u, h])
                cols = slice(h * HEAD, (h + 1) * HEAD)
                dqkv_ref[u, kind, rows, cols] = d_key.astype(BF)
                cols = slice(width + h * HEAD, width + (h + 1) * HEAD)
                dqkv_ref[u, kind, rows, cols] = d_value.astype(BF)

    def project_back(u, kind, part):
        depth = (3 if kind == 0 else 2) * width

        @pl.loop(0, d // 256)
        def _(n):
            cols = pl.ds(pl.multiple_of(n * 256, 256), 256)
            tile = dot_second_t(dqkv_ref[u, kind, :, :depth], wqkv_ref[cols, :depth])
            part[:, :, :, :, cols] = tile.astype(BF).reshape(PER_SEG, 2, 2, PART, 256)

    def norm_end(u, kind, task):
        task.end()

        @pl.loop(0, PER_SEG)
        def _(k):
            scaled, inverse = center_of(own_ref[u, kind, k].astype(F32))
            grad = task.total(k)
            vec_ref[0] += eights(grad * scaled)
            vec_ref[1] += eights(grad)
            result = norm_back(grad, scaled, inverse, gain_0)
            if kind == 0:
                result += dhid_ref[u, k]
            home_ref[kind, u, k] = result.astype(BF)

    def add_window(micro):
        @pl.loop(0, PER_DEV)
        def _(q):
            added = owner_ref[1, micro, q].astype(F32) + win.total(micro * PER_DEV + q)
            owner_ref[1, micro, q] = added.astype(BF)

    def to_grads(rows_from, cols_from, tile):
        per = d // me.count
        n = tile.shape[0] // per
        flat = tile.astype(BF).reshape((n, per, tile.shape[1]))
        for i in range(n):
            at = rows_from // per + i
            index = tuple((at >> b) & 1 for b in reversed(range(bits)))
            grads_ref[index + (slice(None), pl.ds(cols_from, tile.shape[1]))] = flat[i]

    def late_grads():
        for n in range(d // 256):
            cols = slice(n * 256, (n + 1) * 256)
            kv = None
            for u in range(2):
                for kind in range(KINDS):
                    left = normed_ref[u, kind, :, :, :, cols].reshape(SEG, 256)
                    term = dot_first_t(left, dqkv_ref[u, kind, :, : 2 * width])
                    kv = term if kv is None else kv + term
            query = None
            for u in range(2):
                left = normed_ref[u, 0, :, :, :, cols].reshape(SEG, 256)
                term = dot_first_t(left, dqkv_ref[u, 0, :, 2 * width :])
                query = term if query is None else query + term
            to_grads(n * 256, late, kv)
            to_grads(n * 256, late + 2 * width, query)
            for h in range(heads):
                out = None
                for u in range(2):
                    left = datt_ref[u, :, :, :, :, cols].reshape(SEG, 256)
                    term = dot_first_t(left, ctx_ref[u, h])
                    out = term if out is None else out + term
                to_grads(n * 256, late + 3 * width + h * HEAD, out)

    results = {}

    def final_start(kind, micro):
        collect(kind, micro)
        if kind == 1:
            add_window(micro)
        results[kind, micro] = Final(kind, micro)
        results[kind, micro].start()

    to_owner(KINDS, 0)
    to_owner(KINDS, 1)
    loads[7].wait()
    win.start()
    loads[8].wait()
    loads[9].wait()
    seq.turn()
    for load in loads[:4]:
        load.wait()
    context_back(0)
    for load in loads[4:7]:
        load.wait()
    attend_back(0, 0)
    win.middle()
    seq.turn()
    final_start(KINDS, 0)
    attend_back(0, 1)
    for load in loads[10:13]:
        load.wait()
    seq.turn()
    final_start(KINDS, 1)
    tasks = [
        TpReduce(me, parts[i % KINDS], firsts[i], seconds[i], rs, i) for i in range(2 * KINDS)
    ]
    for kind in range(KINDS):
        project_back(0, kind, parts[kind])
        tasks[kind].start()
    seq.turn()
    loads[13].wait()
    context_back(1)
    for kind in range(KINDS):
        tasks[kind].middle()
    win.end()
    attend_back(1, 0)
    results[KINDS, 0].middle()
    results[KINDS, 1].middle()
    seq.turn()
    for load in loads[14:16]:
        load.wait()
    for kind in range(KINDS):
        norm_end(0, kind, tasks[kind])
        to_owner(kind, 0)
    attend_back(1, 1)
    seq.turn()
    for kind in range(KINDS):
        project_back(1, kind, parts[kind])
        tasks[KINDS + kind].start()
    for kind in range(KINDS):
        final_start(kind, 0)
    loads[16].wait()
    late_grads()
    for kind in range(KINDS):
        tasks[KINDS + kind].middle()
    seq.turn()
    seq.turn()
    for kind in range(KINDS):
        results[kind, 0].middle()
    for kind in range(KINDS):
        norm_end(1, kind, tasks[KINDS + kind])
        to_owner(kind, 1)
    seq.turn()
    for kind in range(KINDS):
        final_start(kind, 1)
    seq.turn()
    for kind in range(KINDS):
        results[kind, 1].middle()
    seq.drain()
    saves = [
        pltpu.make_async_copy(total_ref, total_hbm, save_sem.at[0]),
        pltpu.make_async_copy(vec_ref, vec_hbm, save_sem.at[1]),
        pltpu.make_async_copy(aux_ref, aux_hbm, save_sem.at[2]),
    ]
    for save in saves:
        save.start()
    for kind in range(FINALS):
        for at in range(2):
            results[kind, at].end()
            sent(kind, at)
    for save in saves:
        save.wait()


def backward_call(saved, gcomp, win, gains, weights):
    normed, own, q, k, v, prob, ctx, out, dhid, datt, gffn = saved
    count = lax.axis_size("seq")
    bits = count.bit_length() - 1
    d = normed.shape[-1]
    heads = q.shape[1]
    keys = KINDS * SEG
    width = heads * HEAD
    columns = gffn.shape[1] + gcomp.shape[1] + 4 * width
    view = (2,) * bits + (d // count,)
    split = (PER_SEG, 2, 2, PART, d)
    owned = (2 * PER_DEV, 2, 2, PART, d)
    any_space = pl.BlockSpec(memory_space=pl.ANY)
    vmem = pl.BlockSpec(memory_space=pltpu.VMEM)
    dma = pltpu.SemaphoreType.DMA
    chunks = columns // 256
    final = jax.ShapeDtypeStruct((2, PER_DEV, 2, 2, PART, d), BF)
    scratch = [
        pltpu.VMEM(normed.shape, BF),
        pltpu.VMEM(own.shape, BF),
        pltpu.VMEM(q.shape, BF),
        pltpu.VMEM((2, heads, keys, 2 * HEAD), BF),
        pltpu.VMEM(v.shape, BF),
        pltpu.VMEM(prob.shape, BF),
        pltpu.VMEM(ctx.shape, BF),
        pltpu.VMEM(dhid.shape, F32),
        pltpu.VMEM(datt.shape, BF),
        pltpu.VMEM((d, 3 * width), BF),
        pltpu.VMEM((width, d), BF),
        pltpu.VMEM((2, heads, SEG, HEAD), BF),
        pltpu.VMEM((SEG, keys), BF),
        pltpu.VMEM((2, KINDS, SEG, 3 * width), BF),
        [pltpu.VMEM(split, BF) for _ in range(KINDS)],
        [pltpu.VMEM((PER_SEG, 2, PART, d), BF) for _ in range(2 * KINDS)],
        [pltpu.VMEM((PER_SEG, PART, d), BF) for _ in range(2 * KINDS)],
        pltpu.VMEM(owned, BF),
        pltpu.VMEM((2 * PER_DEV, 2, PART, d), BF),
        pltpu.VMEM((2 * PER_DEV, PART, d), BF),
        pltpu.VMEM((KINDS, 2, PER_SEG, PART, d), BF),
        pltpu.VMEM((FINALS, 2, PER_DEV, PART, d), BF),
        pltpu.VMEM(view + (columns,), BF),
        pltpu.VMEM((d // count, columns), F32),
        [pltpu.VMEM((2,) * (bits - 1 - i) + (d // count, columns), BF) for i in range(bits)],
        pltpu.VMEM((2, 8, d), F32),
        pltpu.VMEM((heads, 8, HEAD), F32),
        dma((17,)),
        dma((3,)),
        dma((2 * KINDS + 1, 2)),
        dma((2 * KINDS + 1, 2)),
        dma((FINALS, 2, 2)),
        dma((FINALS, 2, 2)),
        dma((FINALS, 2)),
        dma((FINALS, 2, PER_SEG)),
        dma((FINALS, 2, PER_DEV)),
        dma((bits, chunks)),
        dma((bits, chunks)),
    ]
    return pl.pallas_call(
        backward_kernel,
        out_shape=[
            [final] * FINALS,
            jax.ShapeDtypeStruct((d // count, columns), F32),
            jax.ShapeDtypeStruct((2, 8, d), F32),
            jax.ShapeDtypeStruct((heads, 8, HEAD), F32),
        ],
        in_specs=[any_space] * 13 + [vmem] + [any_space] * 4,
        out_specs=[[any_space] * FINALS] + [any_space] * 3,
        scratch_shapes=scratch,
        compiler_params=pltpu.CompilerParams(
            collective_id=2, has_side_effects=True, vmem_limit_bytes=63 << 20
        ),
    )(
        normed,
        own,
        q,
        k,
        v,
        prob,
        ctx,
        out,
        dhid,
        datt,
        gffn.reshape(view + (gffn.shape[1],)),
        gcomp.reshape(view + (gcomp.shape[1],)),
        win,
        gains,
        *weights,
    )


def shifted(block, distance):
    devices = range(lax.axis_size("seq"))
    route = [(i - distance, i) for i in devices if i - distance in devices]
    return lax.ppermute(block, "seq", route)


def compress(memory, cot_new, w_comp, column):
    rows = memory.shape[1]
    slots = cot_new.shape[1]
    after = shifted(memory[:, :REACH], -1)
    before = shifted(cot_new[:, slots - LEAD :], 1)
    extended = jnp.concatenate([memory, after], axis=1)
    cot_all = jnp.concatenate([before, cot_new], axis=1)
    slot = slots * column - LEAD + jnp.arange(slots + LEAD, dtype=jnp.int32)
    slot_seg = jnp.where(slot < 0, -1, slot // CSEG)
    slot_at = slot - slot_seg * CSEG
    row_at = jnp.arange(rows + REACH, dtype=jnp.int32)
    fresh, grad, d_rows = 0.0, [], 0.0
    for tap in range(3):
        place = 3 * slot_at + tap
        local = jnp.where(place < SEG, slot_seg * SEG + place - rows * column, -1)
        pick = (local[:, None] == row_at[None, :]).astype(BF)
        taken = jnp.einsum(
            "tr,mrd->mtd", pick[LEAD:], extended, preferred_element_type=F32
        ).astype(BF)
        fresh = fresh + jnp.einsum("mtd,de->mte", taken, w_comp[tap], preferred_element_type=F32)
        grad.append(jnp.einsum("mtd,mte->de", taken, cot_new, preferred_element_type=F32))
        d_taken = jnp.einsum(
            "mte,de->mtd", cot_all, w_comp[tap], preferred_element_type=F32
        ).astype(BF)
        d_rows = d_rows + jnp.einsum(
            "tr,mtd->mrd", pick[:, :rows], d_taken, preferred_element_type=F32
        )
    return fresh, jnp.concatenate(grad, axis=1).astype(BF), d_rows.astype(BF)


def per_device(
    inputs,
    memory,
    compressed,
    boundary,
    links,
    gains,
    shifts,
    slopes,
    w_query,
    w_key,
    w_value,
    w_out,
    w_in,
    w_down,
    w_comp,
    cot_out,
    cot_new,
):
    d = inputs.shape[-1]
    rows = inputs.shape[1]
    heads = slopes.shape[0]
    width = heads * HEAD
    ff = w_in.shape[1]
    feats = w_comp.shape[2]
    count = lax.axis_size("seq")
    seq = lax.axis_index("seq")
    tp = lax.axis_index("tp")
    column = lax.rem(seq, PER_SEG)
    base = lax.div(seq, PER_SEG) * PER_DEV
    edges, linked = [], []
    for slot in range(2):
        segment, micro, _ = units_of(column, slot)
        segment = jnp.minimum(segment, PER_DEV - 1) + base
        edges.append(boundary[micro, segment])
        linked.append(links[micro, segment])

    def chunked(array):
        return array.reshape(2, PER_DEV, 4, PART, d)

    saved = forward_call(
        [chunked(inputs), chunked(memory), chunked(compressed)],
        chunked(cot_out),
        jnp.stack(edges),
        jnp.stack(linked),
        slopes,
        gains,
        shifts,
        (w_query, w_key, w_value, w_out, w_in, w_down),
    )
    fresh, gcomp, d_rows = compress(memory, cot_new, w_comp, column)
    finals, total, vec_0, aux = backward_call(
        saved[:11],
        gcomp,
        d_rows.reshape(2 * PER_DEV, 2, 2, PART, d),
        gains,
        (w_query, w_key, w_value, w_out),
    )
    vec_1 = saved[11]
    aux = (aux[:, 0, 0] + aux[:, 0, 1] - SEG * aux[:, 0, 2] - aux[:, 1, 3]) / SEG
    tp_at = lax.broadcasted_iota(jnp.int32, (4, heads), 0)
    spread = jnp.where(tp_at == tp, aux[None, :], 0.0).reshape(1, 4 * heads)
    small = jnp.concatenate(
        [vec_0.sum(1), vec_1.sum(1), jnp.pad(spread, ((0, 0), (0, d - 4 * heads)))], axis=0
    )
    small = lax.psum(small, ("seq", "tp"))
    vectors = lax.dynamic_slice(small, (0, seq * (d // count)), (4, d // count))
    grad_slopes = lax.dynamic_slice(small, (4, tp * heads), (1, heads))[0]

    def whole(array):
        return array.reshape(2, rows, d)

    cuts = [ff, ff] + [feats] * 3 + [width] * 4
    pieces, at = [], 0
    for cut in cuts:
        pieces.append(total[:, at : at + cut])
        at += cut
    g_in, g_down, comp_0, comp_1, comp_2, g_key, g_value, g_query, g_out = pieces
    return (
        whole(finals[3]),
        whole(finals[0]).astype(F32),
        whole(finals[1]).astype(F32),
        whole(finals[2]).astype(F32),
        fresh,
        jnp.stack([vectors[0], vectors[2]]),
        jnp.stack([vectors[1], vectors[3]]),
        grad_slopes,
        g_query,
        g_key,
        g_value,
        g_out.T,
        g_in,
        g_down.T,
        jnp.stack([comp_0, comp_1, comp_2]),
    )


def solution(mesh):
    in_specs = (
        P(None, "seq", None),
        P(None, "seq", None),
        P(None, "seq", None),
        P(),
        P(),
        P(),
        P(),
        P("tp"),
        P(None, "tp"),
        P(None, "tp"),
        P(None, "tp"),
        P("tp", None),
        P(None, "tp"),
        P("tp", None),
        P(None, None, "tp"),
        P(None, "seq", None),
        P(None, "seq", "tp"),
    )
    out_specs = (
        P(None, "seq", None),
        P(None, "seq", None),
        P(None, "seq", None),
        P(None, "seq", None),
        P(None, "seq", "tp"),
        P(None, "seq"),
        P(None, "seq"),
        P("tp"),
        P("seq", "tp"),
        P("seq", "tp"),
        P("seq", "tp"),
        P("tp", "seq"),
        P("seq", "tp"),
        P("tp", "seq"),
        P(None, "seq", "tp"),
    )
    return jax.shard_map(
        per_device, mesh=mesh, in_specs=in_specs, out_specs=out_specs, check_vma=False
    )
```

```python
import functools
import math

import jax
import jax.numpy as jnp
from jax import lax
from jax.experimental import pallas as pl
from jax.experimental.pallas import tpu as pltpu
from jax.sharding import PartitionSpec as P

HEAD = 128
SEG = 512
CSEG = 176
REACH = 32
LEAD = 26
SLOT_PAD = 160
CHUNK = 64
PART = 16
KINDS = 3
NORM_EPS = 1e-05
MESH = pl.DeviceIdType.MESH
BF = jnp.bfloat16
F32 = jnp.float32
GELU_IN = math.sqrt(2.0 / math.pi)
PER_SEG = SEG // CHUNK
PER_DEV = PER_SEG - 1
QUERY_BLOCK = 128


def dot_plain(a, b):
    return jnp.dot(a, b, preferred_element_type=F32)


def dot_first_t(a, b):
    return lax.dot_general(a, b, (((0,), (0,)), ((), ())), preferred_element_type=F32)


def dot_second_t(a, b):
    return lax.dot_general(a, b, (((1,), (1,)), ((), ())), preferred_element_type=F32)


def home_of(segment, micro):
    middle = PER_DEV // 2
    home = jnp.where(
        segment < middle, segment, jnp.where(segment == middle, middle + micro, segment + 1)
    )
    slot = jnp.where(segment == middle, 0, micro)
    return home, slot


def units_of(place, slot):
    middle = PER_DEV // 2
    segment = jnp.where(place <= middle, place, place - 1)
    is_middle = segment == middle
    micro = jnp.where(is_middle, place - middle, slot)
    return segment, micro, jnp.logical_or(jnp.logical_not(is_middle), slot == 0)


class Place:
    def __init__(self):
        self.seq = lax.axis_index("seq")
        self.tp = lax.axis_index("tp")
        self.column = lax.rem(self.seq, PER_SEG)
        self.low = lax.rem(self.tp, 2)
        self.high = lax.div(self.tp, 2)
        self.count = lax.axis_size("seq")
        self.bits = self.count.bit_length() - 1
        self.bit = [lax.rem(lax.div(self.seq, 1 << b), 2) for b in range(self.bits)]

    def flipped(self, bit):
        return self.beside((1 - 2 * self.bit[bit]) * (1 << bit))

    def after(self):
        return (lax.rem(self.seq + 1, self.count), self.tp)

    def before(self):
        return (lax.rem(self.seq + self.count - 1, self.count), self.tp)

    def mate(self):
        return (self.seq, self.tp + 1 - 2 * self.low)

    def across(self):
        return (self.seq, self.tp + 2 - 4 * self.high)

    def corner(self):
        return (self.seq, self.tp + 3 - 2 * self.low - 4 * self.high)

    def beside(self, by):
        return (self.seq + by, self.tp)


def remote(src, dst, send, recv, device):
    return pltpu.make_async_remote_copy(
        src_ref=src,
        dst_ref=dst,
        send_sem=send,
        recv_sem=recv,
        device_id=device,
        device_id_type=MESH,
    )


class TpReduce:
    def __init__(self, me, part, first, second, sems, index):
        self.me, self.part, self.first, self.second = me, part, first, second
        send, recv = sems
        self.one = remote(
            part.at[:, :, 1 - me.low], first, send.at[index, 0], recv.at[index, 0], me.mate()
        )
        self.two = remote(
            part.at[:, 1 - me.high, me.low],
            second,
            send.at[index, 1],
            recv.at[index, 1],
            me.across(),
        )

    def start(self):
        self.one.start()

    def middle(self):
        self.one.wait()
        part, first, low = self.part, self.first, self.me.low

        @pl.loop(0, part.shape[0], step=2)
        def _(at):
            k = pl.ds(at, 2)
            added = part[k, :, low].astype(F32) + first[k].astype(F32)
            part[k, :, low] = added.astype(part.dtype)

        self.two.start()

    def end(self):
        self.two.wait()

    def total(self, k):
        me = self.me
        return self.part[k, me.high, me.low].astype(F32) + self.second[k].astype(F32)


class TpGather:
    def __init__(self, me, whole, sems, index):
        send, recv = sems
        mine = whole.at[:, me.high, me.low]
        self.one = remote(mine, mine, send.at[index, 0], recv.at[index, 0], me.across())
        both = whole.at[:, :, me.low]
        self.two = remote(both, both, send.at[index, 1], recv.at[index, 1], me.mate())

    def start(self):
        self.one.start()

    def middle(self):
        self.one.wait()
        self.two.start()

    def end(self):
        self.two.wait()


def meet(me, friends):
    barrier = pltpu.get_barrier_semaphore()
    for friend in friends:
        pl.semaphore_signal(barrier, inc=1, device_id=friend, device_id_type=MESH)
    pl.semaphore_wait(barrier, len(friends))


def center_of(rows):
    center = rows - jnp.mean(rows, axis=-1, keepdims=True)
    inverse = lax.rsqrt(jnp.mean(center * center, axis=-1, keepdims=True) + NORM_EPS)
    return center * inverse, inverse


def norm_back(grad, scaled, inverse, gain):
    weighted = grad * gain
    first = jnp.mean(weighted, axis=-1, keepdims=True)
    second = jnp.mean(weighted * scaled, axis=-1, keepdims=True)
    return inverse * (weighted - first - scaled * second)


def eights(rows):
    d = rows.shape[-1]
    return jnp.sum(rows.reshape(-1, PART // 2, d), axis=0)


class SeqReduce:
    width = 256

    def __init__(self, me, grads, total, landed, sems, groups):
        self.me, self.grads, self.total, self.landed = me, grads, total, landed
        self.send, self.recv = sems
        self.groups = groups
        self.turn_at = 0

    def cols(self, chunk):
        return pl.ds(chunk * self.width, self.width)

    def plan(self, chunk):
        first = 1 if chunk % 5 == 4 else 0
        return [(i + first) % self.me.bits for i in range(self.me.bits)]

    def index(self, chunk, step, own):
        plan = self.plan(chunk)
        out = [chunk]
        for b in reversed(range(self.me.bits)):
            if b in plan[:step] or (b == plan[step] and own):
                out.append(self.me.bit[b])
            elif b == plan[step]:
                out.append(1 - self.me.bit[b])
            else:
                out.append(slice(None))
        return tuple(out)

    def copy(self, chunk, step):
        return remote(
            self.grads.at[self.index(chunk, step, False)],
            self.landed[step].at[chunk],
            self.send.at[step, chunk],
            self.recv.at[step, chunk],
            self.me.flipped(self.plan(chunk)[step]),
        )

    def finish(self, chunk, step):
        self.copy(chunk, step).wait()
        here = self.index(chunk, step, True)
        added = self.grads[here].astype(F32) + self.landed[step][chunk].astype(F32)
        if step == self.me.bits - 1:
            self.total[:, self.cols(chunk)] = added
        else:
            self.grads[here] = added.astype(BF)
            self.copy(chunk, step + 1).start()

    def launch(self, group):
        for chunk in self.groups[group]:
            self.copy(chunk, 0).start()

    def turn(self):
        at = self.turn_at
        self.turn_at += 1
        for step in reversed(range(self.me.bits)):
            group = at - step
            if 0 <= group < len(self.groups):
                for chunk in self.groups[group]:
                    self.finish(chunk, step)

    def drain(self):
        while self.turn_at < len(self.groups) + self.me.bits - 1:
            self.turn()


def split_store(me, grads, rows_from, first, tile):
    per, wide = grads.shape[-2:]
    n = tile.shape[0] // per
    for c in range(tile.shape[1] // wide):
        parts = tile[:, c * wide : (c + 1) * wide].astype(BF).reshape((n, per, wide))
        for i in range(n):
            at = rows_from // per + i
            grads[(first + c,) + tuple((at >> b) & 1 for b in reversed(range(me.bits)))] = parts[i]


def forward_kernel(
    rows_hbm,
    cot_hbm,
    mem_hbm,
    cot_new,
    w_comp,
    boundary,
    links,
    slopes,
    gains,
    shifts,
    w_query,
    w_key,
    w_value,
    w_out,
    w_in,
    w_down,
    normed_hbm,
    own_hbm,
    q_hbm,
    k_hbm,
    v_hbm,
    lse_hbm,
    ctx_hbm,
    ctxn_hbm,
    out_hbm,
    dhid_hbm,
    datt_hbm,
    gffn_hbm,
    vec_hbm,
    win_hbm,
    fresh_hbm,
    comp_hbm,
    x_ref,
    raw_ref,
    cot_ref,
    q_ref,
    k_ref,
    v_ref,
    lse_ref,
    ctx_ref,
    ctxn_ref,
    all_ref,
    wqkv_ref,
    wo_ref,
    wi_ref,
    wd_ref,
    parts,
    back_parts,
    firsts,
    back_firsts,
    quarters,
    back_quarters,
    nh_ref,
    datt_ref,
    act_ref,
    du_ref,
    hid_ref,
    out_ref,
    vec_ref,
    ext_ref,
    cot_own,
    cot_prev,
    cot_pad,
    lead_pad,
    wc_ref,
    pick_ref,
    spread_ref,
    pool_ref,
    win_part,
    win_first,
    win_second,
    fresh_ref,
    comp_ref,
    comp_total,
    landed,
    load_sem,
    save_sem,
    stage_sem,
    place_sem,
    move_send,
    move_recv,
    pass_send,
    pass_recv,
    ctx_send,
    ctx_recv,
    wo_send,
    wo_recv,
    edge_send,
    edge_recv,
    rs_send,
    rs_recv,
    ag_send,
    ag_recv,
    seq_send,
    seq_recv,
):
    me = Place()
    d = x_ref.shape[-1]
    heads = q_ref.shape[1]
    width = heads * HEAD
    low, high = me.low, me.high
    kinds = list(range(KINDS))
    edge_rows = mem_hbm.shape[1]

    load_pairs = [
        (mem_hbm, ext_ref.at[:, pl.ds(0, edge_rows)]),
        (cot_new, cot_own),
        (w_comp, wc_ref),
        (w_key, wqkv_ref.at[:, pl.ds(0, width)]),
        (w_value, wqkv_ref.at[:, pl.ds(width, width)]),
        (w_query, wqkv_ref.at[:, pl.ds(2 * width, width)]),
        (w_out, wo_ref.at[pl.ds(pl.multiple_of(me.tp * width, width), width)]),
        (w_in, wi_ref),
        (w_down, wd_ref),
    ]
    loads = [
        pltpu.make_async_copy(src, dst, load_sem.at[i]) for i, (src, dst) in enumerate(load_pairs)
    ]
    for load in loads:
        load.start()

    meet(
        me,
        [me.mate(), me.across(), me.corner(), me.after(), me.before()]
        + [me.flipped(b) for b in range(me.bits)],
    )

    sources = [rows_hbm[0], rows_hbm[1], rows_hbm[2], cot_hbm]

    def landing(kind, slot, chunk):
        if kind == KINDS:
            return cot_ref.at[slot, chunk, :, low]
        return raw_ref.at[slot, kind, chunk]

    def route(micro, q):
        segment = jnp.where(q < me.column, me.column - 1, me.column)
        home, slot = home_of(segment, micro)
        return home, slot, PER_DEV * me.column + q - PER_SEG * segment

    def send_out(kinds, wanted):
        @pl.loop(0, 2 * PER_DEV)
        def _(at):
            micro, q = lax.div(at, PER_DEV), lax.rem(at, PER_DEV)
            home, slot, chunk = route(micro, q)
            here = home == me.column
            for kind in kinds:
                src = sources[kind].at[micro, q, :, low]
                dst = landing(kind, slot, chunk)

                @pl.when(jnp.logical_and(slot == wanted, here))
                def _():
                    pltpu.make_async_copy(src, dst, place_sem.at[kind, slot, chunk]).start()

                @pl.when(jnp.logical_and(slot == wanted, jnp.logical_not(here)))
                def _():
                    remote(
                        src,
                        dst,
                        move_send.at[kind, micro, q],
                        move_recv.at[kind, slot, chunk],
                        me.beside(home - me.column),
                    ).start()

    def sent(kinds, micro):
        @pl.loop(0, PER_DEV)
        def _(q):
            home, slot, chunk = route(micro, q)
            for kind in kinds:

                @pl.when(home != me.column)
                def _():
                    remote(
                        sources[kind].at[micro, q, :, low],
                        landing(kind, slot, chunk),
                        move_send.at[kind, micro, q],
                        move_recv.at[kind, slot, chunk],
                        me.beside(home - me.column),
                    ).wait_send()

    spans = []
    for slot in range(2):
        segment, _, there = units_of(me.column, slot)
        first = jnp.maximum(PER_DEV * me.column - PER_SEG * segment, 0)
        last = jnp.minimum(PER_DEV * me.column + PER_DEV - PER_SEG * segment, PER_SEG)
        spans.append((jnp.where(there, first, 0), jnp.where(there, last, PER_SEG), there))

    def wait_own(kind, slot, chunk):
        dst = landing(kind, slot, chunk)
        pltpu.make_async_copy(dst, dst, place_sem.at[kind, slot, chunk]).wait()

    def wait_moved(kind, slot, chunk):
        dst = landing(kind, slot, chunk)
        remote(
            dst, dst, move_send.at[kind, 0, 0], move_recv.at[kind, slot, chunk], me.mate()
        ).wait_recv()

    def over_own(kinds, slot, body):
        first, last, there = spans[slot]

        @pl.loop(first, last)
        def _(chunk):
            @pl.when(there)
            def _():
                for kind in kinds:
                    wait_own(kind, slot, chunk)

            body(chunk)

    def over_moved(kinds, slot, body):
        first, last, _ = spans[slot]

        def step(chunk):
            for kind in kinds:
                wait_moved(kind, slot, chunk)
            body(chunk)

        pl.loop(0, first)(step)
        pl.loop(last, PER_SEG)(step)

    gain_0, shift_0 = gains[0:1], shifts[0:1]
    gain_1, shift_1 = gains[1:2], shifts[1:2]

    def passing(kind, slot):
        here = cot_ref.at[slot, :, :, low] if kind == KINDS else x_ref.at[slot, kind, :, :, low]
        return remote(
            here, here, pass_send.at[kind, slot], pass_recv.at[kind, slot], me.mate()
        )

    def norm_chunk(u):
        def body(k):
            for kind in range(KINDS):
                raw = raw_ref[u, kind, k].reshape(2 * PART, d).astype(F32)
                scaled, _ = center_of(raw)
                normed = (scaled * gain_0 + shift_0).astype(BF)
                x_ref[u, kind, k, :, low] = normed.reshape(2, PART, d)

        return body

    def norm_own(u):
        over_own(kinds, u, norm_chunk(u))

    def norm_moved(u):
        over_moved(kinds, u, norm_chunk(u))
        for kind in kinds:
            passing(kind, u).start()

    def cot_pass(u):
        over_own([KINDS], u, lambda k: None)
        over_moved([KINDS], u, lambda k: None)
        passing(KINDS, u).start()

    saves = []

    def save(src, dst):
        copy = pltpu.make_async_copy(src, dst, save_sem.at[len(saves)])
        copy.start()
        saves.append(copy)

    def project(u):
        for kind in range(KINDS):
            passing(kind, u).wait()
            normed = x_ref[u, kind].reshape(SEG, d)
            span = pl.ds(kind * SEG, SEG)
            keys = dot_plain(normed, wqkv_ref[:, :width]).astype(BF)
            values = dot_plain(normed, wqkv_ref[:, width : 2 * width]).astype(BF)
            for h in range(heads):
                cols = slice(h * HEAD, (h + 1) * HEAD)
                k_ref[u, h, span] = keys[:, cols]
                v_ref[u, h, span] = values[:, cols]
            if kind == 0:
                queries = dot_plain(normed, wqkv_ref[:, 2 * width :]).astype(BF)
                for h in range(heads):
                    q_ref[u, h] = queries[:, h * HEAD : (h + 1) * HEAD]
        save(x_ref.at[u], normed_hbm.at[u])

    segments = lax.div(me.seq, PER_SEG) * PER_DEV

    def attend(u, h):
        scale = HEAD ** (-0.5)
        slope = slopes[h]
        segment, micro, _ = units_of(me.column, u)
        segment = jnp.minimum(segment, PER_DEV - 1) + segments
        edge = boundary[micro, segment]
        linked = links[micro, segment]
        key_at = lax.broadcasted_iota(jnp.int32, (1, KINDS * SEG), 1)
        kind_at = lax.div(key_at, SEG)
        bias = (key_at - 2 * SEG * kind_at).astype(F32) * (slope / SEG)
        key_x = lax.broadcasted_iota(jnp.int32, (QUERY_BLOCK, SEG), 1)
        per = QUERY_BLOCK // CHUNK

        @pl.loop(0, SEG // QUERY_BLOCK)
        def _(b):
            rows = pl.ds(pl.multiple_of(b * QUERY_BLOCK, QUERY_BLOCK), QUERY_BLOCK)
            raw = dot_second_t(q_ref[u, h, rows], k_ref[u, h]) * scale + bias
            at = b * QUERY_BLOCK + lax.broadcasted_iota(jnp.int32, (QUERY_BLOCK, SEG), 0)
            seen = jnp.logical_and(key_x <= at, jnp.logical_or(key_x >= edge, at < edge))
            near = jnp.where(seen, raw[:, :SEG], -1e30)
            open_row = jnp.logical_and(at[:, :1] < edge, linked == 1)
            far = jnp.where(open_row, raw[:, SEG:], -1e30)
            top = jnp.maximum(
                jnp.max(near, axis=-1, keepdims=True), jnp.max(far, axis=-1, keepdims=True)
            )
            near = jnp.exp(near - top)
            far = jnp.exp(far - top)
            whole = jnp.sum(near, axis=-1, keepdims=True) + jnp.sum(far, axis=-1, keepdims=True)
            lse_ref[u, h, rows] = jnp.broadcast_to(top + jnp.log(whole), (QUERY_BLOCK, HEAD))
            share = 1.0 / whole
            near = near * share
            far = far * share
            near_low = near.astype(BF)
            far_low = far.astype(BF)
            value_x, value_far = v_ref[u, h, :SEG], v_ref[u, h, SEG:]
            context = dot_plain(near_low, value_x) + dot_plain(far_low, value_far)
            near_rest = (near - near_low.astype(F32)).astype(BF)
            far_rest = (far - far_low.astype(F32)).astype(BF)
            rest = dot_plain(near_rest, value_x) + dot_plain(far_rest, value_far)
            ctxn_ref[u, h, rows] = context + rest
            ctx_ref[u, pl.ds(b * per, per), :, :, :, h * HEAD : (h + 1) * HEAD] = (
                context.astype(BF).reshape(per, 2, 2, PART, HEAD)
            )

    def my_columns(tp):
        return pl.ds(pl.multiple_of(tp * width, width), width)

    def ctx_copies(u):
        dst = all_ref.at[u, :, :, :, my_columns(me.tp)]
        same, other = ctx_ref.at[u, :, :, low], ctx_ref.at[u, :, :, 1 - low]
        return [
            remote(src, dst, ctx_send.at[u, i], ctx_recv.at[u, i], device)
            for i, (src, device) in enumerate(
                [(same, me.across()), (other, me.corner()), (other, me.mate())]
            )
        ]

    def ctx_start(u):
        for copy in ctx_copies(u):
            copy.start()
        all_ref[u, :, :, :, my_columns(me.tp)] = ctx_ref[u, :, :, low]
        save(ctx_ref.at[u], ctx_hbm.at[u])
        save(ctxn_ref.at[u], ctxn_hbm.at[u])

    def wo_rows(tp):
        return wo_ref.at[pl.ds(pl.multiple_of(tp * width, width), width)]

    across_tp = me.tp + 2 - 4 * high
    mate_tp = me.tp + 1 - 2 * low
    wo_copies = [
        remote(w_out, wo_rows(me.tp), wo_send.at[0], wo_recv.at[0], me.across()),
        remote(w_out, wo_rows(me.tp), wo_send.at[1], wo_recv.at[1], me.mate()),
        remote(
            wo_rows(across_tp), wo_rows(across_tp), wo_send.at[2], wo_recv.at[2], me.mate()
        ),
    ]

    def half_pass(ref, u, kind):
        here = ref.at[u, :, :, low]
        return remote(here, here, pass_send.at[kind, u], pass_recv.at[kind, u], me.mate())

    def hidden_norm(u):
        for copy in ctx_copies(u):
            copy.wait()

        @pl.loop(0, 2)
        def _(r):
            some = pl.ds(r * (PER_SEG // 2), PER_SEG // 2)
            rows = SEG // 4
            hidden = dot_plain(all_ref[u, some].reshape(rows, 4 * width), wo_ref[...])
            hidden += raw_ref[u, 0, some].reshape(rows, d).astype(F32)
            hid_ref[u, some] = hidden.reshape(PER_SEG // 2, 2, PART, d)
            scaled, _ = center_of(hidden)
            normed = (scaled * gain_1 + shift_1).astype(BF)
            nh_ref[u, some, :, low] = normed.reshape(PER_SEG // 2, 2, PART, d)

        half_pass(nh_ref, u, KINDS + 1).start()

    def store_part(part, cols, tile):
        part[:, :, :, :, cols] = tile.astype(part.dtype).reshape(
            PER_SEG, 2, 2, PART, tile.shape[1]
        )

    def ffn_up(u):
        ff = wi_ref.shape[1]

        @pl.loop(0, ff // 256)
        def _(n):
            cols = pl.ds(pl.multiple_of(n * 256, 256), 256)
            for r in range(2):
                chunks = slice(r * PER_SEG // 2, (r + 1) * PER_SEG // 2)
                rows = slice(r * SEG // 2, (r + 1) * SEG // 2)
                upper = dot_plain(nh_ref[u, chunks].reshape(SEG // 2, d), wi_ref[:, cols])
                d_act = dot_second_t(cot_ref[u, chunks].reshape(SEG // 2, d), wd_ref[cols])
                square = upper * upper
                inner = GELU_IN * upper * (1.0 + 0.044715 * square)
                bend = jnp.tanh(inner)
                grown = 0.5 * (1.0 + bend)
                act_ref[u, rows, cols] = (upper * grown).astype(BF)
                slope = grown + 0.5 * upper * (1.0 - bend * bend) * (
                    GELU_IN * (1.0 + 3.0 * 0.044715 * square)
                )
                du_ref[u, rows, cols] = (d_act * slope).astype(BF)

    def ffn_out(u, part):
        @pl.loop(0, d // 256)
        def _(n):
            cols = pl.ds(pl.multiple_of(n * 256, 256), 256)
            store_part(part, cols, dot_plain(act_ref[u], wd_ref[:, cols]))

    def ffn_back(u, part):
        @pl.loop(0, d // 256)
        def _(n):
            cols = pl.ds(pl.multiple_of(n * 256, 256), 256)
            store_part(part, cols, dot_second_t(du_ref[u], wi_ref[cols]))

    def hidden_back(u, task):
        task.end()

        @pl.loop(0, PER_SEG, step=4)
        def _(at):
            k = pl.ds(at, 4)
            scaled, inverse = center_of(hid_ref[u, k, high])
            grad = task.total(k)
            cot = cot_ref[u, k, high, low].astype(F32)
            d_hidden = cot + norm_back(grad, scaled, inverse, gain_1)
            vec_ref[0] += eights(grad * scaled)
            vec_ref[1] += eights(grad)
            task.second[k] = d_hidden
            datt_ref[u, k, high, low] = d_hidden.astype(BF)

        datts[u].start()
        save(task.second, dhid_hbm.at[u])

    def out_end(u, task):
        task.end()

        @pl.loop(0, PER_SEG, step=4)
        def _(at):
            k = pl.ds(at, 4)
            out_ref[u, k] = (hid_ref[u, k, high] + task.total(k)).astype(BF)

        save(out_ref.at[u], out_hbm.at[u])

    staged = []

    def weight_grads(first, left, right):
        for n in range(d // 256):
            cols = slice(n * 256, (n + 1) * 256)
            slot = len(staged) % 2
            if len(staged) >= 2:
                for copy in staged[-2]:
                    copy.wait()
            tile = dot_first_t(left(0, cols), right(0)) + dot_first_t(left(1, cols), right(1))
            chunks = tile.shape[1] // 256
            rows = pl.ds(slot * 256, 256)
            pool_ref[rows, : tile.shape[1]] = tile.astype(BF)
            copies = [
                pltpu.make_async_copy(
                    pool_ref.at[rows, pl.ds(c * 256, 256)],
                    gffn_hbm.at[first + c, cols],
                    stage_sem.at[slot, c],
                )
                for c in range(chunks)
            ]
            for copy in copies:
                copy.start()
            staged.append(copies)

    slots = cot_new.shape[1]
    rows_here = edge_rows * PART
    edges = [
        remote(
            mem_hbm.at[:, pl.ds(0, REACH // PART)],
            ext_ref.at[:, pl.ds(edge_rows, REACH // PART)],
            edge_send.at[0],
            edge_recv.at[0],
            me.before(),
        ),
        remote(cot_new, cot_prev, edge_send.at[1], edge_recv.at[1], me.after()),
    ]
    seq = SeqReduce(me, comp_ref, comp_total, landed, (seq_send, seq_recv), [[0, 1, 2]])
    win = TpReduce(me, win_part, win_first, win_second, (rs_send, rs_recv), 0)

    def local_rows(at, tap, is_lead):
        slot = slots * me.column + at - jnp.where(is_lead, LEAD, 0)
        used = at < jnp.where(is_lead, LEAD, slots)
        slot_seg = lax.div(slot, CSEG)
        place = 3 * (slot - slot_seg * CSEG) + tap
        there = jnp.logical_and(used, jnp.logical_and(slot >= 0, place < SEG))
        return jnp.where(there, slot_seg * SEG + place - rows_here * me.column, -1)

    lead_rows = 32
    own_rows = 3 * SLOT_PAD
    ext_rows = rows_here + REACH
    feats = w_comp.shape[2]

    def compress_masks():
        row = lax.broadcasted_iota(jnp.int32, (own_rows, 1), 0)
        tap = lax.div(row, SLOT_PAD)
        local = local_rows(row - tap * SLOT_PAD, tap, False)
        where_at = lax.broadcasted_iota(jnp.int32, (own_rows, ext_rows), 1)
        pick_ref[...] = jnp.where(local == where_at, 1.0, 0.0).astype(BF)
        col = lax.broadcasted_iota(jnp.int32, (1, own_rows + 3 * lead_rows), 1)
        is_lead = col >= own_rows
        col = jnp.where(is_lead, col - own_rows, col)
        per = jnp.where(is_lead, lead_rows, SLOT_PAD)
        tap = jnp.where(is_lead, lax.div(col, lead_rows), lax.div(col, SLOT_PAD))
        local = local_rows(col - tap * per, tap, is_lead)
        where_at = lax.broadcasted_iota(jnp.int32, spread_ref.shape, 0)
        spread_ref[...] = jnp.where(local == where_at, 1.0, 0.0).astype(BF)
        cot_pad[...] = jnp.zeros(cot_pad.shape, BF)
        lead_pad[...] = jnp.zeros(lead_pad.shape, BF)

    def compress():
        for load in loads[:3]:
            load.wait()
        for copy in edges:
            copy.wait()
        grads = [None] * 3
        for m in range(2):
            cot_pad[m, :slots] = cot_own[m]
            lead_pad[m, :LEAD] = cot_prev[m, slots - LEAD :]
            cot, cot_lead = cot_pad[m], lead_pad[m]
            fresh = None
            taken = dot_plain(pick_ref[...], ext_ref[m].reshape(ext_rows, d)).astype(BF)
            for tap in range(3):
                span = slice(tap * SLOT_PAD, (tap + 1) * SLOT_PAD)
                lead = slice(own_rows + tap * lead_rows, own_rows + (tap + 1) * lead_rows)
                term = dot_plain(taken[span], wc_ref[tap])
                fresh = term if fresh is None else fresh + term
                term = dot_first_t(taken[span], cot)
                grads[tap] = term if grads[tap] is None else grads[tap] + term
                pool_ref[span, :d] = dot_second_t(cot, wc_ref[tap]).astype(BF)
                pool_ref[lead, :d] = dot_second_t(cot_lead, wc_ref[tap]).astype(BF)
            fresh_ref[m] = fresh[:slots]
            for n in range(2):
                cols = slice(n * d // 2, (n + 1) * d // 2)
                tile = dot_plain(spread_ref[...], pool_ref[:, cols])
                win_part[m * PER_DEV : (m + 1) * PER_DEV, :, :, :, cols] = (
                    tile.astype(BF).reshape(PER_DEV, 2, 2, PART, d // 2)
                )
        for tap in range(3):
            split_store(me, comp_ref, 0, tap * (feats // 256), grads[tap])
        save(fresh_ref, fresh_hbm)

    def win_end():
        win.end()

        @pl.loop(0, 2 * PER_DEV, step=2)
        def _(at):
            k = pl.ds(at, 2)
            win_second[k] = win.total(k).astype(BF)

        save(win_second, win_hbm)

    rs = (rs_send, rs_recv)
    outs = [TpReduce(me, parts[u], firsts[u], quarters[u], rs, 1 + u) for u in range(2)]
    backs = [
        TpReduce(me, back_parts[u], back_firsts[u], back_quarters[u], rs, 3 + u) for u in range(2)
    ]
    datts = [TpGather(me, datt_ref.at[u], (ag_send, ag_recv), u) for u in range(2)]

    for copy in edges:
        copy.start()
    send_out(kinds, 0)
    for copy in wo_copies[:2]:
        copy.start()
    vec_ref[...] = jnp.zeros(vec_ref.shape, F32)

    @pl.when(jnp.logical_not(spans[1][2]))
    def _():
        raw_ref[1] = jnp.zeros(raw_ref.shape[1:], BF)
        cot_ref[1, :, :, low] = jnp.zeros((PER_SEG, 2, PART, d), BF)

    compress_masks()
    norm_own(0)
    norm_moved(0)
    send_out(kinds, 1)
    for load in loads[3:6]:
        load.wait()
    project(0)
    attend(0, 0)
    wo_copies[0].wait()
    wo_copies[2].start()
    norm_own(1)
    attend(0, 1)
    ctx_start(0)
    compress()
    win.start()
    norm_moved(1)
    send_out([KINDS], 0)
    send_out([KINDS], 1)
    seq.launch(0)
    win.middle()
    project(1)
    save(q_ref, q_hbm)
    save(k_ref, k_hbm)
    save(v_ref, v_hbm)
    save(raw_ref.at[:, :, :, high], own_hbm)
    loads[6].wait()
    for copy in wo_copies[1:]:
        copy.wait()
    hidden_norm(0)
    attend(1, 0)
    cot_pass(0)
    attend(1, 1)
    win_end()
    save(lse_ref, lse_hbm)
    ctx_start(1)
    cot_pass(1)
    loads[7].wait()
    loads[8].wait()
    half_pass(nh_ref, 0, KINDS + 1).wait()
    passing(KINDS, 0).wait()
    ffn_up(0)
    ffn_back(0, back_parts[0])
    backs[0].start()
    hidden_norm(1)
    backs[0].middle()
    seq.turn()
    ffn_out(0, parts[0])
    outs[0].start()
    half_pass(nh_ref, 1, KINDS + 1).wait()
    passing(KINDS, 1).wait()
    ffn_up(1)
    ffn_back(1, back_parts[1])
    backs[1].start()
    hidden_back(0, backs[0])
    backs[1].middle()
    seq.turn()
    ff = wi_ref.shape[1]
    weight_grads(
        0, lambda u, cols: nh_ref[u, :, :, :, :, cols].reshape(SEG, 256), lambda u: du_ref[u]
    )
    outs[0].middle()
    ffn_out(1, parts[1])
    outs[1].start()
    datts[0].middle()
    seq.drain()
    save(comp_total, comp_hbm)
    weight_grads(
        ff // 256, lambda u, cols: cot_ref[u, :, :, :, :, cols].reshape(SEG, 256), lambda u: act_ref[u]
    )
    hidden_back(1, backs[1])
    save(vec_ref, vec_hbm)
    outs[1].middle()
    datts[0].end()
    save(datt_ref.at[0], datt_hbm.at[0])
    out_end(0, outs[0])
    datts[1].middle()
    out_end(1, outs[1])
    datts[1].end()
    save(datt_ref.at[1], datt_hbm.at[1])
    for micro in range(2):
        sent(kinds + [KINDS], micro)
    for copies in staged[-2:]:
        for copy in copies:
            copy.wait()
    for copy in saves:
        copy.wait()


def forward_call(rows, cot, memory, cot_new, w_comp, boundary, links, slopes, gains, shifts, weights):
    count = lax.axis_size("seq")
    bits = count.bit_length() - 1
    d = cot.shape[-1]
    heads = weights[0].shape[1] // HEAD
    width = heads * HEAD
    ff = weights[4].shape[1]
    slots, feats = cot_new.shape[1:]
    split = (PER_SEG, 2, 2, PART, d)
    half = (PER_SEG, 2, PART, d)
    own = (PER_SEG, PART, d)
    keys = KINDS * SEG
    owned = 2 * PER_DEV
    shard = d // count
    any_space = pl.BlockSpec(memory_space=pl.ANY)
    smem = pl.BlockSpec(memory_space=pltpu.SMEM)
    vmem = pl.BlockSpec(memory_space=pltpu.VMEM)
    shapes = [
        ((2, KINDS) + split, BF),
        ((2, KINDS) + own, BF),
        ((2, heads, SEG, HEAD), BF),
        ((2, heads, keys, HEAD), BF),
        ((2, heads, keys, HEAD), BF),
        ((2, heads, SEG, HEAD), F32),
        ((2, PER_SEG, 2, 2, PART, width), BF),
        ((2, heads, SEG, HEAD), F32),
        ((2,) + own, BF),
        ((2,) + own, F32),
        ((2,) + split, BF),
        ((2 * ff // 256, d, 256), BF),
        ((2, 8, d), F32),
        ((owned, PART, d), BF),
        ((2, slots, feats), F32),
        ((shard, 3 * feats), F32),
    ]
    dma = pltpu.SemaphoreType.DMA
    total_rows = 3 * (SLOT_PAD + 32)
    ext_rows = memory.shape[1] + REACH // PART
    scratch = [
        pltpu.VMEM((2, KINDS) + split, BF),
        pltpu.VMEM((2, KINDS) + half, BF),
        pltpu.VMEM((2,) + split, BF),
        pltpu.VMEM((2, heads, SEG, HEAD), BF),
        pltpu.VMEM((2, heads, keys, HEAD), BF),
        pltpu.VMEM((2, heads, keys, HEAD), BF),
        pltpu.VMEM((2, heads, SEG, HEAD), F32),
        pltpu.VMEM((2, PER_SEG, 2, 2, PART, width), BF),
        pltpu.VMEM((2, heads, SEG, HEAD), F32),
        pltpu.VMEM((2, PER_SEG, 2, PART, 4 * width), BF),
        pltpu.VMEM((d, 3 * width), BF),
        pltpu.VMEM((4 * width, d), BF),
        pltpu.VMEM((d, ff), BF),
        pltpu.VMEM((ff, d), BF),
        [pltpu.VMEM(split, BF) for _ in range(2)],
        [pltpu.VMEM(split, F32) for _ in range(2)],
        [pltpu.VMEM(half, BF) for _ in range(2)],
        [pltpu.VMEM(half, F32) for _ in range(2)],
        [pltpu.VMEM(own, BF) for _ in range(2)],
        [pltpu.VMEM(own, F32) for _ in range(2)],
        pltpu.VMEM((2,) + split, BF),
        pltpu.VMEM((2,) + split, BF),
        pltpu.VMEM((2, SEG, ff), BF),
        pltpu.VMEM((2, SEG, ff), BF),
        pltpu.VMEM((2,) + half, F32),
        pltpu.VMEM((2,) + own, BF),
        pltpu.VMEM((2, 8, d), F32),
        pltpu.VMEM((2, ext_rows, PART, d), BF),
        pltpu.VMEM((2, slots, feats), BF),
        pltpu.VMEM((2, slots, feats), BF),
        pltpu.VMEM((2, SLOT_PAD, feats), BF),
        pltpu.VMEM((2, 32, feats), BF),
        pltpu.VMEM((3, d, feats), BF),
        pltpu.VMEM((3 * SLOT_PAD, ext_rows * PART), BF),
        pltpu.VMEM((memory.shape[1] * PART, total_rows), BF),
        pltpu.VMEM((total_rows, max(d, ff)), BF),
        pltpu.VMEM((owned, 2, 2, PART, d), BF),
        pltpu.VMEM((owned, 2, PART, d), BF),
        pltpu.VMEM((owned, PART, d), BF),
        pltpu.VMEM((2, slots, feats), F32),
        pltpu.VMEM((3 * feats // 256,) + (2,) * bits + (shard, 256), BF),
        pltpu.VMEM((shard, 3 * feats), F32),
        [
            pltpu.VMEM((3 * feats // 256,) + (2,) * (bits - 1 - i) + (shard, 256), BF)
            for i in range(bits)
        ],
        dma((9,)),
        dma((24,)),
        dma((2, ff // 256)),
        dma((KINDS + 1, 2, PER_SEG)),
        dma((KINDS + 1, 2, PER_DEV)),
        dma((KINDS + 1, 2, PER_SEG)),
        dma((KINDS + 3, 2)),
        dma((KINDS + 3, 2)),
        dma((2, 3)),
        dma((2, 3)),
        dma((3,)),
        dma((3,)),
        dma((2,)),
        dma((2,)),
        dma((5, 2)),
        dma((5, 2)),
        dma((2, 2)),
        dma((2, 2)),
        dma((bits, 3)),
        dma((bits, 3)),
    ]
    return pl.pallas_call(
        forward_kernel,
        out_shape=[jax.ShapeDtypeStruct(shape, kind) for shape, kind in shapes],
        in_specs=[[any_space] * KINDS]
        + [any_space] * 4
        + [smem] * 3
        + [vmem] * 2
        + [any_space] * 6,
        out_specs=[any_space] * len(shapes),
        scratch_shapes=scratch,
        compiler_params=pltpu.CompilerParams(
            collective_id=1, has_side_effects=True, vmem_limit_bytes=63 << 20
        ),
    )(rows, cot, memory, cot_new, w_comp, boundary, links, slopes, gains, shifts, *weights)


FINALS = 4


def backward_kernel(
    normed_hbm,
    own_hbm,
    q_hbm,
    k_hbm,
    v_hbm,
    lse_hbm,
    ctx_hbm,
    ctxn_hbm,
    out_hbm,
    dhid_hbm,
    datt_hbm,
    gffn_hbm,
    win_hbm,
    vec_in,
    boundary,
    links,
    slopes,
    gains,
    w_query,
    w_key,
    w_value,
    w_out,
    finals,
    total_hbm,
    small_hbm,
    normed_ref,
    own_ref,
    q_ref,
    kx_ref,
    v_ref,
    lse_ref,
    ctx_ref,
    ctxn_ref,
    dhid_ref,
    datt_ref,
    wqkv_ref,
    wo_ref,
    dctx_ref,
    ds_ref,
    prob_ref,
    dq_ref,
    dqkv_ref,
    parts,
    firsts,
    seconds,
    win_ref,
    home_ref,
    owner_ref,
    grads_ref,
    total_ref,
    landed,
    vec_ref,
    aux_ref,
    small_ref,
    small_came,
    load_sem,
    save_sem,
    rs_send,
    rs_recv,
    ag_send,
    ag_recv,
    ag_here,
    move_send,
    move_recv,
    seq_send,
    seq_recv,
    small_send,
    small_recv,
):
    me = Place()
    d = normed_ref.shape[-1]
    heads = q_ref.shape[1]
    width = heads * HEAD
    late = gffn_hbm.shape[0]
    heads_wide = width // 256

    load_pairs = {
        "gffn": (gffn_hbm, grads_ref.at[pl.ds(0, late)]),
        "datt": (datt_hbm, datt_ref),
        "wo": (w_out, wo_ref),
        "v": (v_hbm, v_ref),
        "ctxn": (ctxn_hbm, ctxn_ref),
        "lse": (lse_hbm, lse_ref),
        "k": (k_hbm, kx_ref.at[:, :, :, pl.ds(0, HEAD)]),
        "q": (q_hbm, q_ref),
        "wk": (w_key, wqkv_ref.at[:, pl.ds(0, width)]),
        "wv": (w_value, wqkv_ref.at[:, pl.ds(width, width)]),
        "wq": (w_query, wqkv_ref.at[:, pl.ds(2 * width, width)]),
        "own": (own_hbm, own_ref),
        "dhid": (dhid_hbm, dhid_ref),
        "win": (win_hbm, win_ref),
        "vec": (vec_in, vec_ref.at[pl.ds(2, 2)]),
        "normed": (normed_hbm, normed_ref),
        "ctx": (ctx_hbm, ctx_ref),
    }
    loads = {
        name: pltpu.make_async_copy(src, dst, load_sem.at[i])
        for i, (name, (src, dst)) in enumerate(load_pairs.items())
    }
    for load in loads.values():
        load.start()

    def ready(*names):
        for name in names:
            loads[name].wait()

    meet(
        me,
        [me.mate(), me.across(), me.after(), me.before()]
        + [me.flipped(b) for b in range(me.bits)],
    )

    gain_0 = gains[0:1]
    vec_ref[:2] = jnp.zeros((2,) + vec_ref.shape[1:], F32)
    aux_ref[...] = jnp.zeros(aux_ref.shape, F32)
    key_at = lax.broadcasted_iota(jnp.int32, (KINDS * SEG, HEAD), 0)
    lane = lax.broadcasted_iota(jnp.int32, (KINDS * SEG, HEAD), 1)
    kind_at = lax.div(key_at, SEG)
    in_kind = key_at - SEG * kind_at
    odd = lax.rem(in_kind, 2)
    marks = jnp.where(
        lane == 0,
        in_kind - odd,
        jnp.where(lane == 1, odd, jnp.where(lane == 2, kind_at, jnp.where(lane == 3, 1, 0))),
    )
    marks = marks.astype(F32).astype(BF)
    for u in range(2):
        for h in range(heads):
            kx_ref[u, h, :, HEAD:] = marks

    rs = (rs_send, rs_recv)
    sems = (seq_send, seq_recv)
    chunks = grads_ref.shape[0]
    seq = SeqReduce(me, grads_ref, total_ref, landed, sems, [[i] for i in range(chunks)])


    def to_owner(kind, slot):
        segment, micro, there = units_of(me.column, slot)

        @pl.loop(0, PER_SEG)
        def _(chunk):
            place = PER_SEG * segment + chunk
            holder = lax.div(place, PER_DEV)
            q = lax.rem(place, PER_DEV)
            src = out_hbm.at[slot, chunk] if kind == KINDS else home_ref.at[kind, slot, chunk]
            dst = owner_ref.at[kind, micro, q]

            @pl.when(jnp.logical_and(there, holder == me.column))
            def _():
                pltpu.make_async_copy(src, dst, move_recv.at[kind, micro, q]).start()

            @pl.when(jnp.logical_and(there, holder != me.column))
            def _():
                remote(
                    src,
                    dst,
                    move_send.at[kind, slot, chunk],
                    move_recv.at[kind, micro, q],
                    me.beside(holder - me.column),
                ).start()

    def sent(kind, slot):
        segment, micro, there = units_of(me.column, slot)

        @pl.loop(0, PER_SEG)
        def _(chunk):
            holder = lax.div(PER_SEG * segment + chunk, PER_DEV)

            @pl.when(jnp.logical_and(there, holder != me.column))
            def _():
                src = home_ref.at[0, slot, chunk]
                remote(
                    src,
                    src,
                    move_send.at[kind, slot, chunk],
                    move_recv.at[kind, 0, 0],
                    me.mate(),
                ).wait_send()

    def collect(kind, micro):
        @pl.loop(0, PER_DEV)
        def _(q):
            segment = jnp.where(q < me.column, me.column - 1, me.column)
            home, slot = home_of(segment, micro)
            dst = owner_ref.at[kind, micro, q]

            @pl.when(home == me.column)
            def _():
                pltpu.make_async_copy(dst, dst, move_recv.at[kind, micro, q]).wait()

            @pl.when(home != me.column)
            def _():
                remote(
                    dst,
                    dst,
                    move_send.at[kind, 0, 0],
                    move_recv.at[kind, micro, q],
                    me.mate(),
                ).wait_recv()

    class Final:
        def __init__(self, kind, micro):
            self.own = owner_ref.at[kind, micro]
            whole = finals[kind].at[micro]
            self.mine = whole.at[:, me.high, me.low]
            self.here = pltpu.make_async_copy(self.own, self.mine, ag_here.at[kind, micro])
            self.one = remote(
                self.own,
                self.mine,
                ag_send.at[kind, micro, 0],
                ag_recv.at[kind, micro, 0],
                me.across(),
            )
            both = whole.at[:, :, me.low]
            self.two = remote(
                both, both, ag_send.at[kind, micro, 1], ag_recv.at[kind, micro, 1], me.mate()
            )

        def start(self):
            self.here.start()
            self.one.start()

        def middle(self):
            self.here.wait()
            self.one.wait()
            self.two.start()

        def end(self):
            self.two.wait()

    def context_back(u):
        datt = datt_ref[u].reshape(SEG, d)
        for h in range(heads):
            rows = slice(h * HEAD, (h + 1) * HEAD)
            dctx_ref[u, h] = dot_second_t(datt, wo_ref[rows]).astype(BF)

    segments = lax.div(me.seq, PER_SEG) * PER_DEV

    def attend_back(u, h, kind):
        scale = HEAD ** (-0.5)
        rows_at_once = 2 * QUERY_BLOCK
        keys = slice(kind * SEG, (kind + 1) * SEG)
        segment, micro, _ = units_of(me.column, u)
        segment = jnp.minimum(segment, PER_DEV - 1) + segments
        edge = boundary[micro, segment]
        linked = links[micro, segment]
        key_x = lax.broadcasted_iota(jnp.int32, (1, SEG), 1)
        bias = (key_x - SEG * kind).astype(F32) * (slopes[h] / SEG)

        @pl.loop(0, SEG // rows_at_once)
        def _(b):
            rows = pl.ds(pl.multiple_of(b * rows_at_once, rows_at_once), rows_at_once)
            scores = dot_second_t(q_ref[u, h, rows], kx_ref[u, h, keys, :HEAD]) * scale + bias
            at = b * rows_at_once + lax.broadcasted_iota(jnp.int32, (rows_at_once, 1), 0)
            if kind == 0:
                seen = jnp.logical_and(key_x <= at, jnp.logical_or(key_x >= edge, at < edge))
            else:
                seen = jnp.logical_and(at < edge, linked == 1)
            prob = jnp.exp(jnp.where(seen, scores - lse_ref[u, h, rows, :1], -1e30))
            prob_ref[rows] = prob.astype(BF)
            d_ctx = dctx_ref[u, h, rows]
            d_prob = dot_second_t(d_ctx, v_ref[u, h, keys])
            mean = jnp.sum(d_ctx.astype(F32) * ctxn_ref[u, h, rows], axis=-1, keepdims=True)
            d_scores = (prob * (d_prob - mean)).astype(BF)
            ds_ref[rows] = d_scores
            both = dot_plain(d_scores, kx_ref[u, h, keys])
            if kind < KINDS - 1:
                both += dq_ref[h, rows]
            if kind > 0:
                dq_ref[h, rows] = both
            else:
                cols = slice(2 * width + h * HEAD, 2 * width + (h + 1) * HEAD)
                dqkv_ref[u, 0, rows, cols] = (both[:, :HEAD] * scale).astype(BF)
                marked = both[:, HEAD:]
                at = b * rows_at_once + lax.broadcasted_iota(jnp.int32, marked.shape, 0)
                aux_ref[h, 0:1] += jnp.sum(marked, axis=0, keepdims=True)
                aux_ref[h, 1:2] += jnp.sum(marked * at.astype(F32), axis=0, keepdims=True)

        d_key = dot_first_t(ds_ref[...], q_ref[u, h]) * scale
        d_value = dot_first_t(prob_ref[...], dctx_ref[u, h])
        dqkv_ref[u, kind, :, h * HEAD : (h + 1) * HEAD] = d_key.astype(BF)
        dqkv_ref[u, kind, :, width + h * HEAD : width + (h + 1) * HEAD] = d_value.astype(BF)

    def project_back(u, kind, part):
        depth = (3 if kind == 0 else 2) * width

        @pl.loop(0, d // 256)
        def _(n):
            cols = pl.ds(pl.multiple_of(n * 256, 256), 256)
            tile = dot_second_t(dqkv_ref[u, kind, :, :depth], wqkv_ref[cols, :depth])
            part[:, :, :, :, cols] = tile.astype(BF).reshape(PER_SEG, 2, 2, PART, 256)

    def norm_end(u, kind, task):
        task.end()

        @pl.loop(0, PER_SEG, step=4)
        def _(at):
            k = pl.ds(at, 4)
            scaled, inverse = center_of(own_ref[u, kind, k].astype(F32))
            grad = task.total(k)
            vec_ref[0] += eights(grad * scaled)
            vec_ref[1] += eights(grad)
            result = norm_back(grad, scaled, inverse, gain_0)
            if kind == 0:
                result += dhid_ref[u, k]
            home_ref[kind, u, k] = result.astype(BF)

    def add_window(micro):
        @pl.loop(0, PER_DEV)
        def _(q):
            added = owner_ref[1, micro, q].astype(F32) + win_ref[micro * PER_DEV + q].astype(F32)
            owner_ref[1, micro, q] = added.astype(BF)

    def late_kv():
        for n in range(d // 256):
            cols = slice(n * 256, (n + 1) * 256)
            kv = None
            for u in range(2):
                for kind in range(KINDS):
                    left = normed_ref[u, kind, :, :, :, :, cols].reshape(SEG, 256)
                    term = dot_first_t(left, dqkv_ref[u, kind, :, : 2 * width])
                    kv = term if kv is None else kv + term
            split_store(me, grads_ref, n * 256, late + heads_wide, kv)

    def late_query():
        for n in range(d // 256):
            cols = slice(n * 256, (n + 1) * 256)
            query = None
            for u in range(2):
                left = normed_ref[u, 0, :, :, :, :, cols].reshape(SEG, 256)
                term = dot_first_t(left, dqkv_ref[u, 0, :, 2 * width :])
                query = term if query is None else query + term
            split_store(me, grads_ref, n * 256, late + 3 * heads_wide, query)

    def out_grad():
        for n in range(d // 256):
            cols = slice(n * 256, (n + 1) * 256)
            out = None
            for u in range(2):
                left = datt_ref[u, :, :, :, :, cols].reshape(SEG, 256)
                term = dot_first_t(left, ctx_ref[u].reshape(SEG, width))
                out = term if out is None else out + term
            split_store(me, grads_ref, n * 256, late, out)

    friends = [me.mate(), me.across()] + [me.flipped(b) for b in range(me.bits)]

    def small_copy(i):
        return remote(
            small_ref, small_came.at[i], small_send.at[i], small_recv.at[i], friends[i]
        )

    def small_start():
        lane = lax.broadcasted_iota(jnp.int32, (1, HEAD), 1)
        plain = jnp.where(lane < 2, 1.0, jnp.where(lane == 2, -float(SEG), 0.0))
        placed = jnp.where(lane == 3, 1.0, 0.0)
        small_ref[...] = jnp.zeros(small_ref.shape, F32)
        for i, at in enumerate((0, 2, 1, 3)):
            small_ref[i : i + 1] = jnp.sum(vec_ref[at], axis=0, keepdims=True)
        row = jnp.zeros((1, HEAD), F32)
        for h in range(heads):
            marked = aux_ref[h, 0:1] * plain - aux_ref[h, 1:2] * placed
            total = jnp.sum(marked, axis=-1, keepdims=True) / SEG
            row += jnp.where(lane == me.tp * heads + h, total, 0.0)
        small_ref[4:5, :HEAD] = row
        small_copy(0).start()

    def small_step(i):
        small_copy(i).wait()
        small_ref[...] += small_came[i]
        if i + 1 < len(friends):
            small_copy(i + 1).start()

    results = {}

    def final_start(kind, micro):
        collect(kind, micro)
        if kind == 1:
            add_window(micro)
        results[kind, micro] = Final(kind, micro)
        results[kind, micro].start()

    tasks = {
        (u, kind): TpReduce(
            me, parts[kind], firsts[u * KINDS + kind], seconds[u * KINDS + kind], rs, u * KINDS + kind
        )
        for u in range(2)
        for kind in range(KINDS)
    }

    def attend_kind(u, kind):
        for h in range(heads):
            attend_back(u, h, kind)

    def send_kind(u, kind):
        project_back(u, kind, parts[kind])
        tasks[u, kind].start()

    def end_kind(u, kind):
        norm_end(u, kind, tasks[u, kind])
        to_owner(kind, u)

    to_owner(KINDS, 0)
    to_owner(KINDS, 1)
    ready("gffn")
    for group in range(3):
        seq.launch(group)
    ready("datt", "wo")
    context_back(0)
    ready("v", "ctxn", "lse", "k", "q")
    attend_kind(0, 2)
    final_start(KINDS, 0)
    final_start(KINDS, 1)
    ready("wk", "wv", "wq")
    send_kind(0, 2)
    seq.turn()
    seq.launch(3)
    attend_kind(0, 1)
    tasks[0, 2].middle()
    send_kind(0, 1)
    seq.turn()
    seq.launch(4)
    attend_kind(0, 0)
    tasks[0, 1].middle()
    send_kind(0, 0)
    seq.turn()
    seq.launch(5)
    context_back(1)
    ready("ctx")
    out_grad()
    tasks[0, 0].middle()
    ready("own", "dhid", "win", "vec")
    attend_kind(1, 2)
    end_kind(0, 2)
    send_kind(1, 2)
    seq.turn()
    seq.launch(6)
    results[KINDS, 0].middle()
    results[KINDS, 1].middle()
    attend_kind(1, 1)
    end_kind(0, 1)
    tasks[1, 2].middle()
    send_kind(1, 1)
    seq.turn()
    seq.launch(7)
    attend_kind(1, 0)
    end_kind(0, 0)
    tasks[1, 1].middle()
    send_kind(1, 0)
    seq.turn()
    seq.launch(8)
    final_start(2, 0)
    ready("normed")
    late_kv()
    seq.launch(9)
    seq.launch(10)
    tasks[1, 0].middle()
    final_start(1, 0)
    late_query()
    seq.launch(11)
    seq.turn()
    final_start(0, 0)
    end_kind(1, 2)
    seq.turn()
    end_kind(1, 1)
    final_start(2, 1)
    seq.turn()
    end_kind(1, 0)
    small_start()
    results[2, 0].middle()
    small_step(0)
    final_start(1, 1)
    seq.turn()
    results[1, 0].middle()
    final_start(0, 1)
    seq.turn()
    results[0, 0].middle()
    small_step(1)
    seq.turn()
    small_step(2)
    results[2, 1].middle()
    seq.turn()
    for i in range(3, len(friends)):
        small_step(i)
    results[1, 1].middle()
    seq.drain()
    results[0, 1].middle()
    saves = [
        pltpu.make_async_copy(total_ref, total_hbm, save_sem.at[0]),
        pltpu.make_async_copy(small_ref, small_hbm, save_sem.at[1]),
    ]
    for save in saves:
        save.start()
    for kind in range(FINALS):
        for at in range(2):
            results[kind, at].end()
            sent(kind, at)
    for save in saves:
        save.wait()


def backward_call(saved, boundary, links, slopes, gains, weights):
    normed, own, q, k, v, lse, ctx, ctxn, out, dhid, datt, gffn, vec, win = saved
    count = lax.axis_size("seq")
    bits = count.bit_length() - 1
    d = normed.shape[-1]
    heads = q.shape[1]
    keys = KINDS * SEG
    width = heads * HEAD
    chunks = gffn.shape[0] + 4 * width // 256
    columns = 256 * chunks
    view = (2,) * bits + (d // count, 256)
    split = (PER_SEG, 2, 2, PART, d)
    any_space = pl.BlockSpec(memory_space=pl.ANY)
    vmem = pl.BlockSpec(memory_space=pltpu.VMEM)
    smem = pl.BlockSpec(memory_space=pltpu.SMEM)
    dma = pltpu.SemaphoreType.DMA
    final = jax.ShapeDtypeStruct((2, PER_DEV, 2, 2, PART, d), BF)
    scratch = [
        pltpu.VMEM(normed.shape, BF),
        pltpu.VMEM(own.shape, BF),
        pltpu.VMEM(q.shape, BF),
        pltpu.VMEM((2, heads, keys, 2 * HEAD), BF),
        pltpu.VMEM(v.shape, BF),
        pltpu.VMEM(lse.shape, F32),
        pltpu.VMEM(ctx.shape, BF),
        pltpu.VMEM(ctxn.shape, F32),
        pltpu.VMEM(dhid.shape, F32),
        pltpu.VMEM(datt.shape, BF),
        pltpu.VMEM((d, 3 * width), BF),
        pltpu.VMEM((width, d), BF),
        pltpu.VMEM((2, heads, SEG, HEAD), BF),
        pltpu.VMEM((SEG, SEG), BF),
        pltpu.VMEM((SEG, SEG), BF),
        pltpu.VMEM((heads, SEG, 2 * HEAD), F32),
        pltpu.VMEM((2, KINDS, SEG, 3 * width), BF),
        [pltpu.VMEM(split, BF) for _ in range(KINDS)],
        [pltpu.VMEM((PER_SEG, 2, PART, d), BF) for _ in range(2 * KINDS)],
        [pltpu.VMEM((PER_SEG, PART, d), BF) for _ in range(2 * KINDS)],
        pltpu.VMEM(win.shape, BF),
        pltpu.VMEM((KINDS, 2, PER_SEG, PART, d), BF),
        pltpu.VMEM((FINALS, 2, PER_DEV, PART, d), BF),
        pltpu.VMEM((chunks,) + view, BF),
        pltpu.VMEM((d // count, columns), F32),
        [pltpu.VMEM((chunks,) + view[i + 1 :], BF) for i in range(bits)],
        pltpu.VMEM((4, 8, d), F32),
        pltpu.VMEM((heads, 8, HEAD), F32),
        pltpu.VMEM((8, d), F32),
        pltpu.VMEM((bits + 2, 8, d), F32),
        dma((17,)),
        dma((2,)),
        dma((2 * KINDS, 2)),
        dma((2 * KINDS, 2)),
        dma((FINALS, 2, 2)),
        dma((FINALS, 2, 2)),
        dma((FINALS, 2)),
        dma((FINALS, 2, PER_SEG)),
        dma((FINALS, 2, PER_DEV)),
        dma((bits, chunks)),
        dma((bits, chunks)),
        dma((bits + 2,)),
        dma((bits + 2,)),
    ]
    return pl.pallas_call(
        backward_kernel,
        out_shape=[
            [final] * FINALS,
            jax.ShapeDtypeStruct((d // count, columns), F32),
            jax.ShapeDtypeStruct((8, d), F32),
        ],
        in_specs=[any_space] * 14 + [smem] * 3 + [vmem] + [any_space] * 4,
        out_specs=[[any_space] * FINALS] + [any_space] * 2,
        scratch_shapes=scratch,
        compiler_params=pltpu.CompilerParams(
            collective_id=2, has_side_effects=True, vmem_limit_bytes=63 << 20
        ),
    )(
        normed,
        own,
        q,
        k,
        v,
        lse,
        ctx,
        ctxn,
        out,
        dhid,
        datt,
        gffn.reshape((gffn.shape[0],) + view),
        win,
        vec,
        boundary,
        links,
        slopes,
        gains,
        *weights,
    )


def per_device(
    inputs,
    memory,
    compressed,
    boundary,
    links,
    gains,
    shifts,
    slopes,
    w_query,
    w_key,
    w_value,
    w_out,
    w_in,
    w_down,
    w_comp,
    cot_out,
    cot_new,
):
    d = inputs.shape[-1]
    rows = inputs.shape[1]
    heads = slopes.shape[0]
    width = heads * HEAD
    ff = w_in.shape[1]
    feats = w_comp.shape[2]
    count = lax.axis_size("seq")
    seq = lax.axis_index("seq")
    tp = lax.axis_index("tp")

    def chunked(array):
        return array.reshape(2, PER_DEV, 2, 2, PART, d)

    *saved, fresh, comp = forward_call(
        [chunked(inputs), chunked(memory), chunked(compressed)],
        chunked(cot_out),
        memory.reshape(2, rows // PART, PART, d),
        cot_new,
        w_comp,
        boundary,
        links,
        slopes,
        gains,
        shifts,
        (w_query, w_key, w_value, w_out, w_in, w_down),
    )
    finals, total, small = backward_call(
        saved, boundary, links, slopes, gains, (w_query, w_key, w_value, w_out)
    )
    vectors = lax.dynamic_slice(small, (0, seq * (d // count)), (4, d // count))
    grad_slopes = lax.dynamic_slice(small, (4, tp * heads), (1, heads))[0]

    def whole(array):
        return array.reshape(2, rows, d)

    pieces, at = [], 0
    for cut in [ff, ff] + [width] * 4:
        pieces.append(total[:, at : at + cut])
        at += cut
    g_in, g_down, g_out, g_key, g_value, g_query = pieces
    return (
        whole(finals[3]),
        whole(finals[0]).astype(F32),
        whole(finals[1]).astype(F32),
        whole(finals[2]).astype(F32),
        fresh,
        vectors[:2],
        vectors[2:],
        grad_slopes,
        g_query,
        g_key,
        g_value,
        g_out.T,
        g_in,
        g_down.T,
        jnp.stack([comp[:, i * feats : (i + 1) * feats] for i in range(3)]),
    )


def solution(mesh):
    in_specs = (
        P(None, "seq", None),
        P(None, "seq", None),
        P(None, "seq", None),
        P(),
        P(),
        P(),
        P(),
        P("tp"),
        P(None, "tp"),
        P(None, "tp"),
        P(None, "tp"),
        P("tp", None),
        P(None, "tp"),
        P("tp", None),
        P(None, None, "tp"),
        P(None, "seq", None),
        P(None, "seq", "tp"),
    )
    out_specs = (
        P(None, "seq", None),
        P(None, "seq", None),
        P(None, "seq", None),
        P(None, "seq", None),
        P(None, "seq", "tp"),
        P(None, "seq"),
        P(None, "seq"),
        P("tp"),
        P("seq", "tp"),
        P("seq", "tp"),
        P("seq", "tp"),
        P("tp", "seq"),
        P("seq", "tp"),
        P("tp", "seq"),
        P(None, "seq", "tp"),
    )
    return jax.shard_map(
        per_device, mesh=mesh, in_specs=in_specs, out_specs=out_specs, check_vma=False
    )
```

```python
import functools
import math

import jax
import jax.numpy as jnp
from jax import lax
from jax.experimental import pallas as pl
from jax.experimental.pallas import tpu as pltpu
from jax.sharding import PartitionSpec as P

HEAD = 128
SEG = 512
CSEG = 176
REACH = 32
LEAD = 26
SLOT_PAD = 160
CHUNK = 64
PART = 16
KINDS = 3
NORM_EPS = 1e-05
MESH = pl.DeviceIdType.MESH
BF = jnp.bfloat16
F32 = jnp.float32
GELU_IN = math.sqrt(2.0 / math.pi)
PER_SEG = SEG // CHUNK
PER_DEV = PER_SEG - 1
QUERY_BLOCK = 128


def dot_plain(a, b):
    return jnp.dot(a, b, preferred_element_type=F32)


def dot_first_t(a, b):
    return lax.dot_general(a, b, (((0,), (0,)), ((), ())), preferred_element_type=F32)


def dot_second_t(a, b):
    return lax.dot_general(a, b, (((1,), (1,)), ((), ())), preferred_element_type=F32)


def home_of(segment, micro):
    middle = PER_DEV // 2
    home = jnp.where(
        segment < middle, segment, jnp.where(segment == middle, middle + micro, segment + 1)
    )
    slot = jnp.where(segment == middle, 0, micro)
    return home, slot


def units_of(place, slot):
    middle = PER_DEV // 2
    segment = jnp.where(place <= middle, place, place - 1)
    is_middle = segment == middle
    micro = jnp.where(is_middle, place - middle, slot)
    return segment, micro, jnp.logical_or(jnp.logical_not(is_middle), slot == 0)


class Place:
    def __init__(self):
        self.seq = lax.axis_index("seq")
        self.tp = lax.axis_index("tp")
        self.column = lax.rem(self.seq, PER_SEG)
        self.low = lax.rem(self.tp, 2)
        self.high = lax.div(self.tp, 2)
        self.count = lax.axis_size("seq")
        self.bits = self.count.bit_length() - 1
        self.bit = [lax.rem(lax.div(self.seq, 1 << b), 2) for b in range(self.bits)]

    def flipped(self, bit):
        return self.beside((1 - 2 * self.bit[bit]) * (1 << bit))

    def after(self):
        return (lax.rem(self.seq + 1, self.count), self.tp)

    def before(self):
        return (lax.rem(self.seq + self.count - 1, self.count), self.tp)

    def mate(self):
        return (self.seq, self.tp + 1 - 2 * self.low)

    def across(self):
        return (self.seq, self.tp + 2 - 4 * self.high)

    def corner(self):
        return (self.seq, self.tp + 3 - 2 * self.low - 4 * self.high)

    def beside(self, by):
        return (self.seq + by, self.tp)


def remote(src, dst, send, recv, device):
    return pltpu.make_async_remote_copy(
        src_ref=src,
        dst_ref=dst,
        send_sem=send,
        recv_sem=recv,
        device_id=device,
        device_id_type=MESH,
    )


class TpReduce:
    def __init__(self, me, part, first, second, sems, index):
        self.me, self.part, self.first, self.second = me, part, first, second
        send, recv = sems
        self.one = remote(
            part.at[:, :, 1 - me.low], first, send.at[index, 0], recv.at[index, 0], me.mate()
        )
        self.two = remote(
            part.at[:, 1 - me.high, me.low],
            second,
            send.at[index, 1],
            recv.at[index, 1],
            me.across(),
        )

    def start(self):
        self.one.start()

    def middle(self):
        self.one.wait()
        part, first, low = self.part, self.first, self.me.low

        @pl.loop(0, part.shape[0], step=2)
        def _(at):
            k = pl.ds(at, 2)
            added = part[k, :, low].astype(F32) + first[k].astype(F32)
            part[k, :, low] = added.astype(part.dtype)

        self.two.start()

    def end(self):
        self.two.wait()

    def total(self, k):
        me = self.me
        return self.part[k, me.high, me.low].astype(F32) + self.second[k].astype(F32)


class TpGather:
    def __init__(self, me, whole, sems, index):
        send, recv = sems
        mine = whole.at[:, me.high, me.low]
        self.one = remote(mine, mine, send.at[index, 0], recv.at[index, 0], me.across())
        both = whole.at[:, :, me.low]
        self.two = remote(both, both, send.at[index, 1], recv.at[index, 1], me.mate())

    def start(self):
        self.one.start()

    def middle(self):
        self.one.wait()
        self.two.start()

    def end(self):
        self.two.wait()


def meet(me, friends):
    barrier = pltpu.get_barrier_semaphore()
    for friend in friends:
        pl.semaphore_signal(barrier, inc=1, device_id=friend, device_id_type=MESH)
    pl.semaphore_wait(barrier, len(friends))


def center_of(rows):
    center = rows - jnp.mean(rows, axis=-1, keepdims=True)
    inverse = lax.rsqrt(jnp.mean(center * center, axis=-1, keepdims=True) + NORM_EPS)
    return center * inverse, inverse


def norm_back(grad, scaled, inverse, gain):
    weighted = grad * gain
    first = jnp.mean(weighted, axis=-1, keepdims=True)
    second = jnp.mean(weighted * scaled, axis=-1, keepdims=True)
    return inverse * (weighted - first - scaled * second)


def eights(rows):
    d = rows.shape[-1]
    return jnp.sum(rows.reshape(-1, PART // 2, d), axis=0)


class SeqReduce:
    width = 256

    def __init__(self, me, grads, total, landed, sems, groups):
        self.me, self.grads, self.total, self.landed = me, grads, total, landed
        self.send, self.recv = sems
        self.groups = groups
        self.turn_at = 0

    def cols(self, chunk):
        return pl.ds(chunk * self.width, self.width)

    def plan(self, chunk):
        first = 1 if chunk % 5 == 4 else 0
        return [(i + first) % self.me.bits for i in range(self.me.bits)]

    def index(self, chunk, step, own):
        plan = self.plan(chunk)
        out = [chunk]
        for b in reversed(range(self.me.bits)):
            if b in plan[:step] or (b == plan[step] and own):
                out.append(self.me.bit[b])
            elif b == plan[step]:
                out.append(1 - self.me.bit[b])
            else:
                out.append(slice(None))
        return tuple(out)

    def copy(self, chunk, step):
        return remote(
            self.grads.at[self.index(chunk, step, False)],
            self.landed[step].at[chunk],
            self.send.at[step, chunk],
            self.recv.at[step, chunk],
            self.me.flipped(self.plan(chunk)[step]),
        )

    def finish(self, chunk, step):
        self.copy(chunk, step).wait()
        here = self.index(chunk, step, True)
        added = self.grads[here].astype(F32) + self.landed[step][chunk].astype(F32)
        if step == self.me.bits - 1:
            self.total[:, self.cols(chunk)] = added
        else:
            self.grads[here] = added.astype(BF)
            self.copy(chunk, step + 1).start()

    def launch(self, group):
        for chunk in self.groups[group]:
            self.copy(chunk, 0).start()

    def turn(self):
        at = self.turn_at
        self.turn_at += 1
        for step in reversed(range(self.me.bits)):
            group = at - step
            if 0 <= group < len(self.groups):
                for chunk in self.groups[group]:
                    self.finish(chunk, step)

    def drain(self):
        while self.turn_at < len(self.groups) + self.me.bits - 1:
            self.turn()


def split_store(me, grads, rows_from, first, tile):
    per, wide = grads.shape[-2:]
    n = tile.shape[0] // per
    for c in range(tile.shape[1] // wide):
        parts = tile[:, c * wide : (c + 1) * wide].astype(BF).reshape((n, per, wide))
        for i in range(n):
            at = rows_from // per + i
            grads[(first + c,) + tuple((at >> b) & 1 for b in reversed(range(me.bits)))] = parts[i]


def forward_kernel(
    rows_hbm,
    cot_hbm,
    mem_hbm,
    cot_new,
    w_comp,
    boundary,
    links,
    slopes,
    gains,
    shifts,
    w_query,
    w_key,
    w_value,
    w_out,
    w_in,
    w_down,
    normed_hbm,
    own_hbm,
    q_hbm,
    k_hbm,
    v_hbm,
    lse_hbm,
    ctx_hbm,
    ctxn_hbm,
    outp_hbm,
    hid_hbm,
    dhid_hbm,
    datt_hbm,
    gffn_hbm,
    vec_hbm,
    win_hbm,
    fresh_hbm,
    comp_hbm,
    x_ref,
    raw_ref,
    cot_ref,
    q_ref,
    k_ref,
    v_ref,
    lse_ref,
    ctx_ref,
    ctxn_ref,
    all_ref,
    wqkv_ref,
    wo_ref,
    wi_ref,
    wd_ref,
    parts,
    back_parts,
    back_firsts,
    back_quarters,
    nh_ref,
    datt_ref,
    act_ref,
    du_ref,
    hid_ref,
    vec_ref,
    ext_ref,
    cot_own,
    cot_prev,
    cot_pad,
    lead_pad,
    wc_ref,
    pick_ref,
    spread_ref,
    pool_ref,
    win_part,
    win_first,
    win_second,
    fresh_ref,
    comp_ref,
    comp_total,
    landed,
    load_sem,
    save_sem,
    stage_sem,
    place_sem,
    move_send,
    move_recv,
    pass_send,
    pass_recv,
    ctx_send,
    ctx_recv,
    wo_send,
    wo_recv,
    edge_send,
    edge_recv,
    rs_send,
    rs_recv,
    ag_send,
    ag_recv,
    seq_send,
    seq_recv,
):
    me = Place()
    d = x_ref.shape[-1]
    heads = q_ref.shape[1]
    width = heads * HEAD
    low, high = me.low, me.high
    kinds = list(range(KINDS))
    edge_rows = mem_hbm.shape[1]

    load_pairs = [
        (mem_hbm, ext_ref.at[:, pl.ds(0, edge_rows)]),
        (cot_new, cot_own),
        (w_comp, wc_ref),
        (w_key, wqkv_ref.at[:, pl.ds(0, width)]),
        (w_value, wqkv_ref.at[:, pl.ds(width, width)]),
        (w_query, wqkv_ref.at[:, pl.ds(2 * width, width)]),
        (w_out, wo_ref.at[pl.ds(pl.multiple_of(me.tp * width, width), width)]),
        (w_in, wi_ref),
        (w_down, wd_ref),
    ]
    loads = [
        pltpu.make_async_copy(src, dst, load_sem.at[i]) for i, (src, dst) in enumerate(load_pairs)
    ]
    for load in loads:
        load.start()

    meet(
        me,
        [me.mate(), me.across(), me.corner(), me.after(), me.before()]
        + [me.flipped(b) for b in range(me.bits)],
    )

    sources = [rows_hbm[0], rows_hbm[1], rows_hbm[2], cot_hbm]

    def landing(kind, slot, chunk):
        if kind == KINDS:
            return cot_ref.at[slot, chunk, :, low]
        return raw_ref.at[slot, kind, chunk]

    def route(micro, q):
        segment = jnp.where(q < me.column, me.column - 1, me.column)
        home, slot = home_of(segment, micro)
        return home, slot, PER_DEV * me.column + q - PER_SEG * segment

    def send_out(kinds, wanted):
        @pl.loop(0, 2 * PER_DEV)
        def _(at):
            micro, q = lax.div(at, PER_DEV), lax.rem(at, PER_DEV)
            home, slot, chunk = route(micro, q)
            here = home == me.column
            for kind in kinds:
                src = sources[kind].at[micro, q, :, low]
                dst = landing(kind, slot, chunk)

                @pl.when(jnp.logical_and(slot == wanted, here))
                def _():
                    pltpu.make_async_copy(src, dst, place_sem.at[kind, slot, chunk]).start()

                @pl.when(jnp.logical_and(slot == wanted, jnp.logical_not(here)))
                def _():
                    remote(
                        src,
                        dst,
                        move_send.at[kind, micro, q],
                        move_recv.at[kind, slot, chunk],
                        me.beside(home - me.column),
                    ).start()

    def sent(kinds, micro):
        @pl.loop(0, PER_DEV)
        def _(q):
            home, slot, chunk = route(micro, q)
            for kind in kinds:

                @pl.when(home != me.column)
                def _():
                    remote(
                        sources[kind].at[micro, q, :, low],
                        landing(kind, slot, chunk),
                        move_send.at[kind, micro, q],
                        move_recv.at[kind, slot, chunk],
                        me.beside(home - me.column),
                    ).wait_send()

    spans = []
    for slot in range(2):
        segment, _, there = units_of(me.column, slot)
        first = jnp.maximum(PER_DEV * me.column - PER_SEG * segment, 0)
        last = jnp.minimum(PER_DEV * me.column + PER_DEV - PER_SEG * segment, PER_SEG)
        spans.append((jnp.where(there, first, 0), jnp.where(there, last, PER_SEG), there))

    def wait_own(kind, slot, chunk):
        dst = landing(kind, slot, chunk)
        pltpu.make_async_copy(dst, dst, place_sem.at[kind, slot, chunk]).wait()

    def wait_moved(kind, slot, chunk):
        dst = landing(kind, slot, chunk)
        remote(
            dst, dst, move_send.at[kind, 0, 0], move_recv.at[kind, slot, chunk], me.mate()
        ).wait_recv()

    def over_own(kinds, slot, body):
        first, last, there = spans[slot]

        @pl.loop(first, last)
        def _(chunk):
            @pl.when(there)
            def _():
                for kind in kinds:
                    wait_own(kind, slot, chunk)

            body(chunk)

    def over_moved(kinds, slot, body):
        first, last, _ = spans[slot]

        def step(chunk):
            for kind in kinds:
                wait_moved(kind, slot, chunk)
            body(chunk)

        pl.loop(0, first)(step)
        pl.loop(last, PER_SEG)(step)

    gain_0, shift_0 = gains[0:1], shifts[0:1]
    gain_1, shift_1 = gains[1:2], shifts[1:2]

    def passing(kind, slot):
        here = cot_ref.at[slot, :, :, low] if kind == KINDS else x_ref.at[slot, kind, :, :, low]
        return remote(
            here, here, pass_send.at[kind, slot], pass_recv.at[kind, slot], me.mate()
        )

    def norm_chunk(u):
        def body(k):
            for kind in range(KINDS):
                raw = raw_ref[u, kind, k].reshape(2 * PART, d).astype(F32)
                scaled, _ = center_of(raw)
                normed = (scaled * gain_0 + shift_0).astype(BF)
                x_ref[u, kind, k, :, low] = normed.reshape(2, PART, d)

        return body

    def norm_own(u):
        over_own(kinds, u, norm_chunk(u))

    def norm_moved(u):
        over_moved(kinds, u, norm_chunk(u))
        for kind in kinds:
            passing(kind, u).start()

    def cot_pass(u):
        over_own([KINDS], u, lambda k: None)
        over_moved([KINDS], u, lambda k: None)
        passing(KINDS, u).start()

    saves = []

    def save(src, dst):
        copy = pltpu.make_async_copy(src, dst, save_sem.at[len(saves)])
        copy.start()
        saves.append(copy)

    def project(u):
        for kind in range(KINDS):
            passing(kind, u).wait()
            normed = x_ref[u, kind].reshape(SEG, d)
            span = pl.ds(kind * SEG, SEG)
            keys = dot_plain(normed, wqkv_ref[:, :width]).astype(BF)
            values = dot_plain(normed, wqkv_ref[:, width : 2 * width]).astype(BF)
            for h in range(heads):
                cols = slice(h * HEAD, (h + 1) * HEAD)
                k_ref[u, h, span] = keys[:, cols]
                v_ref[u, h, span] = values[:, cols]
            if kind == 0:
                queries = dot_plain(normed, wqkv_ref[:, 2 * width :]).astype(BF)
                for h in range(heads):
                    q_ref[u, h] = queries[:, h * HEAD : (h + 1) * HEAD]
        save(x_ref.at[u], normed_hbm.at[u])

    segments = lax.div(me.seq, PER_SEG) * PER_DEV

    def attend(u, h):
        scale = HEAD ** (-0.5)
        slope = slopes[h]
        segment, micro, _ = units_of(me.column, u)
        segment = jnp.minimum(segment, PER_DEV - 1) + segments
        edge = boundary[micro, segment]
        linked = links[micro, segment]
        key_at = lax.broadcasted_iota(jnp.int32, (1, KINDS * SEG), 1)
        kind_at = lax.div(key_at, SEG)
        bias = (key_at - 2 * SEG * kind_at).astype(F32) * (slope / SEG)
        key_x = lax.broadcasted_iota(jnp.int32, (QUERY_BLOCK, SEG), 1)
        per = QUERY_BLOCK // CHUNK

        @pl.loop(0, SEG // QUERY_BLOCK)
        def _(b):
            rows = pl.ds(pl.multiple_of(b * QUERY_BLOCK, QUERY_BLOCK), QUERY_BLOCK)
            raw = dot_second_t(q_ref[u, h, rows], k_ref[u, h]) * scale + bias
            at = b * QUERY_BLOCK + lax.broadcasted_iota(jnp.int32, (QUERY_BLOCK, SEG), 0)
            seen = jnp.logical_and(key_x <= at, jnp.logical_or(key_x >= edge, at < edge))
            near = jnp.where(seen, raw[:, :SEG], -1e30)
            open_row = jnp.logical_and(at[:, :1] < edge, linked == 1)
            far = jnp.where(open_row, raw[:, SEG:], -1e30)
            top = jnp.maximum(
                jnp.max(near, axis=-1, keepdims=True), jnp.max(far, axis=-1, keepdims=True)
            )
            near = jnp.exp(near - top)
            far = jnp.exp(far - top)
            whole = jnp.sum(near, axis=-1, keepdims=True) + jnp.sum(far, axis=-1, keepdims=True)
            lse_ref[u, h, rows] = jnp.broadcast_to(top + jnp.log(whole), (QUERY_BLOCK, HEAD))
            share = 1.0 / whole
            near = near * share
            far = far * share
            near_low = near.astype(BF)
            far_low = far.astype(BF)
            value_x, value_far = v_ref[u, h, :SEG], v_ref[u, h, SEG:]
            context = dot_plain(near_low, value_x) + dot_plain(far_low, value_far)
            near_rest = (near - near_low.astype(F32)).astype(BF)
            far_rest = (far - far_low.astype(F32)).astype(BF)
            rest = dot_plain(near_rest, value_x) + dot_plain(far_rest, value_far)
            ctxn_ref[u, h, rows] = context + rest
            ctx_ref[u, pl.ds(b * per, per), :, :, :, h * HEAD : (h + 1) * HEAD] = (
                context.astype(BF).reshape(per, 2, 2, PART, HEAD)
            )

    def my_columns(tp):
        return pl.ds(pl.multiple_of(tp * width, width), width)

    def ctx_copies(u):
        dst = all_ref.at[u, :, :, :, my_columns(me.tp)]
        same, other = ctx_ref.at[u, :, :, low], ctx_ref.at[u, :, :, 1 - low]
        return [
            remote(src, dst, ctx_send.at[u, i], ctx_recv.at[u, i], device)
            for i, (src, device) in enumerate(
                [(same, me.across()), (other, me.corner()), (other, me.mate())]
            )
        ]

    def ctx_start(u):
        for copy in ctx_copies(u):
            copy.start()
        all_ref[u, :, :, :, my_columns(me.tp)] = ctx_ref[u, :, :, low]
        save(ctx_ref.at[u], ctx_hbm.at[u])
        save(ctxn_ref.at[u], ctxn_hbm.at[u])

    def wo_rows(tp):
        return wo_ref.at[pl.ds(pl.multiple_of(tp * width, width), width)]

    across_tp = me.tp + 2 - 4 * high
    mate_tp = me.tp + 1 - 2 * low
    wo_copies = [
        remote(w_out, wo_rows(me.tp), wo_send.at[0], wo_recv.at[0], me.across()),
        remote(w_out, wo_rows(me.tp), wo_send.at[1], wo_recv.at[1], me.mate()),
        remote(
            wo_rows(across_tp), wo_rows(across_tp), wo_send.at[2], wo_recv.at[2], me.mate()
        ),
    ]

    def half_pass(ref, u, kind):
        here = ref.at[u, :, :, low]
        return remote(here, here, pass_send.at[kind, u], pass_recv.at[kind, u], me.mate())

    def hidden_norm(u):
        for copy in ctx_copies(u):
            copy.wait()

        @pl.loop(0, 2)
        def _(r):
            some = pl.ds(r * (PER_SEG // 2), PER_SEG // 2)
            rows = SEG // 4
            hidden = dot_plain(all_ref[u, some].reshape(rows, 4 * width), wo_ref[...])
            hidden += raw_ref[u, 0, some].reshape(rows, d).astype(F32)
            hid_ref[u, some] = hidden.reshape(PER_SEG // 2, 2, PART, d)
            scaled, _ = center_of(hidden)
            normed = (scaled * gain_1 + shift_1).astype(BF)
            nh_ref[u, some, :, low] = normed.reshape(PER_SEG // 2, 2, PART, d)

        half_pass(nh_ref, u, KINDS + 1).start()
        save(hid_ref.at[u, :, high], hid_hbm.at[u])

    def store_part(part, cols, tile):
        part[:, :, :, :, cols] = tile.astype(part.dtype).reshape(
            PER_SEG, 2, 2, PART, tile.shape[1]
        )

    def ffn_up(u):
        ff = wi_ref.shape[1]

        @pl.loop(0, ff // 256)
        def _(n):
            cols = pl.ds(pl.multiple_of(n * 256, 256), 256)
            for r in range(2):
                chunks = slice(r * PER_SEG // 2, (r + 1) * PER_SEG // 2)
                rows = slice(r * SEG // 2, (r + 1) * SEG // 2)
                upper = dot_plain(nh_ref[u, chunks].reshape(SEG // 2, d), wi_ref[:, cols])
                d_act = dot_second_t(cot_ref[u, chunks].reshape(SEG // 2, d), wd_ref[cols])
                square = upper * upper
                inner = GELU_IN * upper * (1.0 + 0.044715 * square)
                bend = jnp.tanh(inner)
                grown = 0.5 * (1.0 + bend)
                act_ref[u, rows, cols] = (upper * grown).astype(BF)
                slope = grown + 0.5 * upper * (1.0 - bend * bend) * (
                    GELU_IN * (1.0 + 3.0 * 0.044715 * square)
                )
                du_ref[u, rows, cols] = (d_act * slope).astype(BF)

    def ffn_out(u, part):
        @pl.loop(0, d // 256)
        def _(n):
            cols = pl.ds(pl.multiple_of(n * 256, 256), 256)
            store_part(part, cols, dot_plain(act_ref[u], wd_ref[:, cols]))

    def ffn_back(u, part):
        @pl.loop(0, d // 256)
        def _(n):
            cols = pl.ds(pl.multiple_of(n * 256, 256), 256)
            store_part(part, cols, dot_second_t(du_ref[u], wi_ref[cols]))

    def hidden_back(u, task):
        task.end()

        @pl.loop(0, PER_SEG, step=4)
        def _(at):
            k = pl.ds(at, 4)
            scaled, inverse = center_of(hid_ref[u, k, high])
            grad = task.total(k)
            cot = cot_ref[u, k, high, low].astype(F32)
            d_hidden = cot + norm_back(grad, scaled, inverse, gain_1)
            vec_ref[0] += eights(grad * scaled)
            vec_ref[1] += eights(grad)
            task.second[k] = d_hidden
            datt_ref[u, k, high, low] = d_hidden.astype(BF)

        datts[u].start()
        save(task.second, dhid_hbm.at[u])

    staged = []

    def weight_grads(first, left, right):
        for n in range(d // 256):
            cols = slice(n * 256, (n + 1) * 256)
            slot = len(staged) % 2
            if len(staged) >= 2:
                for copy in staged[-2]:
                    copy.wait()
            tile = dot_first_t(left(0, cols), right(0)) + dot_first_t(left(1, cols), right(1))
            chunks = tile.shape[1] // 256
            rows = pl.ds(slot * 256, 256)
            pool_ref[rows, : tile.shape[1]] = tile.astype(BF)
            copies = [
                pltpu.make_async_copy(
                    pool_ref.at[rows, pl.ds(c * 256, 256)],
                    gffn_hbm.at[first + c, cols],
                    stage_sem.at[slot, c],
                )
                for c in range(chunks)
            ]
            for copy in copies:
                copy.start()
            staged.append(copies)

    slots = cot_new.shape[1]
    rows_here = edge_rows * PART
    edges = [
        remote(
            mem_hbm.at[:, pl.ds(0, REACH // PART)],
            ext_ref.at[:, pl.ds(edge_rows, REACH // PART)],
            edge_send.at[0],
            edge_recv.at[0],
            me.before(),
        ),
        remote(cot_new, cot_prev, edge_send.at[1], edge_recv.at[1], me.after()),
    ]
    seq = SeqReduce(me, comp_ref, comp_total, landed, (seq_send, seq_recv), [[0, 1, 2]])
    win = TpReduce(me, win_part, win_first, win_second, (rs_send, rs_recv), 0)

    def local_rows(at, tap, is_lead):
        slot = slots * me.column + at - jnp.where(is_lead, LEAD, 0)
        used = at < jnp.where(is_lead, LEAD, slots)
        slot_seg = lax.div(slot, CSEG)
        place = 3 * (slot - slot_seg * CSEG) + tap
        there = jnp.logical_and(used, jnp.logical_and(slot >= 0, place < SEG))
        return jnp.where(there, slot_seg * SEG + place - rows_here * me.column, -1)

    lead_rows = 32
    own_rows = 3 * SLOT_PAD
    ext_rows = rows_here + REACH
    feats = w_comp.shape[2]

    def compress_masks():
        row = lax.broadcasted_iota(jnp.int32, (own_rows, 1), 0)
        tap = lax.div(row, SLOT_PAD)
        local = local_rows(row - tap * SLOT_PAD, tap, False)
        where_at = lax.broadcasted_iota(jnp.int32, (own_rows, ext_rows), 1)
        pick_ref[...] = jnp.where(local == where_at, 1.0, 0.0).astype(BF)
        col = lax.broadcasted_iota(jnp.int32, (1, own_rows + 3 * lead_rows), 1)
        is_lead = col >= own_rows
        col = jnp.where(is_lead, col - own_rows, col)
        per = jnp.where(is_lead, lead_rows, SLOT_PAD)
        tap = jnp.where(is_lead, lax.div(col, lead_rows), lax.div(col, SLOT_PAD))
        local = local_rows(col - tap * per, tap, is_lead)
        where_at = lax.broadcasted_iota(jnp.int32, spread_ref.shape, 0)
        spread_ref[...] = jnp.where(local == where_at, 1.0, 0.0).astype(BF)
        cot_pad[...] = jnp.zeros(cot_pad.shape, BF)
        lead_pad[...] = jnp.zeros(lead_pad.shape, BF)

    def compress():
        for load in loads[:3]:
            load.wait()
        for copy in edges:
            copy.wait()
        grads = [None] * 3
        for m in range(2):
            cot_pad[m, :slots] = cot_own[m]
            lead_pad[m, :LEAD] = cot_prev[m, slots - LEAD :]
            cot, cot_lead = cot_pad[m], lead_pad[m]
            fresh = None
            taken = dot_plain(pick_ref[...], ext_ref[m].reshape(ext_rows, d)).astype(BF)
            for tap in range(3):
                span = slice(tap * SLOT_PAD, (tap + 1) * SLOT_PAD)
                lead = slice(own_rows + tap * lead_rows, own_rows + (tap + 1) * lead_rows)
                term = dot_plain(taken[span], wc_ref[tap])
                fresh = term if fresh is None else fresh + term
                term = dot_first_t(taken[span], cot)
                grads[tap] = term if grads[tap] is None else grads[tap] + term
                pool_ref[span, :d] = dot_second_t(cot, wc_ref[tap]).astype(BF)
                pool_ref[lead, :d] = dot_second_t(cot_lead, wc_ref[tap]).astype(BF)
            fresh_ref[m] = fresh[:slots]
            for n in range(2):
                cols = slice(n * d // 2, (n + 1) * d // 2)
                tile = dot_plain(spread_ref[...], pool_ref[:, cols])
                win_part[m * PER_DEV : (m + 1) * PER_DEV, :, :, :, cols] = (
                    tile.astype(BF).reshape(PER_DEV, 2, 2, PART, d // 2)
                )
        for tap in range(3):
            split_store(me, comp_ref, 0, tap * (feats // 256), grads[tap])
        save(fresh_ref, fresh_hbm)

    def win_end():
        win.end()

        @pl.loop(0, 2 * PER_DEV, step=2)
        def _(at):
            k = pl.ds(at, 2)
            win_second[k] = win.total(k).astype(BF)

        save(win_second, win_hbm)

    rs = (rs_send, rs_recv)
    backs = [
        TpReduce(me, back_parts[u], back_firsts[u], back_quarters[u], rs, 1 + u) for u in range(2)
    ]
    datts = [TpGather(me, datt_ref.at[u], (ag_send, ag_recv), u) for u in range(2)]

    send_out(kinds, 0)
    for copy in edges:
        copy.start()
    for copy in wo_copies[:2]:
        copy.start()
    vec_ref[...] = jnp.zeros(vec_ref.shape, F32)

    @pl.when(jnp.logical_not(spans[1][2]))
    def _():
        raw_ref[1] = jnp.zeros(raw_ref.shape[1:], BF)
        cot_ref[1, :, :, low] = jnp.zeros((PER_SEG, 2, PART, d), BF)

    compress_masks()
    norm_own(0)
    norm_moved(0)
    send_out(kinds, 1)
    for load in loads[3:6]:
        load.wait()
    project(0)
    attend(0, 0)
    wo_copies[0].wait()
    wo_copies[2].start()
    norm_own(1)
    attend(0, 1)
    ctx_start(0)
    compress()
    win.start()
    norm_moved(1)
    send_out([KINDS], 0)
    send_out([KINDS], 1)
    seq.launch(0)
    win.middle()
    project(1)
    save(q_ref, q_hbm)
    save(k_ref, k_hbm)
    save(v_ref, v_hbm)
    save(raw_ref.at[:, :, :, high], own_hbm)
    loads[6].wait()
    for copy in wo_copies[1:]:
        copy.wait()
    hidden_norm(0)
    attend(1, 0)
    cot_pass(0)
    attend(1, 1)
    win_end()
    save(lse_ref, lse_hbm)
    ctx_start(1)
    cot_pass(1)
    loads[7].wait()
    loads[8].wait()
    half_pass(nh_ref, 0, KINDS + 1).wait()
    passing(KINDS, 0).wait()
    ffn_up(0)
    ffn_back(0, back_parts[0])
    backs[0].start()
    hidden_norm(1)
    backs[0].middle()
    seq.turn()
    ffn_out(0, parts[0])
    save(parts[0], outp_hbm.at[0])
    half_pass(nh_ref, 1, KINDS + 1).wait()
    passing(KINDS, 1).wait()
    ffn_up(1)
    ffn_back(1, back_parts[1])
    backs[1].start()
    ffn_out(1, parts[1])
    save(parts[1], outp_hbm.at[1])
    seq.turn()
    backs[1].middle()
    hidden_back(0, backs[0])
    ff = wi_ref.shape[1]
    weight_grads(
        0, lambda u, cols: nh_ref[u, :, :, :, :, cols].reshape(SEG, 256), lambda u: du_ref[u]
    )
    weight_grads(
        ff // 256, lambda u, cols: cot_ref[u, :, :, :, :, cols].reshape(SEG, 256), lambda u: act_ref[u]
    )
    seq.drain()
    save(comp_total, comp_hbm)
    hidden_back(1, backs[1])
    save(vec_ref, vec_hbm)
    datts[0].middle()
    datts[0].end()
    save(datt_ref.at[0], datt_hbm.at[0])
    datts[1].middle()
    datts[1].end()
    save(datt_ref.at[1], datt_hbm.at[1])
    for micro in range(2):
        sent(kinds + [KINDS], micro)
    for copies in staged[-2:]:
        for copy in copies:
            copy.wait()
    for copy in saves:
        copy.wait()


def forward_call(rows, cot, memory, cot_new, w_comp, boundary, links, slopes, gains, shifts, weights):
    count = lax.axis_size("seq")
    bits = count.bit_length() - 1
    d = cot.shape[-1]
    heads = weights[0].shape[1] // HEAD
    width = heads * HEAD
    ff = weights[4].shape[1]
    slots, feats = cot_new.shape[1:]
    split = (PER_SEG, 2, 2, PART, d)
    half = (PER_SEG, 2, PART, d)
    own = (PER_SEG, PART, d)
    keys = KINDS * SEG
    owned = 2 * PER_DEV
    shard = d // count
    any_space = pl.BlockSpec(memory_space=pl.ANY)
    smem = pl.BlockSpec(memory_space=pltpu.SMEM)
    vmem = pl.BlockSpec(memory_space=pltpu.VMEM)
    shapes = [
        ((2, KINDS) + split, BF),
        ((2, KINDS) + own, BF),
        ((2, heads, SEG, HEAD), BF),
        ((2, heads, keys, HEAD), BF),
        ((2, heads, keys, HEAD), BF),
        ((2, heads, SEG, HEAD), F32),
        ((2, PER_SEG, 2, 2, PART, width), BF),
        ((2, heads, SEG, HEAD), F32),
        ((2,) + split, BF),
        ((2,) + own, F32),
        ((2,) + own, F32),
        ((2,) + split, BF),
        ((2 * ff // 256, d, 256), BF),
        ((2, 8, d), F32),
        ((owned, PART, d), BF),
        ((2, slots, feats), F32),
        ((shard, 3 * feats), F32),
    ]
    dma = pltpu.SemaphoreType.DMA
    total_rows = 3 * (SLOT_PAD + 32)
    ext_rows = memory.shape[1] + REACH // PART
    scratch = [
        pltpu.VMEM((2, KINDS) + split, BF),
        pltpu.VMEM((2, KINDS) + half, BF),
        pltpu.VMEM((2,) + split, BF),
        pltpu.VMEM((2, heads, SEG, HEAD), BF),
        pltpu.VMEM((2, heads, keys, HEAD), BF),
        pltpu.VMEM((2, heads, keys, HEAD), BF),
        pltpu.VMEM((2, heads, SEG, HEAD), F32),
        pltpu.VMEM((2, PER_SEG, 2, 2, PART, width), BF),
        pltpu.VMEM((2, heads, SEG, HEAD), F32),
        pltpu.VMEM((2, PER_SEG, 2, PART, 4 * width), BF),
        pltpu.VMEM((d, 3 * width), BF),
        pltpu.VMEM((4 * width, d), BF),
        pltpu.VMEM((d, ff), BF),
        pltpu.VMEM((ff, d), BF),
        [pltpu.VMEM(split, BF) for _ in range(2)],
        [pltpu.VMEM(split, F32) for _ in range(2)],
        [pltpu.VMEM(half, F32) for _ in range(2)],
        [pltpu.VMEM(own, F32) for _ in range(2)],
        pltpu.VMEM((2,) + split, BF),
        pltpu.VMEM((2,) + split, BF),
        pltpu.VMEM((2, SEG, ff), BF),
        pltpu.VMEM((2, SEG, ff), BF),
        pltpu.VMEM((2,) + half, F32),
        pltpu.VMEM((2, 8, d), F32),
        pltpu.VMEM((2, ext_rows, PART, d), BF),
        pltpu.VMEM((2, slots, feats), BF),
        pltpu.VMEM((2, slots, feats), BF),
        pltpu.VMEM((2, SLOT_PAD, feats), BF),
        pltpu.VMEM((2, 32, feats), BF),
        pltpu.VMEM((3, d, feats), BF),
        pltpu.VMEM((3 * SLOT_PAD, ext_rows * PART), BF),
        pltpu.VMEM((memory.shape[1] * PART, total_rows), BF),
        pltpu.VMEM((total_rows, max(d, ff)), BF),
        pltpu.VMEM((owned, 2, 2, PART, d), BF),
        pltpu.VMEM((owned, 2, PART, d), BF),
        pltpu.VMEM((owned, PART, d), BF),
        pltpu.VMEM((2, slots, feats), F32),
        pltpu.VMEM((3 * feats // 256,) + (2,) * bits + (shard, 256), BF),
        pltpu.VMEM((shard, 3 * feats), F32),
        [
            pltpu.VMEM((3 * feats // 256,) + (2,) * (bits - 1 - i) + (shard, 256), BF)
            for i in range(bits)
        ],
        dma((9,)),
        dma((24,)),
        dma((2, ff // 256)),
        dma((KINDS + 1, 2, PER_SEG)),
        dma((KINDS + 1, 2, PER_DEV)),
        dma((KINDS + 1, 2, PER_SEG)),
        dma((KINDS + 3, 2)),
        dma((KINDS + 3, 2)),
        dma((2, 3)),
        dma((2, 3)),
        dma((3,)),
        dma((3,)),
        dma((2,)),
        dma((2,)),
        dma((3, 2)),
        dma((3, 2)),
        dma((2, 2)),
        dma((2, 2)),
        dma((bits, 3)),
        dma((bits, 3)),
    ]
    return pl.pallas_call(
        forward_kernel,
        out_shape=[jax.ShapeDtypeStruct(shape, kind) for shape, kind in shapes],
        in_specs=[[any_space] * KINDS]
        + [any_space] * 4
        + [smem] * 3
        + [vmem] * 2
        + [any_space] * 6,
        out_specs=[any_space] * len(shapes),
        scratch_shapes=scratch,
        compiler_params=pltpu.CompilerParams(
            collective_id=1, has_side_effects=True, vmem_limit_bytes=63 << 20
        ),
    )(rows, cot, memory, cot_new, w_comp, boundary, links, slopes, gains, shifts, *weights)


FINALS = 4


def backward_kernel(
    normed_hbm,
    own_hbm,
    q_hbm,
    k_hbm,
    v_hbm,
    lse_hbm,
    ctx_hbm,
    ctxn_hbm,
    outp_hbm,
    hid_hbm,
    dhid_hbm,
    datt_hbm,
    gffn_hbm,
    win_hbm,
    vec_in,
    boundary,
    links,
    slopes,
    gains,
    w_query,
    w_key,
    w_value,
    w_out,
    finals,
    total_hbm,
    small_hbm,
    normed_ref,
    own_ref,
    q_ref,
    kx_ref,
    v_ref,
    lse_ref,
    ctx_ref,
    ctxn_ref,
    dhid_ref,
    datt_ref,
    wqkv_ref,
    wo_ref,
    dctx_ref,
    ds_ref,
    prob_ref,
    dq_ref,
    dqkv_ref,
    parts,
    firsts,
    seconds,
    out_parts,
    hid_ref,
    out_ref,
    win_ref,
    home_ref,
    owner_ref,
    grads_ref,
    total_ref,
    landed,
    vec_ref,
    aux_ref,
    small_ref,
    small_came,
    load_sem,
    save_sem,
    rs_send,
    rs_recv,
    ag_send,
    ag_recv,
    ag_here,
    move_send,
    move_recv,
    seq_send,
    seq_recv,
    small_send,
    small_recv,
):
    me = Place()
    d = normed_ref.shape[-1]
    heads = q_ref.shape[1]
    width = heads * HEAD
    late = gffn_hbm.shape[0]
    heads_wide = width // 256

    load_pairs = {
        "gffn": (gffn_hbm, grads_ref.at[pl.ds(0, late)]),
        "outp0": (outp_hbm.at[0], out_parts[0]),
        "outp1": (outp_hbm.at[1], out_parts[1]),
        "datt": (datt_hbm, datt_ref),
        "wo": (w_out, wo_ref),
        "v": (v_hbm, v_ref),
        "ctxn": (ctxn_hbm, ctxn_ref),
        "lse": (lse_hbm, lse_ref),
        "k": (k_hbm, kx_ref.at[:, :, :, pl.ds(0, HEAD)]),
        "q": (q_hbm, q_ref),
        "wk": (w_key, wqkv_ref.at[:, pl.ds(0, width)]),
        "wv": (w_value, wqkv_ref.at[:, pl.ds(width, width)]),
        "wq": (w_query, wqkv_ref.at[:, pl.ds(2 * width, width)]),
        "hid": (hid_hbm, hid_ref),
        "own": (own_hbm, own_ref),
        "dhid": (dhid_hbm, dhid_ref),
        "win": (win_hbm, win_ref),
        "vec": (vec_in, vec_ref.at[pl.ds(2, 2)]),
        "normed": (normed_hbm, normed_ref),
        "ctx": (ctx_hbm, ctx_ref),
    }
    loads = {
        name: pltpu.make_async_copy(src, dst, load_sem.at[i])
        for i, (name, (src, dst)) in enumerate(load_pairs.items())
    }
    for load in loads.values():
        load.start()

    def ready(*names):
        for name in names:
            loads[name].wait()

    meet(
        me,
        [me.mate(), me.across(), me.after(), me.before()]
        + [me.flipped(b) for b in range(me.bits)],
    )

    gain_0 = gains[0:1]
    vec_ref[:2] = jnp.zeros((2,) + vec_ref.shape[1:], F32)
    aux_ref[...] = jnp.zeros(aux_ref.shape, F32)
    key_at = lax.broadcasted_iota(jnp.int32, (KINDS * SEG, HEAD), 0)
    lane = lax.broadcasted_iota(jnp.int32, (KINDS * SEG, HEAD), 1)
    kind_at = lax.div(key_at, SEG)
    in_kind = key_at - SEG * kind_at
    odd = lax.rem(in_kind, 2)
    marks = jnp.where(
        lane == 0,
        in_kind - odd,
        jnp.where(lane == 1, odd, jnp.where(lane == 2, kind_at, jnp.where(lane == 3, 1, 0))),
    )
    marks = marks.astype(F32).astype(BF)
    for u in range(2):
        for h in range(heads):
            kx_ref[u, h, :, HEAD:] = marks

    rs = (rs_send, rs_recv)
    sems = (seq_send, seq_recv)
    chunks = grads_ref.shape[0]
    n = chunks - 8
    groups = [[i] for i in range(n)] + [[n, n + 1], [n + 2, n + 3, n + 4], [n + 5, n + 6, n + 7]]
    seq = SeqReduce(me, grads_ref, total_ref, landed, sems, groups)


    def to_owner(kind, slot):
        segment, micro, there = units_of(me.column, slot)

        @pl.loop(0, PER_SEG)
        def _(chunk):
            place = PER_SEG * segment + chunk
            holder = lax.div(place, PER_DEV)
            q = lax.rem(place, PER_DEV)
            src = out_ref.at[slot, chunk] if kind == KINDS else home_ref.at[kind, slot, chunk]
            dst = owner_ref.at[kind, micro, q]

            @pl.when(jnp.logical_and(there, holder == me.column))
            def _():
                pltpu.make_async_copy(src, dst, move_recv.at[kind, micro, q]).start()

            @pl.when(jnp.logical_and(there, holder != me.column))
            def _():
                remote(
                    src,
                    dst,
                    move_send.at[kind, slot, chunk],
                    move_recv.at[kind, micro, q],
                    me.beside(holder - me.column),
                ).start()

    def sent(kind, slot):
        segment, micro, there = units_of(me.column, slot)

        @pl.loop(0, PER_SEG)
        def _(chunk):
            holder = lax.div(PER_SEG * segment + chunk, PER_DEV)

            @pl.when(jnp.logical_and(there, holder != me.column))
            def _():
                src = home_ref.at[0, slot, chunk]
                remote(
                    src,
                    src,
                    move_send.at[kind, slot, chunk],
                    move_recv.at[kind, 0, 0],
                    me.mate(),
                ).wait_send()

    def collect(kind, micro):
        @pl.loop(0, PER_DEV)
        def _(q):
            segment = jnp.where(q < me.column, me.column - 1, me.column)
            home, slot = home_of(segment, micro)
            dst = owner_ref.at[kind, micro, q]

            @pl.when(home == me.column)
            def _():
                pltpu.make_async_copy(dst, dst, move_recv.at[kind, micro, q]).wait()

            @pl.when(home != me.column)
            def _():
                remote(
                    dst,
                    dst,
                    move_send.at[kind, 0, 0],
                    move_recv.at[kind, micro, q],
                    me.mate(),
                ).wait_recv()

    class Final:
        def __init__(self, kind, micro):
            self.own = owner_ref.at[kind, micro]
            whole = finals[kind].at[micro]
            self.mine = whole.at[:, me.high, me.low]
            self.here = pltpu.make_async_copy(self.own, self.mine, ag_here.at[kind, micro])
            self.one = remote(
                self.own,
                self.mine,
                ag_send.at[kind, micro, 0],
                ag_recv.at[kind, micro, 0],
                me.across(),
            )
            both = whole.at[:, :, me.low]
            self.two = remote(
                both, both, ag_send.at[kind, micro, 1], ag_recv.at[kind, micro, 1], me.mate()
            )

        def start(self):
            self.here.start()
            self.one.start()

        def middle(self):
            self.here.wait()
            self.one.wait()
            self.two.start()

        def end(self):
            self.two.wait()

    def context_back(u):
        datt = datt_ref[u].reshape(SEG, d)
        for h in range(heads):
            rows = slice(h * HEAD, (h + 1) * HEAD)
            dctx_ref[u, h] = dot_second_t(datt, wo_ref[rows]).astype(BF)

    segments = lax.div(me.seq, PER_SEG) * PER_DEV

    def attend_back(u, h, kind):
        scale = HEAD ** (-0.5)
        rows_at_once = 2 * QUERY_BLOCK
        keys = slice(kind * SEG, (kind + 1) * SEG)
        segment, micro, _ = units_of(me.column, u)
        segment = jnp.minimum(segment, PER_DEV - 1) + segments
        edge = boundary[micro, segment]
        linked = links[micro, segment]
        key_x = lax.broadcasted_iota(jnp.int32, (1, SEG), 1)
        bias = (key_x - SEG * kind).astype(F32) * (slopes[h] / SEG)

        @pl.loop(0, SEG // rows_at_once)
        def _(b):
            rows = pl.ds(pl.multiple_of(b * rows_at_once, rows_at_once), rows_at_once)
            scores = dot_second_t(q_ref[u, h, rows], kx_ref[u, h, keys, :HEAD]) * scale + bias
            at = b * rows_at_once + lax.broadcasted_iota(jnp.int32, (rows_at_once, 1), 0)
            if kind == 0:
                seen = jnp.logical_and(key_x <= at, jnp.logical_or(key_x >= edge, at < edge))
            else:
                seen = jnp.logical_and(at < edge, linked == 1)
            prob = jnp.exp(jnp.where(seen, scores - lse_ref[u, h, rows, :1], -1e30))
            prob_ref[rows] = prob.astype(BF)
            d_ctx = dctx_ref[u, h, rows]
            d_prob = dot_second_t(d_ctx, v_ref[u, h, keys])
            mean = jnp.sum(d_ctx.astype(F32) * ctxn_ref[u, h, rows], axis=-1, keepdims=True)
            d_scores = (prob * (d_prob - mean)).astype(BF)
            ds_ref[rows] = d_scores
            both = dot_plain(d_scores, kx_ref[u, h, keys])
            if kind < KINDS - 1:
                both += dq_ref[h, rows]
            if kind > 0:
                dq_ref[h, rows] = both
            else:
                cols = slice(2 * width + h * HEAD, 2 * width + (h + 1) * HEAD)
                dqkv_ref[u, 0, rows, cols] = (both[:, :HEAD] * scale).astype(BF)
                marked = both[:, HEAD:]
                at = b * rows_at_once + lax.broadcasted_iota(jnp.int32, marked.shape, 0)
                aux_ref[h, 0:1] += jnp.sum(marked, axis=0, keepdims=True)
                aux_ref[h, 1:2] += jnp.sum(marked * at.astype(F32), axis=0, keepdims=True)

        d_key = dot_first_t(ds_ref[...], q_ref[u, h]) * scale
        d_value = dot_first_t(prob_ref[...], dctx_ref[u, h])
        dqkv_ref[u, kind, :, h * HEAD : (h + 1) * HEAD] = d_key.astype(BF)
        dqkv_ref[u, kind, :, width + h * HEAD : width + (h + 1) * HEAD] = d_value.astype(BF)

    def project_back(u, kind, part):
        depth = (3 if kind == 0 else 2) * width

        @pl.loop(0, d // 256)
        def _(n):
            cols = pl.ds(pl.multiple_of(n * 256, 256), 256)
            tile = dot_second_t(dqkv_ref[u, kind, :, :depth], wqkv_ref[cols, :depth])
            part[:, :, :, :, cols] = tile.astype(BF).reshape(PER_SEG, 2, 2, PART, 256)

    def norm_end(u, kind, task):
        task.end()

        @pl.loop(0, PER_SEG, step=4)
        def _(at):
            k = pl.ds(at, 4)
            scaled, inverse = center_of(own_ref[u, kind, k].astype(F32))
            grad = task.total(k)
            vec_ref[0] += eights(grad * scaled)
            vec_ref[1] += eights(grad)
            result = norm_back(grad, scaled, inverse, gain_0)
            if kind == 0:
                result += dhid_ref[u, k]
            home_ref[kind, u, k] = result.astype(BF)

    def add_window(micro):
        @pl.loop(0, PER_DEV)
        def _(q):
            added = owner_ref[1, micro, q].astype(F32) + win_ref[micro * PER_DEV + q].astype(F32)
            owner_ref[1, micro, q] = added.astype(BF)

    def late_kv():
        for n in range(d // 256):
            cols = slice(n * 256, (n + 1) * 256)
            kv = None
            for u in range(2):
                for kind in range(KINDS):
                    left = normed_ref[u, kind, :, :, :, :, cols].reshape(SEG, 256)
                    term = dot_first_t(left, dqkv_ref[u, kind, :, : 2 * width])
                    kv = term if kv is None else kv + term
            split_store(me, grads_ref, n * 256, late + heads_wide, kv)

    def late_query():
        for n in range(d // 256):
            cols = slice(n * 256, (n + 1) * 256)
            query = None
            for u in range(2):
                left = normed_ref[u, 0, :, :, :, :, cols].reshape(SEG, 256)
                term = dot_first_t(left, dqkv_ref[u, 0, :, 2 * width :])
                query = term if query is None else query + term
            split_store(me, grads_ref, n * 256, late + 3 * heads_wide, query)

    def out_grad():
        for n in range(d // 256):
            cols = slice(n * 256, (n + 1) * 256)
            out = None
            for u in range(2):
                left = datt_ref[u, :, :, :, :, cols].reshape(SEG, 256)
                term = dot_first_t(left, ctx_ref[u].reshape(SEG, width))
                out = term if out is None else out + term
            split_store(me, grads_ref, n * 256, late, out)

    friends = [me.mate(), me.across()] + [me.flipped(b) for b in range(me.bits)]

    def small_copy(i):
        return remote(
            small_ref, small_came.at[i], small_send.at[i], small_recv.at[i], friends[i]
        )

    def small_start():
        lane = lax.broadcasted_iota(jnp.int32, (1, HEAD), 1)
        plain = jnp.where(lane < 2, 1.0, jnp.where(lane == 2, -float(SEG), 0.0))
        placed = jnp.where(lane == 3, 1.0, 0.0)
        small_ref[...] = jnp.zeros(small_ref.shape, F32)
        for i, at in enumerate((0, 2, 1, 3)):
            small_ref[i : i + 1] = jnp.sum(vec_ref[at], axis=0, keepdims=True)
        row = jnp.zeros((1, HEAD), F32)
        for h in range(heads):
            marked = aux_ref[h, 0:1] * plain - aux_ref[h, 1:2] * placed
            total = jnp.sum(marked, axis=-1, keepdims=True) / SEG
            row += jnp.where(lane == me.tp * heads + h, total, 0.0)
        small_ref[4:5, :HEAD] = row
        small_copy(0).start()

    def small_step(i):
        small_copy(i).wait()
        small_ref[...] += small_came[i]
        if i + 1 < len(friends):
            small_copy(i + 1).start()

    results = {}

    def final_start(kind, micro):
        collect(kind, micro)
        if kind == 1:
            add_window(micro)
        results[kind, micro] = Final(kind, micro)
        results[kind, micro].start()

    tasks = {
        (u, kind): TpReduce(
            me, parts[kind], firsts[u * KINDS + kind], seconds[u * KINDS + kind], rs, u * KINDS + kind
        )
        for u in range(2)
        for kind in range(KINDS)
    }

    def attend_kind(u, kind):
        for h in range(heads):
            attend_back(u, h, kind)

    def send_kind(u, kind):
        project_back(u, kind, parts[kind])
        tasks[u, kind].start()

    def end_kind(u, kind):
        norm_end(u, kind, tasks[u, kind])
        to_owner(kind, u)

    outs = [
        TpReduce(
            me, out_parts[u], firsts[2 * KINDS + u], seconds[2 * KINDS + u], rs, 2 * KINDS + u
        )
        for u in range(2)
    ]

    def out_end(u):
        outs[u].end()

        @pl.loop(0, PER_SEG, step=4)
        def _(at):
            k = pl.ds(at, 4)
            out_ref[u, k] = (hid_ref[u, k] + outs[u].total(k)).astype(BF)

        to_owner(KINDS, u)

    ready("outp0", "outp1")
    for u in range(2):
        outs[u].start()
    ready("gffn")
    for group in range(3):
        seq.launch(group)
    ready("datt", "wo")
    context_back(0)
    ready("v", "ctxn", "lse", "k", "q")
    for u in range(2):
        outs[u].middle()
    attend_kind(0, 2)
    ready("wk", "wv", "wq")
    send_kind(0, 2)
    seq.turn()
    seq.launch(3)
    attend_kind(0, 1)
    tasks[0, 2].middle()
    send_kind(0, 1)
    seq.turn()
    seq.launch(4)
    attend_kind(0, 0)
    tasks[0, 1].middle()
    send_kind(0, 0)
    ready("hid")
    out_end(0)
    out_end(1)
    seq.turn()
    context_back(1)
    ready("ctx")
    out_grad()
    tasks[0, 0].middle()
    ready("own", "dhid", "win", "vec")
    attend_kind(1, 2)
    end_kind(0, 2)
    send_kind(1, 2)
    seq.turn()
    seq.launch(5)
    final_start(KINDS, 0)
    final_start(KINDS, 1)
    attend_kind(1, 1)
    end_kind(0, 1)
    tasks[1, 2].middle()
    send_kind(1, 1)
    seq.turn()
    attend_kind(1, 0)
    end_kind(0, 0)
    tasks[1, 1].middle()
    send_kind(1, 0)
    final_start(2, 0)
    ready("normed")
    late_kv()
    tasks[1, 0].middle()
    late_query()
    seq.launch(6)
    seq.turn()
    results[KINDS, 0].middle()
    results[KINDS, 1].middle()
    final_start(1, 0)
    end_kind(1, 2)
    final_start(0, 0)
    end_kind(1, 1)
    results[2, 0].middle()
    final_start(2, 1)
    end_kind(1, 0)
    small_start()
    results[1, 0].middle()
    small_step(0)
    final_start(1, 1)
    seq.turn()
    results[0, 0].middle()
    final_start(0, 1)
    small_step(1)
    results[2, 1].middle()
    seq.turn()
    for i in range(2, len(friends)):
        small_step(i)
    results[1, 1].middle()
    seq.drain()
    results[0, 1].middle()
    saves = [
        pltpu.make_async_copy(total_ref, total_hbm, save_sem.at[0]),
        pltpu.make_async_copy(small_ref, small_hbm, save_sem.at[1]),
    ]
    for save in saves:
        save.start()
    for kind in range(FINALS):
        for at in range(2):
            results[kind, at].end()
            sent(kind, at)
    for save in saves:
        save.wait()


def backward_call(saved, boundary, links, slopes, gains, weights):
    normed, own, q, k, v, lse, ctx, ctxn, outp, hid, dhid, datt, gffn, vec, win = saved
    count = lax.axis_size("seq")
    bits = count.bit_length() - 1
    d = normed.shape[-1]
    heads = q.shape[1]
    keys = KINDS * SEG
    width = heads * HEAD
    chunks = gffn.shape[0] + 4 * width // 256
    columns = 256 * chunks
    view = (2,) * bits + (d // count, 256)
    split = (PER_SEG, 2, 2, PART, d)
    any_space = pl.BlockSpec(memory_space=pl.ANY)
    vmem = pl.BlockSpec(memory_space=pltpu.VMEM)
    smem = pl.BlockSpec(memory_space=pltpu.SMEM)
    dma = pltpu.SemaphoreType.DMA
    final = jax.ShapeDtypeStruct((2, PER_DEV, 2, 2, PART, d), BF)
    scratch = [
        pltpu.VMEM(normed.shape, BF),
        pltpu.VMEM(own.shape, BF),
        pltpu.VMEM(q.shape, BF),
        pltpu.VMEM((2, heads, keys, 2 * HEAD), BF),
        pltpu.VMEM(v.shape, BF),
        pltpu.VMEM(lse.shape, F32),
        pltpu.VMEM(ctx.shape, BF),
        pltpu.VMEM(ctxn.shape, F32),
        pltpu.VMEM(dhid.shape, F32),
        pltpu.VMEM(datt.shape, BF),
        pltpu.VMEM((d, 3 * width), BF),
        pltpu.VMEM((width, d), BF),
        pltpu.VMEM((2, heads, SEG, HEAD), BF),
        pltpu.VMEM((SEG, SEG), BF),
        pltpu.VMEM((SEG, SEG), BF),
        pltpu.VMEM((heads, SEG, 2 * HEAD), F32),
        pltpu.VMEM((2, KINDS, SEG, 3 * width), BF),
        [pltpu.VMEM(split, BF) for _ in range(KINDS)],
        [pltpu.VMEM((PER_SEG, 2, PART, d), BF) for _ in range(2 * KINDS + 2)],
        [pltpu.VMEM((PER_SEG, PART, d), BF) for _ in range(2 * KINDS + 2)],
        [pltpu.VMEM(split, BF) for _ in range(2)],
        pltpu.VMEM(hid.shape, F32),
        pltpu.VMEM(hid.shape, BF),
        pltpu.VMEM(win.shape, BF),
        pltpu.VMEM((KINDS, 2, PER_SEG, PART, d), BF),
        pltpu.VMEM((FINALS, 2, PER_DEV, PART, d), BF),
        pltpu.VMEM((chunks,) + view, BF),
        pltpu.VMEM((d // count, columns), F32),
        [pltpu.VMEM((chunks,) + view[i + 1 :], BF) for i in range(bits)],
        pltpu.VMEM((4, 8, d), F32),
        pltpu.VMEM((heads, 8, HEAD), F32),
        pltpu.VMEM((8, d), F32),
        pltpu.VMEM((bits + 2, 8, d), F32),
        dma((20,)),
        dma((2,)),
        dma((2 * KINDS + 2, 2)),
        dma((2 * KINDS + 2, 2)),
        dma((FINALS, 2, 2)),
        dma((FINALS, 2, 2)),
        dma((FINALS, 2)),
        dma((FINALS, 2, PER_SEG)),
        dma((FINALS, 2, PER_DEV)),
        dma((bits, chunks)),
        dma((bits, chunks)),
        dma((bits + 2,)),
        dma((bits + 2,)),
    ]
    return pl.pallas_call(
        backward_kernel,
        out_shape=[
            [final] * FINALS,
            jax.ShapeDtypeStruct((d // count, columns), F32),
            jax.ShapeDtypeStruct((8, d), F32),
        ],
        in_specs=[any_space] * 15 + [smem] * 3 + [vmem] + [any_space] * 4,
        out_specs=[[any_space] * FINALS] + [any_space] * 2,
        scratch_shapes=scratch,
        compiler_params=pltpu.CompilerParams(
            collective_id=2, has_side_effects=True, vmem_limit_bytes=63 << 20
        ),
    )(
        normed,
        own,
        q,
        k,
        v,
        lse,
        ctx,
        ctxn,
        outp,
        hid,
        dhid,
        datt,
        gffn.reshape((gffn.shape[0],) + view),
        win,
        vec,
        boundary,
        links,
        slopes,
        gains,
        *weights,
    )


def per_device(
    inputs,
    memory,
    compressed,
    boundary,
    links,
    gains,
    shifts,
    slopes,
    w_query,
    w_key,
    w_value,
    w_out,
    w_in,
    w_down,
    w_comp,
    cot_out,
    cot_new,
):
    d = inputs.shape[-1]
    rows = inputs.shape[1]
    heads = slopes.shape[0]
    width = heads * HEAD
    ff = w_in.shape[1]
    feats = w_comp.shape[2]
    count = lax.axis_size("seq")
    seq = lax.axis_index("seq")
    tp = lax.axis_index("tp")

    def chunked(array):
        return array.reshape(2, PER_DEV, 2, 2, PART, d)

    *saved, fresh, comp = forward_call(
        [chunked(inputs), chunked(memory), chunked(compressed)],
        chunked(cot_out),
        memory.reshape(2, rows // PART, PART, d),
        cot_new,
        w_comp,
        boundary,
        links,
        slopes,
        gains,
        shifts,
        (w_query, w_key, w_value, w_out, w_in, w_down),
    )
    finals, total, small = backward_call(
        saved, boundary, links, slopes, gains, (w_query, w_key, w_value, w_out)
    )
    vectors = lax.dynamic_slice(small, (0, seq * (d // count)), (4, d // count))
    grad_slopes = lax.dynamic_slice(small, (4, tp * heads), (1, heads))[0]

    def whole(array):
        return array.reshape(2, rows, d)

    pieces, at = [], 0
    for cut in [ff, ff] + [width] * 4:
        pieces.append(total[:, at : at + cut])
        at += cut
    g_in, g_down, g_out, g_key, g_value, g_query = pieces
    return (
        whole(finals[3]),
        whole(finals[0]).astype(F32),
        whole(finals[1]).astype(F32),
        whole(finals[2]).astype(F32),
        fresh,
        vectors[:2],
        vectors[2:],
        grad_slopes,
        g_query,
        g_key,
        g_value,
        g_out.T,
        g_in,
        g_down.T,
        jnp.stack([comp[:, i * feats : (i + 1) * feats] for i in range(3)]),
    )


def solution(mesh):
    in_specs = (
        P(None, "seq", None),
        P(None, "seq", None),
        P(None, "seq", None),
        P(),
        P(),
        P(),
        P(),
        P("tp"),
        P(None, "tp"),
        P(None, "tp"),
        P(None, "tp"),
        P("tp", None),
        P(None, "tp"),
        P("tp", None),
        P(None, None, "tp"),
        P(None, "seq", None),
        P(None, "seq", "tp"),
    )
    out_specs = (
        P(None, "seq", None),
        P(None, "seq", None),
        P(None, "seq", None),
        P(None, "seq", None),
        P(None, "seq", "tp"),
        P(None, "seq"),
        P(None, "seq"),
        P("tp"),
        P("seq", "tp"),
        P("seq", "tp"),
        P("seq", "tp"),
        P("tp", "seq"),
        P("seq", "tp"),
        P("tp", "seq"),
        P(None, "seq", "tp"),
    )
    return jax.shard_map(
        per_device, mesh=mesh, in_specs=in_specs, out_specs=out_specs, check_vma=False
    )
```

```python
import functools
import math

import jax
import jax.numpy as jnp
from jax import lax
from jax.experimental import pallas as pl
from jax.experimental.pallas import tpu as pltpu
from jax.sharding import PartitionSpec as P

HEAD = 128
SEG = 512
CSEG = 176
REACH = 32
LEAD = 26
SLOT_PAD = 160
CHUNK = 64
PART = 16
KINDS = 3
NORM_EPS = 1e-05
MESH = pl.DeviceIdType.MESH
BF = jnp.bfloat16
F32 = jnp.float32
GELU_IN = math.sqrt(2.0 / math.pi)
PER_SEG = SEG // CHUNK
PER_DEV = PER_SEG - 1
QUERY_BLOCK = 128


def dot_plain(a, b):
    return jnp.dot(a, b, preferred_element_type=F32)


def dot_first_t(a, b):
    return lax.dot_general(a, b, (((0,), (0,)), ((), ())), preferred_element_type=F32)


def dot_second_t(a, b):
    return lax.dot_general(a, b, (((1,), (1,)), ((), ())), preferred_element_type=F32)


def home_of(segment, micro):
    middle = PER_DEV // 2
    home = jnp.where(
        segment < middle, segment, jnp.where(segment == middle, middle + micro, segment + 1)
    )
    slot = jnp.where(segment == middle, 0, micro)
    return home, slot


def units_of(place, slot):
    middle = PER_DEV // 2
    segment = jnp.where(place <= middle, place, place - 1)
    is_middle = segment == middle
    micro = jnp.where(is_middle, place - middle, slot)
    return segment, micro, jnp.logical_or(jnp.logical_not(is_middle), slot == 0)


class Place:
    def __init__(self):
        self.seq = lax.axis_index("seq")
        self.tp = lax.axis_index("tp")
        self.column = lax.rem(self.seq, PER_SEG)
        self.low = lax.rem(self.tp, 2)
        self.high = lax.div(self.tp, 2)
        self.count = lax.axis_size("seq")
        self.bits = self.count.bit_length() - 1
        self.bit = [lax.rem(lax.div(self.seq, 1 << b), 2) for b in range(self.bits)]

    def flipped(self, bit):
        return self.beside((1 - 2 * self.bit[bit]) * (1 << bit))

    def after(self):
        return (lax.rem(self.seq + 1, self.count), self.tp)

    def before(self):
        return (lax.rem(self.seq + self.count - 1, self.count), self.tp)

    def mate(self):
        return (self.seq, self.tp + 1 - 2 * self.low)

    def across(self):
        return (self.seq, self.tp + 2 - 4 * self.high)

    def corner(self):
        return (self.seq, self.tp + 3 - 2 * self.low - 4 * self.high)

    def beside(self, by):
        return (self.seq + by, self.tp)


def remote(src, dst, send, recv, device):
    return pltpu.make_async_remote_copy(
        src_ref=src,
        dst_ref=dst,
        send_sem=send,
        recv_sem=recv,
        device_id=device,
        device_id_type=MESH,
    )


class TpReduce:
    def __init__(self, me, part, first, second, sems, index):
        self.me, self.part, self.first, self.second = me, part, first, second
        send, recv = sems
        self.one = remote(
            part.at[:, :, 1 - me.low], first, send.at[index, 0], recv.at[index, 0], me.mate()
        )
        self.two = remote(
            part.at[:, 1 - me.high, me.low],
            second,
            send.at[index, 1],
            recv.at[index, 1],
            me.across(),
        )

    def start(self):
        self.one.start()

    def middle(self):
        self.one.wait()
        part, first, low = self.part, self.first, self.me.low

        @pl.loop(0, part.shape[0], step=2)
        def _(at):
            k = pl.ds(at, 2)
            added = part[k, :, low].astype(F32) + first[k].astype(F32)
            part[k, :, low] = added.astype(part.dtype)

        self.two.start()

    def end(self):
        self.two.wait()

    def total(self, k):
        me = self.me
        return self.part[k, me.high, me.low].astype(F32) + self.second[k].astype(F32)


class TpGather:
    def __init__(self, me, whole, sems, index):
        send, recv = sems
        mine = whole.at[:, me.high, me.low]
        self.one = remote(mine, mine, send.at[index, 0], recv.at[index, 0], me.across())
        both = whole.at[:, :, me.low]
        self.two = remote(both, both, send.at[index, 1], recv.at[index, 1], me.mate())

    def start(self):
        self.one.start()

    def middle(self):
        self.one.wait()
        self.two.start()

    def end(self):
        self.two.wait()


def meet(me, friends):
    barrier = pltpu.get_barrier_semaphore()
    for friend in friends:
        pl.semaphore_signal(barrier, inc=1, device_id=friend, device_id_type=MESH)
    pl.semaphore_wait(barrier, len(friends))


def center_of(rows):
    center = rows - jnp.mean(rows, axis=-1, keepdims=True)
    inverse = lax.rsqrt(jnp.mean(center * center, axis=-1, keepdims=True) + NORM_EPS)
    return center * inverse, inverse


def norm_back(grad, scaled, inverse, gain):
    weighted = grad * gain
    first = jnp.mean(weighted, axis=-1, keepdims=True)
    second = jnp.mean(weighted * scaled, axis=-1, keepdims=True)
    return inverse * (weighted - first - scaled * second)


def eights(rows):
    d = rows.shape[-1]
    return jnp.sum(rows.reshape(-1, PART // 2, d), axis=0)


class SeqReduce:
    width = 256

    def __init__(self, me, grads, total, landed, sems, groups):
        self.me, self.grads, self.total, self.landed = me, grads, total, landed
        self.send, self.recv = sems
        self.groups = groups
        self.turn_at = 0

    def cols(self, chunk):
        return pl.ds(chunk * self.width, self.width)

    def plan(self, chunk):
        first = 1 if chunk % 5 == 4 else 0
        return [(i + first) % self.me.bits for i in range(self.me.bits)]

    def index(self, chunk, step, own):
        plan = self.plan(chunk)
        out = [chunk]
        for b in reversed(range(self.me.bits)):
            if b in plan[:step] or (b == plan[step] and own):
                out.append(self.me.bit[b])
            elif b == plan[step]:
                out.append(1 - self.me.bit[b])
            else:
                out.append(slice(None))
        return tuple(out)

    def copy(self, chunk, step):
        return remote(
            self.grads.at[self.index(chunk, step, False)],
            self.landed[step].at[chunk],
            self.send.at[step, chunk],
            self.recv.at[step, chunk],
            self.me.flipped(self.plan(chunk)[step]),
        )

    def finish(self, chunk, step):
        self.copy(chunk, step).wait()
        here = self.index(chunk, step, True)
        added = self.grads[here].astype(F32) + self.landed[step][chunk].astype(F32)
        if step == self.me.bits - 1:
            self.total[:, self.cols(chunk)] = added
        else:
            self.grads[here] = added.astype(BF)
            self.copy(chunk, step + 1).start()

    def launch(self, group):
        for chunk in self.groups[group]:
            self.copy(chunk, 0).start()

    def turn(self):
        at = self.turn_at
        self.turn_at += 1
        for step in reversed(range(self.me.bits)):
            group = at - step
            if 0 <= group < len(self.groups):
                for chunk in self.groups[group]:
                    self.finish(chunk, step)

    def drain(self):
        while self.turn_at < len(self.groups) + self.me.bits - 1:
            self.turn()


def split_store(me, grads, rows_from, first, tile):
    per, wide = grads.shape[-2:]
    n = tile.shape[0] // per
    for c in range(tile.shape[1] // wide):
        parts = tile[:, c * wide : (c + 1) * wide].astype(BF).reshape((n, per, wide))
        for i in range(n):
            at = rows_from // per + i
            grads[(first + c,) + tuple((at >> b) & 1 for b in reversed(range(me.bits)))] = parts[i]


def forward_kernel(
    rows_hbm,
    cot_hbm,
    mem_hbm,
    cot_new,
    w_comp,
    boundary,
    links,
    slopes,
    gains,
    shifts,
    w_query,
    w_key,
    w_value,
    w_out,
    w_in,
    w_down,
    normed_hbm,
    own_hbm,
    q_hbm,
    k_hbm,
    v_hbm,
    lse_hbm,
    ctx_hbm,
    ctxn_hbm,
    outp_hbm,
    hid_hbm,
    dhid_hbm,
    datt_hbm,
    gffn_hbm,
    vec_hbm,
    win_hbm,
    fresh_hbm,
    comp_hbm,
    x_ref,
    raw_ref,
    cot_ref,
    q_ref,
    k_ref,
    v_ref,
    lse_ref,
    ctx_ref,
    ctxn_ref,
    all_ref,
    wqkv_ref,
    wo_ref,
    wi_ref,
    wd_ref,
    parts,
    back_parts,
    back_firsts,
    back_quarters,
    nh_ref,
    datt_ref,
    act_ref,
    du_ref,
    hid_ref,
    vec_ref,
    ext_ref,
    cot_own,
    cot_prev,
    cot_pad,
    lead_pad,
    wc_ref,
    pick_ref,
    spread_ref,
    pool_ref,
    win_part,
    win_first,
    win_second,
    fresh_ref,
    comp_ref,
    comp_total,
    landed,
    load_sem,
    save_sem,
    stage_sem,
    place_sem,
    move_send,
    move_recv,
    pass_send,
    pass_recv,
    ctx_send,
    ctx_recv,
    wo_send,
    wo_recv,
    edge_send,
    edge_recv,
    rs_send,
    rs_recv,
    ag_send,
    ag_recv,
    seq_send,
    seq_recv,
):
    me = Place()
    d = x_ref.shape[-1]
    heads = q_ref.shape[1]
    width = heads * HEAD
    low, high = me.low, me.high
    kinds = list(range(KINDS))
    edge_rows = mem_hbm.shape[1]

    load_pairs = [
        (mem_hbm, ext_ref.at[:, pl.ds(0, edge_rows)]),
        (cot_new, cot_own),
        (w_comp, wc_ref),
        (w_key, wqkv_ref.at[:, pl.ds(0, width)]),
        (w_value, wqkv_ref.at[:, pl.ds(width, width)]),
        (w_query, wqkv_ref.at[:, pl.ds(2 * width, width)]),
        (w_out, wo_ref.at[pl.ds(pl.multiple_of(me.tp * width, width), width)]),
        (w_in, wi_ref),
        (w_down, wd_ref),
    ]
    loads = [
        pltpu.make_async_copy(src, dst, load_sem.at[i]) for i, (src, dst) in enumerate(load_pairs)
    ]
    for load in loads:
        load.start()

    meet(
        me,
        [me.mate(), me.across(), me.corner(), me.after(), me.before()]
        + [me.flipped(b) for b in range(me.bits)],
    )

    sources = [rows_hbm[0], rows_hbm[1], rows_hbm[2], cot_hbm]

    def landing(kind, slot, chunk):
        if kind == KINDS:
            return cot_ref.at[slot, chunk, :, low]
        return raw_ref.at[slot, kind, chunk]

    def route(micro, q):
        segment = jnp.where(q < me.column, me.column - 1, me.column)
        home, slot = home_of(segment, micro)
        return home, slot, PER_DEV * me.column + q - PER_SEG * segment

    def send_out(kinds, wanted):
        @pl.loop(0, 2 * PER_DEV)
        def _(at):
            micro, q = lax.div(at, PER_DEV), lax.rem(at, PER_DEV)
            home, slot, chunk = route(micro, q)
            here = home == me.column
            for kind in kinds:
                src = sources[kind].at[micro, q, :, low]
                dst = landing(kind, slot, chunk)

                @pl.when(jnp.logical_and(slot == wanted, here))
                def _():
                    pltpu.make_async_copy(src, dst, place_sem.at[kind, slot, chunk]).start()

                @pl.when(jnp.logical_and(slot == wanted, jnp.logical_not(here)))
                def _():
                    remote(
                        src,
                        dst,
                        move_send.at[kind, micro, q],
                        move_recv.at[kind, slot, chunk],
                        me.beside(home - me.column),
                    ).start()

    def sent(kinds, micro):
        @pl.loop(0, PER_DEV)
        def _(q):
            home, slot, chunk = route(micro, q)
            for kind in kinds:

                @pl.when(home != me.column)
                def _():
                    remote(
                        sources[kind].at[micro, q, :, low],
                        landing(kind, slot, chunk),
                        move_send.at[kind, micro, q],
                        move_recv.at[kind, slot, chunk],
                        me.beside(home - me.column),
                    ).wait_send()

    spans = []
    for slot in range(2):
        segment, _, there = units_of(me.column, slot)
        first = jnp.maximum(PER_DEV * me.column - PER_SEG * segment, 0)
        last = jnp.minimum(PER_DEV * me.column + PER_DEV - PER_SEG * segment, PER_SEG)
        spans.append((jnp.where(there, first, 0), jnp.where(there, last, PER_SEG), there))

    def wait_own(kind, slot, chunk):
        dst = landing(kind, slot, chunk)
        pltpu.make_async_copy(dst, dst, place_sem.at[kind, slot, chunk]).wait()

    def wait_moved(kind, slot, chunk):
        dst = landing(kind, slot, chunk)
        remote(
            dst, dst, move_send.at[kind, 0, 0], move_recv.at[kind, slot, chunk], me.mate()
        ).wait_recv()

    def over_own(kinds, slot, body):
        first, last, there = spans[slot]

        @pl.loop(first, last)
        def _(chunk):
            @pl.when(there)
            def _():
                for kind in kinds:
                    wait_own(kind, slot, chunk)

            body(chunk)

    def over_moved(kinds, slot, body):
        first, last, _ = spans[slot]

        def step(chunk):
            for kind in kinds:
                wait_moved(kind, slot, chunk)
            body(chunk)

        pl.loop(0, first)(step)
        pl.loop(last, PER_SEG)(step)

    gain_0, shift_0 = gains[0:1], shifts[0:1]
    gain_1, shift_1 = gains[1:2], shifts[1:2]

    def passing(kind, slot):
        here = cot_ref.at[slot, :, :, low] if kind == KINDS else x_ref.at[slot, kind, :, :, low]
        return remote(
            here, here, pass_send.at[kind, slot], pass_recv.at[kind, slot], me.mate()
        )

    def norm_chunk(u):
        def body(k):
            for kind in range(KINDS):
                raw = raw_ref[u, kind, k].reshape(2 * PART, d).astype(F32)
                scaled, _ = center_of(raw)
                normed = (scaled * gain_0 + shift_0).astype(BF)
                x_ref[u, kind, k, :, low] = normed.reshape(2, PART, d)

        return body

    def norm_own(u):
        over_own(kinds, u, norm_chunk(u))

    def norm_moved(u):
        over_moved(kinds, u, norm_chunk(u))
        for kind in kinds:
            passing(kind, u).start()

    def cot_pass(u):
        over_own([KINDS], u, lambda k: None)
        over_moved([KINDS], u, lambda k: None)
        passing(KINDS, u).start()

    saves = []

    def save(src, dst):
        copy = pltpu.make_async_copy(src, dst, save_sem.at[len(saves)])
        copy.start()
        saves.append(copy)

    def project(u):
        for kind in range(KINDS):
            passing(kind, u).wait()
            normed = x_ref[u, kind].reshape(SEG, d)
            span = pl.ds(kind * SEG, SEG)
            keys = dot_plain(normed, wqkv_ref[:, :width]).astype(BF)
            values = dot_plain(normed, wqkv_ref[:, width : 2 * width]).astype(BF)
            for h in range(heads):
                cols = slice(h * HEAD, (h + 1) * HEAD)
                k_ref[u, h, span] = keys[:, cols]
                v_ref[u, h, span] = values[:, cols]
            if kind == 0:
                queries = dot_plain(normed, wqkv_ref[:, 2 * width :]).astype(BF)
                for h in range(heads):
                    q_ref[u, h] = queries[:, h * HEAD : (h + 1) * HEAD]
        save(x_ref.at[u], normed_hbm.at[u])

    segments = lax.div(me.seq, PER_SEG) * PER_DEV

    def attend(u, h):
        scale = HEAD ** (-0.5)
        slope = slopes[h]
        segment, micro, _ = units_of(me.column, u)
        segment = jnp.minimum(segment, PER_DEV - 1) + segments
        edge = boundary[micro, segment]
        linked = links[micro, segment]
        key_at = lax.broadcasted_iota(jnp.int32, (1, KINDS * SEG), 1)
        kind_at = lax.div(key_at, SEG)
        bias = (key_at - 2 * SEG * kind_at).astype(F32) * (slope / SEG)
        key_x = lax.broadcasted_iota(jnp.int32, (QUERY_BLOCK, SEG), 1)
        per = QUERY_BLOCK // CHUNK

        @pl.loop(0, SEG // QUERY_BLOCK)
        def _(b):
            rows = pl.ds(pl.multiple_of(b * QUERY_BLOCK, QUERY_BLOCK), QUERY_BLOCK)
            raw = dot_second_t(q_ref[u, h, rows], k_ref[u, h]) * scale + bias
            at = b * QUERY_BLOCK + lax.broadcasted_iota(jnp.int32, (QUERY_BLOCK, SEG), 0)
            seen = jnp.logical_and(key_x <= at, jnp.logical_or(key_x >= edge, at < edge))
            near = jnp.where(seen, raw[:, :SEG], -1e30)
            open_row = jnp.logical_and(at[:, :1] < edge, linked == 1)
            far = jnp.where(open_row, raw[:, SEG:], -1e30)
            top = jnp.maximum(
                jnp.max(near, axis=-1, keepdims=True), jnp.max(far, axis=-1, keepdims=True)
            )
            near = jnp.exp(near - top)
            far = jnp.exp(far - top)
            whole = jnp.sum(near, axis=-1, keepdims=True) + jnp.sum(far, axis=-1, keepdims=True)
            lse_ref[u, h, rows] = jnp.broadcast_to(top + jnp.log(whole), (QUERY_BLOCK, HEAD))
            share = 1.0 / whole
            near = near * share
            far = far * share
            near_low = near.astype(BF)
            far_low = far.astype(BF)
            value_x, value_far = v_ref[u, h, :SEG], v_ref[u, h, SEG:]
            context = dot_plain(near_low, value_x) + dot_plain(far_low, value_far)
            near_rest = (near - near_low.astype(F32)).astype(BF)
            far_rest = (far - far_low.astype(F32)).astype(BF)
            rest = dot_plain(near_rest, value_x) + dot_plain(far_rest, value_far)
            ctxn_ref[u, h, rows] = context + rest
            ctx_ref[u, pl.ds(b * per, per), :, :, :, h * HEAD : (h + 1) * HEAD] = (
                context.astype(BF).reshape(per, 2, 2, PART, HEAD)
            )

    def my_columns(tp):
        return pl.ds(pl.multiple_of(tp * width, width), width)

    def ctx_copies(u):
        dst = all_ref.at[u, :, :, :, my_columns(me.tp)]
        same, other = ctx_ref.at[u, :, :, low], ctx_ref.at[u, :, :, 1 - low]
        return [
            remote(src, dst, ctx_send.at[u, i], ctx_recv.at[u, i], device)
            for i, (src, device) in enumerate(
                [(same, me.across()), (other, me.corner()), (other, me.mate())]
            )
        ]

    def ctx_start(u):
        for copy in ctx_copies(u):
            copy.start()
        all_ref[u, :, :, :, my_columns(me.tp)] = ctx_ref[u, :, :, low]
        save(ctx_ref.at[u], ctx_hbm.at[u])
        save(ctxn_ref.at[u], ctxn_hbm.at[u])

    def wo_rows(tp):
        return wo_ref.at[pl.ds(pl.multiple_of(tp * width, width), width)]

    across_tp = me.tp + 2 - 4 * high
    mate_tp = me.tp + 1 - 2 * low
    wo_copies = [
        remote(w_out, wo_rows(me.tp), wo_send.at[0], wo_recv.at[0], me.across()),
        remote(w_out, wo_rows(me.tp), wo_send.at[1], wo_recv.at[1], me.mate()),
        remote(
            wo_rows(across_tp), wo_rows(across_tp), wo_send.at[2], wo_recv.at[2], me.mate()
        ),
    ]

    def half_pass(ref, u, kind):
        here = ref.at[u, :, :, low]
        return remote(here, here, pass_send.at[kind, u], pass_recv.at[kind, u], me.mate())

    def hidden_norm(u):
        for copy in ctx_copies(u):
            copy.wait()

        @pl.loop(0, 2)
        def _(r):
            some = pl.ds(r * (PER_SEG // 2), PER_SEG // 2)
            rows = SEG // 4
            hidden = dot_plain(all_ref[u, some].reshape(rows, 4 * width), wo_ref[...])
            hidden += raw_ref[u, 0, some].reshape(rows, d).astype(F32)
            hid_ref[u, some] = hidden.reshape(PER_SEG // 2, 2, PART, d)
            scaled, _ = center_of(hidden)
            normed = (scaled * gain_1 + shift_1).astype(BF)
            nh_ref[u, some, :, low] = normed.reshape(PER_SEG // 2, 2, PART, d)

        half_pass(nh_ref, u, KINDS + 1).start()
        save(hid_ref.at[u, :, high], hid_hbm.at[u])

    def store_part(part, cols, tile):
        part[:, :, :, :, cols] = tile.astype(part.dtype).reshape(
            PER_SEG, 2, 2, PART, tile.shape[1]
        )

    def ffn_up(u):
        ff = wi_ref.shape[1]

        @pl.loop(0, ff // 256)
        def _(n):
            cols = pl.ds(pl.multiple_of(n * 256, 256), 256)
            for r in range(2):
                chunks = slice(r * PER_SEG // 2, (r + 1) * PER_SEG // 2)
                rows = slice(r * SEG // 2, (r + 1) * SEG // 2)
                upper = dot_plain(nh_ref[u, chunks].reshape(SEG // 2, d), wi_ref[:, cols])
                d_act = dot_second_t(cot_ref[u, chunks].reshape(SEG // 2, d), wd_ref[cols])
                square = upper * upper
                inner = GELU_IN * upper * (1.0 + 0.044715 * square)
                bend = jnp.tanh(inner)
                grown = 0.5 * (1.0 + bend)
                act_ref[u, rows, cols] = (upper * grown).astype(BF)
                slope = grown + 0.5 * upper * (1.0 - bend * bend) * (
                    GELU_IN * (1.0 + 3.0 * 0.044715 * square)
                )
                du_ref[u, rows, cols] = (d_act * slope).astype(BF)

    def ffn_out(u, part):
        @pl.loop(0, d // 256)
        def _(n):
            cols = pl.ds(pl.multiple_of(n * 256, 256), 256)
            store_part(part, cols, dot_plain(act_ref[u], wd_ref[:, cols]))

    def ffn_back(u, part):
        @pl.loop(0, d // 256)
        def _(n):
            cols = pl.ds(pl.multiple_of(n * 256, 256), 256)
            store_part(part, cols, dot_second_t(du_ref[u], wi_ref[cols]))

    def hidden_back(u, task):
        task.end()

        @pl.loop(0, PER_SEG, step=4)
        def _(at):
            k = pl.ds(at, 4)
            scaled, inverse = center_of(hid_ref[u, k, high])
            grad = task.total(k)
            cot = cot_ref[u, k, high, low].astype(F32)
            d_hidden = cot + norm_back(grad, scaled, inverse, gain_1)
            vec_ref[0] += eights(grad * scaled)
            vec_ref[1] += eights(grad)
            task.second[k] = d_hidden
            datt_ref[u, k, high, low] = d_hidden.astype(BF)

        datts[u].start()
        save(task.second, dhid_hbm.at[u])

    staged = []

    def weight_grads(first, left, right):
        for n in range(d // 256):
            cols = slice(n * 256, (n + 1) * 256)
            slot = len(staged) % 2
            if len(staged) >= 2:
                for copy in staged[-2]:
                    copy.wait()
            tile = dot_first_t(left(0, cols), right(0)) + dot_first_t(left(1, cols), right(1))
            chunks = tile.shape[1] // 256
            rows = pl.ds(slot * 256, 256)
            pool_ref[rows, : tile.shape[1]] = tile.astype(BF)
            copies = [
                pltpu.make_async_copy(
                    pool_ref.at[rows, pl.ds(c * 256, 256)],
                    gffn_hbm.at[first + c, cols],
                    stage_sem.at[slot, c],
                )
                for c in range(chunks)
            ]
            for copy in copies:
                copy.start()
            staged.append(copies)

    slots = cot_new.shape[1]
    rows_here = edge_rows * PART
    edges = [
        remote(
            mem_hbm.at[:, pl.ds(0, REACH // PART)],
            ext_ref.at[:, pl.ds(edge_rows, REACH // PART)],
            edge_send.at[0],
            edge_recv.at[0],
            me.before(),
        ),
        remote(cot_new, cot_prev, edge_send.at[1], edge_recv.at[1], me.after()),
    ]
    seq = SeqReduce(me, comp_ref, comp_total, landed, (seq_send, seq_recv), [[0, 1, 2]])
    win = TpReduce(me, win_part, win_first, win_second, (rs_send, rs_recv), 0)

    def local_rows(at, tap, is_lead):
        slot = slots * me.column + at - jnp.where(is_lead, LEAD, 0)
        used = at < jnp.where(is_lead, LEAD, slots)
        slot_seg = lax.div(slot, CSEG)
        place = 3 * (slot - slot_seg * CSEG) + tap
        there = jnp.logical_and(used, jnp.logical_and(slot >= 0, place < SEG))
        return jnp.where(there, slot_seg * SEG + place - rows_here * me.column, -1)

    lead_rows = 32
    own_rows = 3 * SLOT_PAD
    ext_rows = rows_here + REACH
    feats = w_comp.shape[2]

    def compress_masks():
        row = lax.broadcasted_iota(jnp.int32, (own_rows, 1), 0)
        tap = lax.div(row, SLOT_PAD)
        local = local_rows(row - tap * SLOT_PAD, tap, False)
        where_at = lax.broadcasted_iota(jnp.int32, (own_rows, ext_rows), 1)
        pick_ref[...] = jnp.where(local == where_at, 1.0, 0.0).astype(BF)
        col = lax.broadcasted_iota(jnp.int32, (1, own_rows + 3 * lead_rows), 1)
        is_lead = col >= own_rows
        col = jnp.where(is_lead, col - own_rows, col)
        per = jnp.where(is_lead, lead_rows, SLOT_PAD)
        tap = jnp.where(is_lead, lax.div(col, lead_rows), lax.div(col, SLOT_PAD))
        local = local_rows(col - tap * per, tap, is_lead)
        where_at = lax.broadcasted_iota(jnp.int32, spread_ref.shape, 0)
        spread_ref[...] = jnp.where(local == where_at, 1.0, 0.0).astype(BF)
        cot_pad[...] = jnp.zeros(cot_pad.shape, BF)
        lead_pad[...] = jnp.zeros(lead_pad.shape, BF)

    def compress():
        for load in loads[:3]:
            load.wait()
        for copy in edges:
            copy.wait()
        grads = [None] * 3
        for m in range(2):
            cot_pad[m, :slots] = cot_own[m]
            lead_pad[m, :LEAD] = cot_prev[m, slots - LEAD :]
            cot, cot_lead = cot_pad[m], lead_pad[m]
            fresh = None
            taken = dot_plain(pick_ref[...], ext_ref[m].reshape(ext_rows, d)).astype(BF)
            for tap in range(3):
                span = slice(tap * SLOT_PAD, (tap + 1) * SLOT_PAD)
                lead = slice(own_rows + tap * lead_rows, own_rows + (tap + 1) * lead_rows)
                term = dot_plain(taken[span], wc_ref[tap])
                fresh = term if fresh is None else fresh + term
                term = dot_first_t(taken[span], cot)
                grads[tap] = term if grads[tap] is None else grads[tap] + term
                pool_ref[span, :d] = dot_second_t(cot, wc_ref[tap]).astype(BF)
                pool_ref[lead, :d] = dot_second_t(cot_lead, wc_ref[tap]).astype(BF)
            fresh_ref[m] = fresh[:slots]
            for n in range(2):
                cols = slice(n * d // 2, (n + 1) * d // 2)
                tile = dot_plain(spread_ref[...], pool_ref[:, cols])
                win_part[m * PER_DEV : (m + 1) * PER_DEV, :, :, :, cols] = (
                    tile.astype(BF).reshape(PER_DEV, 2, 2, PART, d // 2)
                )
        for tap in range(3):
            split_store(me, comp_ref, 0, tap * (feats // 256), grads[tap])
        save(fresh_ref, fresh_hbm)

    def win_end():
        win.end()

        @pl.loop(0, 2 * PER_DEV, step=2)
        def _(at):
            k = pl.ds(at, 2)
            win_second[k] = win.total(k).astype(BF)

        save(win_second, win_hbm)

    rs = (rs_send, rs_recv)
    backs = [
        TpReduce(me, back_parts[u], back_firsts[u], back_quarters[u], rs, 1 + u) for u in range(2)
    ]
    datts = [TpGather(me, datt_ref.at[u], (ag_send, ag_recv), u) for u in range(2)]

    send_out(kinds, 0)
    for copy in edges:
        copy.start()
    for copy in wo_copies[:2]:
        copy.start()
    vec_ref[...] = jnp.zeros(vec_ref.shape, F32)

    @pl.when(jnp.logical_not(spans[1][2]))
    def _():
        raw_ref[1] = jnp.zeros(raw_ref.shape[1:], BF)
        cot_ref[1, :, :, low] = jnp.zeros((PER_SEG, 2, PART, d), BF)

    compress_masks()
    norm_own(0)
    norm_moved(0)
    send_out(kinds, 1)
    for load in loads[3:6]:
        load.wait()
    project(0)
    attend(0, 0)
    wo_copies[0].wait()
    wo_copies[2].start()
    norm_own(1)
    attend(0, 1)
    ctx_start(0)
    compress()
    win.start()
    norm_moved(1)
    send_out([KINDS], 0)
    send_out([KINDS], 1)
    seq.launch(0)
    win.middle()
    project(1)
    save(q_ref, q_hbm)
    save(k_ref, k_hbm)
    save(v_ref, v_hbm)
    save(raw_ref.at[:, :, :, high], own_hbm)
    loads[6].wait()
    for copy in wo_copies[1:]:
        copy.wait()
    hidden_norm(0)
    attend(1, 0)
    cot_pass(0)
    attend(1, 1)
    win_end()
    save(lse_ref, lse_hbm)
    ctx_start(1)
    cot_pass(1)
    loads[7].wait()
    loads[8].wait()
    half_pass(nh_ref, 0, KINDS + 1).wait()
    passing(KINDS, 0).wait()
    ffn_up(0)
    ffn_back(0, back_parts[0])
    backs[0].start()
    hidden_norm(1)
    backs[0].middle()
    seq.turn()
    ffn_out(0, parts[0])
    save(parts[0], outp_hbm.at[0])
    half_pass(nh_ref, 1, KINDS + 1).wait()
    passing(KINDS, 1).wait()
    ffn_up(1)
    ffn_back(1, back_parts[1])
    backs[1].start()
    ffn_out(1, parts[1])
    save(parts[1], outp_hbm.at[1])
    seq.turn()
    backs[1].middle()
    hidden_back(0, backs[0])
    ff = wi_ref.shape[1]
    weight_grads(
        0, lambda u, cols: nh_ref[u, :, :, :, :, cols].reshape(SEG, 256), lambda u: du_ref[u]
    )
    weight_grads(
        ff // 256, lambda u, cols: cot_ref[u, :, :, :, :, cols].reshape(SEG, 256), lambda u: act_ref[u]
    )
    seq.drain()
    save(comp_total, comp_hbm)
    hidden_back(1, backs[1])
    save(vec_ref, vec_hbm)
    datts[0].middle()
    datts[1].middle()
    datts[0].end()
    save(datt_ref.at[0], datt_hbm.at[0])
    datts[1].end()
    save(datt_ref.at[1], datt_hbm.at[1])
    for micro in range(2):
        sent(kinds + [KINDS], micro)
    for copies in staged[-2:]:
        for copy in copies:
            copy.wait()
    for copy in saves:
        copy.wait()


def forward_call(rows, cot, memory, cot_new, w_comp, boundary, links, slopes, gains, shifts, weights):
    count = lax.axis_size("seq")
    bits = count.bit_length() - 1
    d = cot.shape[-1]
    heads = weights[0].shape[1] // HEAD
    width = heads * HEAD
    ff = weights[4].shape[1]
    slots, feats = cot_new.shape[1:]
    split = (PER_SEG, 2, 2, PART, d)
    half = (PER_SEG, 2, PART, d)
    own = (PER_SEG, PART, d)
    keys = KINDS * SEG
    owned = 2 * PER_DEV
    shard = d // count
    any_space = pl.BlockSpec(memory_space=pl.ANY)
    smem = pl.BlockSpec(memory_space=pltpu.SMEM)
    vmem = pl.BlockSpec(memory_space=pltpu.VMEM)
    shapes = [
        ((2, KINDS) + split, BF),
        ((2, KINDS) + own, BF),
        ((2, heads, SEG, HEAD), BF),
        ((2, heads, keys, HEAD), BF),
        ((2, heads, keys, HEAD), BF),
        ((2, heads, SEG, HEAD), F32),
        ((2, PER_SEG, 2, 2, PART, width), BF),
        ((2, heads, SEG, HEAD), F32),
        ((2,) + split, BF),
        ((2,) + own, F32),
        ((2,) + own, F32),
        ((2,) + split, BF),
        ((2 * ff // 256, d, 256), BF),
        ((2, 8, d), F32),
        ((owned, PART, d), BF),
        ((2, slots, feats), F32),
        ((shard, 3 * feats), F32),
    ]
    dma = pltpu.SemaphoreType.DMA
    total_rows = 3 * (SLOT_PAD + 32)
    ext_rows = memory.shape[1] + REACH // PART
    scratch = [
        pltpu.VMEM((2, KINDS) + split, BF),
        pltpu.VMEM((2, KINDS) + half, BF),
        pltpu.VMEM((2,) + split, BF),
        pltpu.VMEM((2, heads, SEG, HEAD), BF),
        pltpu.VMEM((2, heads, keys, HEAD), BF),
        pltpu.VMEM((2, heads, keys, HEAD), BF),
        pltpu.VMEM((2, heads, SEG, HEAD), F32),
        pltpu.VMEM((2, PER_SEG, 2, 2, PART, width), BF),
        pltpu.VMEM((2, heads, SEG, HEAD), F32),
        pltpu.VMEM((2, PER_SEG, 2, PART, 4 * width), BF),
        pltpu.VMEM((d, 3 * width), BF),
        pltpu.VMEM((4 * width, d), BF),
        pltpu.VMEM((d, ff), BF),
        pltpu.VMEM((ff, d), BF),
        [pltpu.VMEM(split, BF) for _ in range(2)],
        [pltpu.VMEM(split, F32) for _ in range(2)],
        [pltpu.VMEM(half, F32) for _ in range(2)],
        [pltpu.VMEM(own, F32) for _ in range(2)],
        pltpu.VMEM((2,) + split, BF),
        pltpu.VMEM((2,) + split, BF),
        pltpu.VMEM((2, SEG, ff), BF),
        pltpu.VMEM((2, SEG, ff), BF),
        pltpu.VMEM((2,) + half, F32),
        pltpu.VMEM((2, 8, d), F32),
        pltpu.VMEM((2, ext_rows, PART, d), BF),
        pltpu.VMEM((2, slots, feats), BF),
        pltpu.VMEM((2, slots, feats), BF),
        pltpu.VMEM((2, SLOT_PAD, feats), BF),
        pltpu.VMEM((2, 32, feats), BF),
        pltpu.VMEM((3, d, feats), BF),
        pltpu.VMEM((3 * SLOT_PAD, ext_rows * PART), BF),
        pltpu.VMEM((memory.shape[1] * PART, total_rows), BF),
        pltpu.VMEM((total_rows, max(d, ff)), BF),
        pltpu.VMEM((owned, 2, 2, PART, d), BF),
        pltpu.VMEM((owned, 2, PART, d), BF),
        pltpu.VMEM((owned, PART, d), BF),
        pltpu.VMEM((2, slots, feats), F32),
        pltpu.VMEM((3 * feats // 256,) + (2,) * bits + (shard, 256), BF),
        pltpu.VMEM((shard, 3 * feats), F32),
        [
            pltpu.VMEM((3 * feats // 256,) + (2,) * (bits - 1 - i) + (shard, 256), BF)
            for i in range(bits)
        ],
        dma((9,)),
        dma((24,)),
        dma((2, ff // 256)),
        dma((KINDS + 1, 2, PER_SEG)),
        dma((KINDS + 1, 2, PER_DEV)),
        dma((KINDS + 1, 2, PER_SEG)),
        dma((KINDS + 3, 2)),
        dma((KINDS + 3, 2)),
        dma((2, 3)),
        dma((2, 3)),
        dma((3,)),
        dma((3,)),
        dma((2,)),
        dma((2,)),
        dma((3, 2)),
        dma((3, 2)),
        dma((2, 2)),
        dma((2, 2)),
        dma((bits, 3)),
        dma((bits, 3)),
    ]
    return pl.pallas_call(
        forward_kernel,
        out_shape=[jax.ShapeDtypeStruct(shape, kind) for shape, kind in shapes],
        in_specs=[[any_space] * KINDS]
        + [any_space] * 4
        + [smem] * 3
        + [vmem] * 2
        + [any_space] * 6,
        out_specs=[any_space] * len(shapes),
        scratch_shapes=scratch,
        compiler_params=pltpu.CompilerParams(
            collective_id=1, has_side_effects=True, vmem_limit_bytes=63 << 20
        ),
    )(rows, cot, memory, cot_new, w_comp, boundary, links, slopes, gains, shifts, *weights)


FINALS = 4


def backward_kernel(
    normed_hbm,
    own_hbm,
    q_hbm,
    k_hbm,
    v_hbm,
    lse_hbm,
    ctx_hbm,
    ctxn_hbm,
    outp_hbm,
    hid_hbm,
    dhid_hbm,
    datt_hbm,
    gffn_hbm,
    win_hbm,
    vec_in,
    boundary,
    links,
    slopes,
    gains,
    w_query,
    w_key,
    w_value,
    w_out,
    finals,
    total_hbm,
    small_hbm,
    normed_ref,
    own_ref,
    q_ref,
    kx_ref,
    v_ref,
    lse_ref,
    ctx_ref,
    ctxn_ref,
    dhid_ref,
    datt_ref,
    wqkv_ref,
    wo_ref,
    dctx_ref,
    ds_ref,
    prob_ref,
    dq_ref,
    dqkv_ref,
    parts,
    firsts,
    seconds,
    out_parts,
    hid_ref,
    out_ref,
    win_ref,
    home_ref,
    owner_ref,
    grads_ref,
    total_ref,
    landed,
    vec_ref,
    aux_ref,
    small_ref,
    small_came,
    load_sem,
    save_sem,
    rs_send,
    rs_recv,
    ag_send,
    ag_recv,
    ag_here,
    move_send,
    move_recv,
    seq_send,
    seq_recv,
    small_send,
    small_recv,
):
    me = Place()
    d = normed_ref.shape[-1]
    heads = q_ref.shape[1]
    width = heads * HEAD
    late = gffn_hbm.shape[0]
    heads_wide = width // 256

    load_pairs = {
        "gffn": (gffn_hbm, grads_ref.at[pl.ds(0, late)]),
        "outp0": (outp_hbm.at[0], out_parts[0]),
        "outp1": (outp_hbm.at[1], out_parts[1]),
        "datt": (datt_hbm, datt_ref),
        "wo": (w_out, wo_ref),
        "v": (v_hbm, v_ref),
        "ctxn": (ctxn_hbm, ctxn_ref),
        "lse": (lse_hbm, lse_ref),
        "k": (k_hbm, kx_ref.at[:, :, :, pl.ds(0, HEAD)]),
        "q": (q_hbm, q_ref),
        "wk": (w_key, wqkv_ref.at[:, pl.ds(0, width)]),
        "wv": (w_value, wqkv_ref.at[:, pl.ds(width, width)]),
        "wq": (w_query, wqkv_ref.at[:, pl.ds(2 * width, width)]),
        "hid": (hid_hbm, hid_ref),
        "own": (own_hbm, own_ref),
        "dhid": (dhid_hbm, dhid_ref),
        "win": (win_hbm, win_ref),
        "vec": (vec_in, vec_ref.at[pl.ds(2, 2)]),
        "normed": (normed_hbm, normed_ref),
        "ctx": (ctx_hbm, ctx_ref),
    }
    loads = {
        name: pltpu.make_async_copy(src, dst, load_sem.at[i])
        for i, (name, (src, dst)) in enumerate(load_pairs.items())
    }
    for load in loads.values():
        load.start()

    def ready(*names):
        for name in names:
            loads[name].wait()

    meet(
        me,
        [me.mate(), me.across(), me.after(), me.before()]
        + [me.flipped(b) for b in range(me.bits)],
    )

    gain_0 = gains[0:1]
    vec_ref[:2] = jnp.zeros((2,) + vec_ref.shape[1:], F32)
    aux_ref[...] = jnp.zeros(aux_ref.shape, F32)
    key_at = lax.broadcasted_iota(jnp.int32, (KINDS * SEG, HEAD), 0)
    lane = lax.broadcasted_iota(jnp.int32, (KINDS * SEG, HEAD), 1)
    kind_at = lax.div(key_at, SEG)
    in_kind = key_at - SEG * kind_at
    odd = lax.rem(in_kind, 2)
    marks = jnp.where(
        lane == 0,
        in_kind - odd,
        jnp.where(lane == 1, odd, jnp.where(lane == 2, kind_at, jnp.where(lane == 3, 1, 0))),
    )
    marks = marks.astype(F32).astype(BF)
    for u in range(2):
        for h in range(heads):
            kx_ref[u, h, :, HEAD:] = marks

    rs = (rs_send, rs_recv)
    sems = (seq_send, seq_recv)
    chunks = grads_ref.shape[0]
    n = chunks - 8

    def reducer(groups):
        return SeqReduce(me, grads_ref, total_ref, landed, sems, groups)

    seq = reducer([[i] for i in range(n)] + [[n, n + 1]])
    mid = reducer([[n + 2, n + 3, n + 4]])
    tail = reducer([[n + 5, n + 6, n + 7]])


    def to_owner(kind, slot):
        segment, micro, there = units_of(me.column, slot)

        @pl.loop(0, PER_SEG)
        def _(chunk):
            place = PER_SEG * segment + chunk
            holder = lax.div(place, PER_DEV)
            q = lax.rem(place, PER_DEV)
            src = out_ref.at[slot, chunk] if kind == KINDS else home_ref.at[kind, slot, chunk]
            dst = owner_ref.at[kind, micro, q]

            @pl.when(jnp.logical_and(there, holder == me.column))
            def _():
                pltpu.make_async_copy(src, dst, move_recv.at[kind, micro, q]).start()

            @pl.when(jnp.logical_and(there, holder != me.column))
            def _():
                remote(
                    src,
                    dst,
                    move_send.at[kind, slot, chunk],
                    move_recv.at[kind, micro, q],
                    me.beside(holder - me.column),
                ).start()

    def sent(kind, slot):
        segment, micro, there = units_of(me.column, slot)

        @pl.loop(0, PER_SEG)
        def _(chunk):
            holder = lax.div(PER_SEG * segment + chunk, PER_DEV)

            @pl.when(jnp.logical_and(there, holder != me.column))
            def _():
                src = home_ref.at[0, slot, chunk]
                remote(
                    src,
                    src,
                    move_send.at[kind, slot, chunk],
                    move_recv.at[kind, 0, 0],
                    me.mate(),
                ).wait_send()

    def collect(kind, micro):
        @pl.loop(0, PER_DEV)
        def _(q):
            segment = jnp.where(q < me.column, me.column - 1, me.column)
            home, slot = home_of(segment, micro)
            dst = owner_ref.at[kind, micro, q]

            @pl.when(home == me.column)
            def _():
                pltpu.make_async_copy(dst, dst, move_recv.at[kind, micro, q]).wait()

            @pl.when(home != me.column)
            def _():
                remote(
                    dst,
                    dst,
                    move_send.at[kind, 0, 0],
                    move_recv.at[kind, micro, q],
                    me.mate(),
                ).wait_recv()

    class Final:
        def __init__(self, kind, micro):
            self.own = owner_ref.at[kind, micro]
            whole = finals[kind].at[micro]
            self.mine = whole.at[:, me.high, me.low]
            self.here = pltpu.make_async_copy(self.own, self.mine, ag_here.at[kind, micro])
            self.one = remote(
                self.own,
                self.mine,
                ag_send.at[kind, micro, 0],
                ag_recv.at[kind, micro, 0],
                me.across(),
            )
            both = whole.at[:, :, me.low]
            self.two = remote(
                both, both, ag_send.at[kind, micro, 1], ag_recv.at[kind, micro, 1], me.mate()
            )

        def start(self):
            self.here.start()
            self.one.start()

        def middle(self):
            self.here.wait()
            self.one.wait()
            self.two.start()

        def end(self):
            self.two.wait()

    def context_back(u):
        datt = datt_ref[u].reshape(SEG, d)
        for h in range(heads):
            rows = slice(h * HEAD, (h + 1) * HEAD)
            dctx_ref[u, h] = dot_second_t(datt, wo_ref[rows]).astype(BF)

    segments = lax.div(me.seq, PER_SEG) * PER_DEV

    def attend_back(u, h, kind):
        scale = HEAD ** (-0.5)
        rows_at_once = 2 * QUERY_BLOCK
        keys = slice(kind * SEG, (kind + 1) * SEG)
        segment, micro, _ = units_of(me.column, u)
        segment = jnp.minimum(segment, PER_DEV - 1) + segments
        edge = boundary[micro, segment]
        linked = links[micro, segment]
        key_x = lax.broadcasted_iota(jnp.int32, (1, SEG), 1)
        bias = (key_x - SEG * kind).astype(F32) * (slopes[h] / SEG)

        @pl.loop(0, SEG // rows_at_once)
        def _(b):
            rows = pl.ds(pl.multiple_of(b * rows_at_once, rows_at_once), rows_at_once)
            scores = dot_second_t(q_ref[u, h, rows], kx_ref[u, h, keys, :HEAD]) * scale + bias
            at = b * rows_at_once + lax.broadcasted_iota(jnp.int32, (rows_at_once, 1), 0)
            if kind == 0:
                seen = jnp.logical_and(key_x <= at, jnp.logical_or(key_x >= edge, at < edge))
            else:
                seen = jnp.logical_and(at < edge, linked == 1)
            prob = jnp.exp(jnp.where(seen, scores - lse_ref[u, h, rows, :1], -1e30))
            prob_ref[rows] = prob.astype(BF)
            d_ctx = dctx_ref[u, h, rows]
            d_prob = dot_second_t(d_ctx, v_ref[u, h, keys])
            mean = jnp.sum(d_ctx.astype(F32) * ctxn_ref[u, h, rows], axis=-1, keepdims=True)
            d_scores = (prob * (d_prob - mean)).astype(BF)
            ds_ref[rows] = d_scores
            both = dot_plain(d_scores, kx_ref[u, h, keys])
            if kind < KINDS - 1:
                both += dq_ref[h, rows]
            if kind > 0:
                dq_ref[h, rows] = both
            else:
                cols = slice(2 * width + h * HEAD, 2 * width + (h + 1) * HEAD)
                dqkv_ref[u, 0, rows, cols] = (both[:, :HEAD] * scale).astype(BF)
                marked = both[:, HEAD:]
                at = b * rows_at_once + lax.broadcasted_iota(jnp.int32, marked.shape, 0)
                aux_ref[h, 0:1] += jnp.sum(marked, axis=0, keepdims=True)
                aux_ref[h, 1:2] += jnp.sum(marked * at.astype(F32), axis=0, keepdims=True)

        d_key = dot_first_t(ds_ref[...], q_ref[u, h]) * scale
        d_value = dot_first_t(prob_ref[...], dctx_ref[u, h])
        dqkv_ref[u, kind, :, h * HEAD : (h + 1) * HEAD] = d_key.astype(BF)
        dqkv_ref[u, kind, :, width + h * HEAD : width + (h + 1) * HEAD] = d_value.astype(BF)

    def project_back(u, kind, part):
        depth = (3 if kind == 0 else 2) * width

        @pl.loop(0, d // 256)
        def _(n):
            cols = pl.ds(pl.multiple_of(n * 256, 256), 256)
            tile = dot_second_t(dqkv_ref[u, kind, :, :depth], wqkv_ref[cols, :depth])
            part[:, :, :, :, cols] = tile.astype(BF).reshape(PER_SEG, 2, 2, PART, 256)

    def norm_end(u, kind, task):
        task.end()

        @pl.loop(0, PER_SEG, step=4)
        def _(at):
            k = pl.ds(at, 4)
            scaled, inverse = center_of(own_ref[u, kind, k].astype(F32))
            grad = task.total(k)
            vec_ref[0] += eights(grad * scaled)
            vec_ref[1] += eights(grad)
            result = norm_back(grad, scaled, inverse, gain_0)
            if kind == 0:
                result += dhid_ref[u, k]
            home_ref[kind, u, k] = result.astype(BF)

    def add_window(micro):
        @pl.loop(0, PER_DEV)
        def _(q):
            added = owner_ref[1, micro, q].astype(F32) + win_ref[micro * PER_DEV + q].astype(F32)
            owner_ref[1, micro, q] = added.astype(BF)

    def late_kv():
        for n in range(d // 256):
            cols = slice(n * 256, (n + 1) * 256)
            kv = None
            for u in range(2):
                for kind in range(KINDS):
                    left = normed_ref[u, kind, :, :, :, :, cols].reshape(SEG, 256)
                    term = dot_first_t(left, dqkv_ref[u, kind, :, : 2 * width])
                    kv = term if kv is None else kv + term
            split_store(me, grads_ref, n * 256, late + heads_wide, kv)

    def late_query():
        for n in range(d // 256):
            cols = slice(n * 256, (n + 1) * 256)
            query = None
            for u in range(2):
                left = normed_ref[u, 0, :, :, :, :, cols].reshape(SEG, 256)
                term = dot_first_t(left, dqkv_ref[u, 0, :, 2 * width :])
                query = term if query is None else query + term
            split_store(me, grads_ref, n * 256, late + 3 * heads_wide, query)

    def out_grad():
        for n in range(d // 256):
            cols = slice(n * 256, (n + 1) * 256)
            out = None
            for u in range(2):
                left = datt_ref[u, :, :, :, :, cols].reshape(SEG, 256)
                term = dot_first_t(left, ctx_ref[u].reshape(SEG, width))
                out = term if out is None else out + term
            split_store(me, grads_ref, n * 256, late, out)

    friends = [me.mate(), me.across()] + [me.flipped(b) for b in range(me.bits)]

    def small_copy(i):
        return remote(
            small_ref, small_came.at[i], small_send.at[i], small_recv.at[i], friends[i]
        )

    def small_start():
        lane = lax.broadcasted_iota(jnp.int32, (1, HEAD), 1)
        plain = jnp.where(lane < 2, 1.0, jnp.where(lane == 2, -float(SEG), 0.0))
        placed = jnp.where(lane == 3, 1.0, 0.0)
        small_ref[...] = jnp.zeros(small_ref.shape, F32)
        for i, at in enumerate((0, 2, 1, 3)):
            small_ref[i : i + 1] = jnp.sum(vec_ref[at], axis=0, keepdims=True)
        row = jnp.zeros((1, HEAD), F32)
        for h in range(heads):
            marked = aux_ref[h, 0:1] * plain - aux_ref[h, 1:2] * placed
            total = jnp.sum(marked, axis=-1, keepdims=True) / SEG
            row += jnp.where(lane == me.tp * heads + h, total, 0.0)
        small_ref[4:5, :HEAD] = row
        small_copy(0).start()

    def small_step(i):
        small_copy(i).wait()
        small_ref[...] += small_came[i]
        if i + 1 < len(friends):
            small_copy(i + 1).start()

    results = {}

    def final_start(kind, micro):
        collect(kind, micro)
        if kind == 1:
            add_window(micro)
        results[kind, micro] = Final(kind, micro)
        results[kind, micro].start()

    tasks = {
        (u, kind): TpReduce(
            me, parts[kind], firsts[u * KINDS + kind], seconds[u * KINDS + kind], rs, u * KINDS + kind
        )
        for u in range(2)
        for kind in range(KINDS)
    }

    def attend_kind(u, kind):
        for h in range(heads):
            attend_back(u, h, kind)

    def send_kind(u, kind):
        project_back(u, kind, parts[kind])
        tasks[u, kind].start()

    def end_kind(u, kind):
        norm_end(u, kind, tasks[u, kind])
        to_owner(kind, u)

    outs = [
        TpReduce(
            me, out_parts[u], firsts[2 * KINDS + u], seconds[2 * KINDS + u], rs, 2 * KINDS + u
        )
        for u in range(2)
    ]

    def out_end(u):
        outs[u].end()

        @pl.loop(0, PER_SEG, step=4)
        def _(at):
            k = pl.ds(at, 4)
            out_ref[u, k] = (hid_ref[u, k] + outs[u].total(k)).astype(BF)

        to_owner(KINDS, u)

    ready("outp0", "outp1")
    for u in range(2):
        outs[u].start()
    ready("gffn")
    for group in range(3):
        seq.launch(group)
    ready("datt", "wo")
    context_back(0)
    ready("v", "ctxn", "lse", "k", "q")
    for u in range(2):
        outs[u].middle()
    attend_kind(0, 2)
    ready("wk", "wv", "wq")
    send_kind(0, 2)
    seq.turn()
    seq.launch(3)
    attend_kind(0, 1)
    tasks[0, 2].middle()
    send_kind(0, 1)
    seq.turn()
    seq.launch(4)
    attend_kind(0, 0)
    tasks[0, 1].middle()
    send_kind(0, 0)
    ready("hid")
    out_end(0)
    out_end(1)
    seq.turn()
    context_back(1)
    ready("ctx")
    out_grad()
    mid.launch(0)
    tasks[0, 0].middle()
    ready("own", "dhid", "win", "vec")
    attend_kind(1, 2)
    end_kind(0, 2)
    send_kind(1, 2)
    seq.turn()
    final_start(KINDS, 0)
    final_start(KINDS, 1)
    attend_kind(1, 1)
    end_kind(0, 1)
    tasks[1, 2].middle()
    send_kind(1, 1)
    seq.turn()
    attend_kind(1, 0)
    end_kind(0, 0)
    tasks[1, 1].middle()
    send_kind(1, 0)
    mid.turn()
    seq.turn()
    final_start(2, 0)
    ready("normed")
    late_kv()
    tasks[1, 0].middle()
    late_query()
    tail.launch(0)
    results[KINDS, 0].middle()
    results[KINDS, 1].middle()
    final_start(1, 0)
    mid.turn()
    seq.turn()
    end_kind(1, 2)
    final_start(0, 0)
    end_kind(1, 1)
    results[2, 0].middle()
    mid.turn()
    end_kind(1, 0)
    small_start()
    tail.turn()
    final_start(2, 1)
    small_step(0)
    results[1, 0].middle()
    final_start(1, 1)
    results[0, 0].middle()
    tail.turn()
    final_start(0, 1)
    small_step(1)
    results[2, 1].middle()
    tail.turn()
    for i in range(2, len(friends)):
        small_step(i)
    results[1, 1].middle()
    seq.drain()
    mid.drain()
    tail.drain()
    results[0, 1].middle()
    saves = [
        pltpu.make_async_copy(total_ref, total_hbm, save_sem.at[0]),
        pltpu.make_async_copy(small_ref, small_hbm, save_sem.at[1]),
    ]
    for save in saves:
        save.start()
    for kind in range(FINALS):
        for at in range(2):
            results[kind, at].end()
            sent(kind, at)
    for save in saves:
        save.wait()


def backward_call(saved, boundary, links, slopes, gains, weights):
    normed, own, q, k, v, lse, ctx, ctxn, outp, hid, dhid, datt, gffn, vec, win = saved
    count = lax.axis_size("seq")
    bits = count.bit_length() - 1
    d = normed.shape[-1]
    heads = q.shape[1]
    keys = KINDS * SEG
    width = heads * HEAD
    chunks = gffn.shape[0] + 4 * width // 256
    columns = 256 * chunks
    view = (2,) * bits + (d // count, 256)
    split = (PER_SEG, 2, 2, PART, d)
    any_space = pl.BlockSpec(memory_space=pl.ANY)
    vmem = pl.BlockSpec(memory_space=pltpu.VMEM)
    smem = pl.BlockSpec(memory_space=pltpu.SMEM)
    dma = pltpu.SemaphoreType.DMA
    final = jax.ShapeDtypeStruct((2, PER_DEV, 2, 2, PART, d), BF)
    scratch = [
        pltpu.VMEM(normed.shape, BF),
        pltpu.VMEM(own.shape, BF),
        pltpu.VMEM(q.shape, BF),
        pltpu.VMEM((2, heads, keys, 2 * HEAD), BF),
        pltpu.VMEM(v.shape, BF),
        pltpu.VMEM(lse.shape, F32),
        pltpu.VMEM(ctx.shape, BF),
        pltpu.VMEM(ctxn.shape, F32),
        pltpu.VMEM(dhid.shape, F32),
        pltpu.VMEM(datt.shape, BF),
        pltpu.VMEM((d, 3 * width), BF),
        pltpu.VMEM((width, d), BF),
        pltpu.VMEM((2, heads, SEG, HEAD), BF),
        pltpu.VMEM((SEG, SEG), BF),
        pltpu.VMEM((SEG, SEG), BF),
        pltpu.VMEM((heads, SEG, 2 * HEAD), F32),
        pltpu.VMEM((2, KINDS, SEG, 3 * width), BF),
        [pltpu.VMEM(split, BF) for _ in range(KINDS)],
        [pltpu.VMEM((PER_SEG, 2, PART, d), BF) for _ in range(2 * KINDS + 2)],
        [pltpu.VMEM((PER_SEG, PART, d), BF) for _ in range(2 * KINDS + 2)],
        [pltpu.VMEM(split, BF) for _ in range(2)],
        pltpu.VMEM(hid.shape, F32),
        pltpu.VMEM(hid.shape, BF),
        pltpu.VMEM(win.shape, BF),
        pltpu.VMEM((KINDS, 2, PER_SEG, PART, d), BF),
        pltpu.VMEM((FINALS, 2, PER_DEV, PART, d), BF),
        pltpu.VMEM((chunks,) + view, BF),
        pltpu.VMEM((d // count, columns), F32),
        [pltpu.VMEM((chunks,) + view[i + 1 :], BF) for i in range(bits)],
        pltpu.VMEM((4, 8, d), F32),
        pltpu.VMEM((heads, 8, HEAD), F32),
        pltpu.VMEM((8, d), F32),
        pltpu.VMEM((bits + 2, 8, d), F32),
        dma((20,)),
        dma((2,)),
        dma((2 * KINDS + 2, 2)),
        dma((2 * KINDS + 2, 2)),
        dma((FINALS, 2, 2)),
        dma((FINALS, 2, 2)),
        dma((FINALS, 2)),
        dma((FINALS, 2, PER_SEG)),
        dma((FINALS, 2, PER_DEV)),
        dma((bits, chunks)),
        dma((bits, chunks)),
        dma((bits + 2,)),
        dma((bits + 2,)),
    ]
    return pl.pallas_call(
        backward_kernel,
        out_shape=[
            [final] * FINALS,
            jax.ShapeDtypeStruct((d // count, columns), F32),
            jax.ShapeDtypeStruct((8, d), F32),
        ],
        in_specs=[any_space] * 15 + [smem] * 3 + [vmem] + [any_space] * 4,
        out_specs=[[any_space] * FINALS] + [any_space] * 2,
        scratch_shapes=scratch,
        compiler_params=pltpu.CompilerParams(
            collective_id=2, has_side_effects=True, vmem_limit_bytes=63 << 20
        ),
    )(
        normed,
        own,
        q,
        k,
        v,
        lse,
        ctx,
        ctxn,
        outp,
        hid,
        dhid,
        datt,
        gffn.reshape((gffn.shape[0],) + view),
        win,
        vec,
        boundary,
        links,
        slopes,
        gains,
        *weights,
    )


def per_device(
    inputs,
    memory,
    compressed,
    boundary,
    links,
    gains,
    shifts,
    slopes,
    w_query,
    w_key,
    w_value,
    w_out,
    w_in,
    w_down,
    w_comp,
    cot_out,
    cot_new,
):
    d = inputs.shape[-1]
    rows = inputs.shape[1]
    heads = slopes.shape[0]
    width = heads * HEAD
    ff = w_in.shape[1]
    feats = w_comp.shape[2]
    count = lax.axis_size("seq")
    seq = lax.axis_index("seq")
    tp = lax.axis_index("tp")

    def chunked(array):
        return array.reshape(2, PER_DEV, 2, 2, PART, d)

    *saved, fresh, comp = forward_call(
        [chunked(inputs), chunked(memory), chunked(compressed)],
        chunked(cot_out),
        memory.reshape(2, rows // PART, PART, d),
        cot_new,
        w_comp,
        boundary,
        links,
        slopes,
        gains,
        shifts,
        (w_query, w_key, w_value, w_out, w_in, w_down),
    )
    finals, total, small = backward_call(
        saved, boundary, links, slopes, gains, (w_query, w_key, w_value, w_out)
    )
    vectors = lax.dynamic_slice(small, (0, seq * (d // count)), (4, d // count))
    grad_slopes = lax.dynamic_slice(small, (4, tp * heads), (1, heads))[0]

    def whole(array):
        return array.reshape(2, rows, d)

    pieces, at = [], 0
    for cut in [ff, ff] + [width] * 4:
        pieces.append(total[:, at : at + cut])
        at += cut
    g_in, g_down, g_out, g_key, g_value, g_query = pieces
    return (
        whole(finals[3]),
        whole(finals[0]).astype(F32),
        whole(finals[1]).astype(F32),
        whole(finals[2]).astype(F32),
        fresh,
        vectors[:2],
        vectors[2:],
        grad_slopes,
        g_query,
        g_key,
        g_value,
        g_out.T,
        g_in,
        g_down.T,
        jnp.stack([comp[:, i * feats : (i + 1) * feats] for i in range(3)]),
    )


def solution(mesh):
    in_specs = (
        P(None, "seq", None),
        P(None, "seq", None),
        P(None, "seq", None),
        P(),
        P(),
        P(),
        P(),
        P("tp"),
        P(None, "tp"),
        P(None, "tp"),
        P(None, "tp"),
        P("tp", None),
        P(None, "tp"),
        P("tp", None),
        P(None, None, "tp"),
        P(None, "seq", None),
        P(None, "seq", "tp"),
    )
    out_specs = (
        P(None, "seq", None),
        P(None, "seq", None),
        P(None, "seq", None),
        P(None, "seq", None),
        P(None, "seq", "tp"),
        P(None, "seq"),
        P(None, "seq"),
        P("tp"),
        P("seq", "tp"),
        P("seq", "tp"),
        P("seq", "tp"),
        P("tp", "seq"),
        P("seq", "tp"),
        P("tp", "seq"),
        P(None, "seq", "tp"),
    )
    return jax.shard_map(
        per_device, mesh=mesh, in_specs=in_specs, out_specs=out_specs, check_vma=False
    )
```

```python
import functools
import math

import jax
import jax.numpy as jnp
from jax import lax
from jax.experimental import pallas as pl
from jax.experimental.pallas import tpu as pltpu
from jax.sharding import PartitionSpec as P

HEAD = 128
SEG = 512
CSEG = 176
REACH = 32
LEAD = 26
SLOT_PAD = 160
CHUNK = 64
PART = 16
KINDS = 3
NORM_EPS = 1e-05
MESH = pl.DeviceIdType.MESH
BF = jnp.bfloat16
F32 = jnp.float32
GELU_IN = math.sqrt(2.0 / math.pi)
PER_SEG = SEG // CHUNK
PER_DEV = PER_SEG - 1
QUERY_BLOCK = 128


def dot_plain(a, b):
    return jnp.dot(a, b, preferred_element_type=F32)


def dot_first_t(a, b):
    return lax.dot_general(a, b, (((0,), (0,)), ((), ())), preferred_element_type=F32)


def dot_second_t(a, b):
    return lax.dot_general(a, b, (((1,), (1,)), ((), ())), preferred_element_type=F32)


def home_of(segment, micro):
    middle = PER_DEV // 2
    home = jnp.where(
        segment < middle, segment, jnp.where(segment == middle, middle + micro, segment + 1)
    )
    slot = jnp.where(segment == middle, 0, micro)
    return home, slot


def units_of(place, slot):
    middle = PER_DEV // 2
    segment = jnp.where(place <= middle, place, place - 1)
    is_middle = segment == middle
    micro = jnp.where(is_middle, place - middle, slot)
    return segment, micro, jnp.logical_or(jnp.logical_not(is_middle), slot == 0)


class Place:
    def __init__(self):
        self.seq = lax.axis_index("seq")
        self.tp = lax.axis_index("tp")
        self.column = lax.rem(self.seq, PER_SEG)
        self.low = lax.rem(self.tp, 2)
        self.high = lax.div(self.tp, 2)
        self.count = lax.axis_size("seq")
        self.bits = self.count.bit_length() - 1
        self.bit = [lax.rem(lax.div(self.seq, 1 << b), 2) for b in range(self.bits)]

    def flipped(self, bit):
        return self.beside((1 - 2 * self.bit[bit]) * (1 << bit))

    def after(self):
        return (lax.rem(self.seq + 1, self.count), self.tp)

    def before(self):
        return (lax.rem(self.seq + self.count - 1, self.count), self.tp)

    def mate(self):
        return (self.seq, self.tp + 1 - 2 * self.low)

    def across(self):
        return (self.seq, self.tp + 2 - 4 * self.high)

    def corner(self):
        return (self.seq, self.tp + 3 - 2 * self.low - 4 * self.high)

    def beside(self, by):
        return (self.seq + by, self.tp)


def remote(src, dst, send, recv, device):
    return pltpu.make_async_remote_copy(
        src_ref=src,
        dst_ref=dst,
        send_sem=send,
        recv_sem=recv,
        device_id=device,
        device_id_type=MESH,
    )


class TpReduce:
    def __init__(self, me, part, first, second, sems, index):
        self.me, self.part, self.first, self.second = me, part, first, second
        send, recv = sems
        self.one = remote(
            part.at[:, :, 1 - me.low], first, send.at[index, 0], recv.at[index, 0], me.mate()
        )
        self.two = remote(
            part.at[:, 1 - me.high, me.low],
            second,
            send.at[index, 1],
            recv.at[index, 1],
            me.across(),
        )

    def start(self):
        self.one.start()

    def middle(self):
        self.one.wait()
        part, first, low = self.part, self.first, self.me.low

        @pl.loop(0, part.shape[0], step=2)
        def _(at):
            k = pl.ds(at, 2)
            added = part[k, :, low].astype(F32) + first[k].astype(F32)
            part[k, :, low] = added.astype(part.dtype)

        self.two.start()

    def end(self):
        self.two.wait()

    def total(self, k):
        me = self.me
        return self.part[k, me.high, me.low].astype(F32) + self.second[k].astype(F32)


class TpGather:
    def __init__(self, me, whole, sems, index):
        send, recv = sems
        mine = whole.at[:, me.high, me.low]
        self.one = remote(mine, mine, send.at[index, 0], recv.at[index, 0], me.across())
        both = whole.at[:, :, me.low]
        self.two = remote(both, both, send.at[index, 1], recv.at[index, 1], me.mate())

    def start(self):
        self.one.start()

    def middle(self):
        self.one.wait()
        self.two.start()

    def end(self):
        self.two.wait()


def meet(me, friends):
    barrier = pltpu.get_barrier_semaphore()
    for friend in friends:
        pl.semaphore_signal(barrier, inc=1, device_id=friend, device_id_type=MESH)
    pl.semaphore_wait(barrier, len(friends))


def center_of(rows):
    center = rows - jnp.mean(rows, axis=-1, keepdims=True)
    inverse = lax.rsqrt(jnp.mean(center * center, axis=-1, keepdims=True) + NORM_EPS)
    return center * inverse, inverse


def norm_back(grad, scaled, inverse, gain):
    weighted = grad * gain
    first = jnp.mean(weighted, axis=-1, keepdims=True)
    second = jnp.mean(weighted * scaled, axis=-1, keepdims=True)
    return inverse * (weighted - first - scaled * second)


def eights(rows):
    d = rows.shape[-1]
    return jnp.sum(rows.reshape(-1, PART // 2, d), axis=0)


class SeqReduce:
    width = 256

    def __init__(self, me, grads, total, landed, sems, groups):
        self.me, self.grads, self.total, self.landed = me, grads, total, landed
        self.send, self.recv = sems
        self.groups = groups
        self.turn_at = 0

    def cols(self, chunk):
        return pl.ds(chunk * self.width, self.width)

    def plan(self, chunk):
        first = 1 if chunk % 5 == 4 else 0
        return [(i + first) % self.me.bits for i in range(self.me.bits)]

    def index(self, chunk, step, own):
        plan = self.plan(chunk)
        out = [chunk]
        for b in reversed(range(self.me.bits)):
            if b in plan[:step] or (b == plan[step] and own):
                out.append(self.me.bit[b])
            elif b == plan[step]:
                out.append(1 - self.me.bit[b])
            else:
                out.append(slice(None))
        return tuple(out)

    def copy(self, chunk, step):
        return remote(
            self.grads.at[self.index(chunk, step, False)],
            self.landed[step].at[chunk],
            self.send.at[step, chunk],
            self.recv.at[step, chunk],
            self.me.flipped(self.plan(chunk)[step]),
        )

    def finish(self, chunk, step):
        self.copy(chunk, step).wait()
        here = self.index(chunk, step, True)
        added = self.grads[here].astype(F32) + self.landed[step][chunk].astype(F32)
        if step == self.me.bits - 1:
            self.total[:, self.cols(chunk)] = added
        else:
            self.grads[here] = added.astype(BF)
            self.copy(chunk, step + 1).start()

    def launch(self, group):
        for chunk in self.groups[group]:
            self.copy(chunk, 0).start()

    def turn(self):
        at = self.turn_at
        self.turn_at += 1
        for step in reversed(range(self.me.bits)):
            group = at - step
            if 0 <= group < len(self.groups):
                for chunk in self.groups[group]:
                    self.finish(chunk, step)

    def drain(self):
        while self.turn_at < len(self.groups) + self.me.bits - 1:
            self.turn()


def split_store(me, grads, rows_from, first, tile):
    per, wide = grads.shape[-2:]
    n = tile.shape[0] // per
    for c in range(tile.shape[1] // wide):
        parts = tile[:, c * wide : (c + 1) * wide].astype(BF).reshape((n, per, wide))
        for i in range(n):
            at = rows_from // per + i
            grads[(first + c,) + tuple((at >> b) & 1 for b in reversed(range(me.bits)))] = parts[i]


def forward_kernel(
    rows_hbm,
    cot_hbm,
    mem_hbm,
    cot_new,
    w_comp,
    boundary,
    links,
    slopes,
    gains,
    shifts,
    w_query,
    w_key,
    w_value,
    w_out,
    w_in,
    w_down,
    normed_hbm,
    own_hbm,
    q_hbm,
    k_hbm,
    v_hbm,
    lse_hbm,
    ctx_hbm,
    ctxn_hbm,
    outp_hbm,
    hid_hbm,
    dhid_hbm,
    datt_hbm,
    gffn_hbm,
    vec_hbm,
    win_hbm,
    fresh_hbm,
    comp_hbm,
    x_ref,
    raw_ref,
    cot_ref,
    q_ref,
    k_ref,
    v_ref,
    lse_ref,
    ctx_ref,
    ctxn_ref,
    all_ref,
    wqkv_ref,
    wo_ref,
    wi_ref,
    wd_ref,
    parts,
    back_parts,
    back_firsts,
    back_quarters,
    nh_ref,
    datt_ref,
    act_ref,
    du_ref,
    hid_ref,
    vec_ref,
    ext_ref,
    cot_own,
    cot_prev,
    cot_pad,
    lead_pad,
    wc_ref,
    pick_ref,
    spread_ref,
    pool_ref,
    win_part,
    win_first,
    win_second,
    fresh_ref,
    comp_ref,
    comp_total,
    landed,
    load_sem,
    save_sem,
    stage_sem,
    place_sem,
    move_send,
    move_recv,
    pass_send,
    pass_recv,
    ctx_send,
    ctx_recv,
    wo_send,
    wo_recv,
    edge_send,
    edge_recv,
    rs_send,
    rs_recv,
    ag_send,
    ag_recv,
    seq_send,
    seq_recv,
):
    me = Place()
    d = x_ref.shape[-1]
    heads = q_ref.shape[1]
    width = heads * HEAD
    low, high = me.low, me.high
    kinds = list(range(KINDS))
    edge_rows = mem_hbm.shape[1]

    load_pairs = [
        (mem_hbm, ext_ref.at[:, pl.ds(0, edge_rows)]),
        (cot_new, cot_own),
        (w_comp, wc_ref),
        (w_key, wqkv_ref.at[:, pl.ds(0, width)]),
        (w_value, wqkv_ref.at[:, pl.ds(width, width)]),
        (w_query, wqkv_ref.at[:, pl.ds(2 * width, width)]),
        (w_out, wo_ref.at[pl.ds(pl.multiple_of(me.tp * width, width), width)]),
        (w_in, wi_ref),
        (w_down, wd_ref),
    ]
    loads = [
        pltpu.make_async_copy(src, dst, load_sem.at[i]) for i, (src, dst) in enumerate(load_pairs)
    ]
    for load in loads:
        load.start()

    meet(
        me,
        [me.mate(), me.across(), me.corner(), me.after(), me.before()]
        + [me.flipped(b) for b in range(me.bits)],
    )

    sources = [rows_hbm[0], rows_hbm[1], rows_hbm[2], cot_hbm]

    def landing(kind, slot, chunk):
        if kind == KINDS:
            return cot_ref.at[slot, chunk, :, low]
        return raw_ref.at[slot, kind, chunk]

    def route(micro, q):
        segment = jnp.where(q < me.column, me.column - 1, me.column)
        home, slot = home_of(segment, micro)
        return home, slot, PER_DEV * me.column + q - PER_SEG * segment

    def send_out(kinds, wanted):
        @pl.loop(0, 2 * PER_DEV)
        def _(at):
            micro, q = lax.div(at, PER_DEV), lax.rem(at, PER_DEV)
            home, slot, chunk = route(micro, q)
            here = home == me.column
            for kind in kinds:
                src = sources[kind].at[micro, q, :, low]
                dst = landing(kind, slot, chunk)

                @pl.when(jnp.logical_and(slot == wanted, here))
                def _():
                    pltpu.make_async_copy(src, dst, place_sem.at[kind, slot, chunk]).start()

                @pl.when(jnp.logical_and(slot == wanted, jnp.logical_not(here)))
                def _():
                    remote(
                        src,
                        dst,
                        move_send.at[kind, micro, q],
                        move_recv.at[kind, slot, chunk],
                        me.beside(home - me.column),
                    ).start()

    def sent(kinds, micro):
        @pl.loop(0, PER_DEV)
        def _(q):
            home, slot, chunk = route(micro, q)
            for kind in kinds:

                @pl.when(home != me.column)
                def _():
                    remote(
                        sources[kind].at[micro, q, :, low],
                        landing(kind, slot, chunk),
                        move_send.at[kind, micro, q],
                        move_recv.at[kind, slot, chunk],
                        me.beside(home - me.column),
                    ).wait_send()

    spans = []
    for slot in range(2):
        segment, _, there = units_of(me.column, slot)
        first = jnp.maximum(PER_DEV * me.column - PER_SEG * segment, 0)
        last = jnp.minimum(PER_DEV * me.column + PER_DEV - PER_SEG * segment, PER_SEG)
        spans.append((jnp.where(there, first, 0), jnp.where(there, last, PER_SEG), there))

    def wait_own(kind, slot, chunk):
        dst = landing(kind, slot, chunk)
        pltpu.make_async_copy(dst, dst, place_sem.at[kind, slot, chunk]).wait()

    def wait_moved(kind, slot, chunk):
        dst = landing(kind, slot, chunk)
        remote(
            dst, dst, move_send.at[kind, 0, 0], move_recv.at[kind, slot, chunk], me.mate()
        ).wait_recv()

    def over_own(kinds, slot, body):
        first, last, there = spans[slot]

        @pl.loop(first, last)
        def _(chunk):
            @pl.when(there)
            def _():
                for kind in kinds:
                    wait_own(kind, slot, chunk)

            body(chunk)

    def over_moved(kinds, slot, body):
        first, last, _ = spans[slot]

        def step(chunk):
            for kind in kinds:
                wait_moved(kind, slot, chunk)
            body(chunk)

        pl.loop(0, first)(step)
        pl.loop(last, PER_SEG)(step)

    gain_0, shift_0 = gains[0:1], shifts[0:1]
    gain_1, shift_1 = gains[1:2], shifts[1:2]

    def passing(kind, slot):
        here = cot_ref.at[slot, :, :, low] if kind == KINDS else x_ref.at[slot, kind, :, :, low]
        return remote(
            here, here, pass_send.at[kind, slot], pass_recv.at[kind, slot], me.mate()
        )

    def norm_chunk(u):
        def body(k):
            for kind in range(KINDS):
                raw = raw_ref[u, kind, k].reshape(2 * PART, d).astype(F32)
                scaled, _ = center_of(raw)
                normed = (scaled * gain_0 + shift_0).astype(BF)
                x_ref[u, kind, k, :, low] = normed.reshape(2, PART, d)

        return body

    def norm_own(u):
        over_own(kinds, u, norm_chunk(u))

    def norm_moved(u):
        over_moved(kinds, u, norm_chunk(u))
        for kind in kinds:
            passing(kind, u).start()

    def cot_pass(u):
        over_own([KINDS], u, lambda k: None)
        over_moved([KINDS], u, lambda k: None)
        passing(KINDS, u).start()

    saves = []

    def save(src, dst):
        copy = pltpu.make_async_copy(src, dst, save_sem.at[len(saves)])
        copy.start()
        saves.append(copy)

    def project(u):
        for kind in range(KINDS):
            passing(kind, u).wait()
            normed = x_ref[u, kind].reshape(SEG, d)
            span = pl.ds(kind * SEG, SEG)
            keys = dot_plain(normed, wqkv_ref[:, :width]).astype(BF)
            values = dot_plain(normed, wqkv_ref[:, width : 2 * width]).astype(BF)
            for h in range(heads):
                cols = slice(h * HEAD, (h + 1) * HEAD)
                k_ref[u, h, span] = keys[:, cols]
                v_ref[u, h, span] = values[:, cols]
            if kind == 0:
                queries = dot_plain(normed, wqkv_ref[:, 2 * width :]).astype(BF)
                for h in range(heads):
                    q_ref[u, h] = queries[:, h * HEAD : (h + 1) * HEAD]
        save(x_ref.at[u], normed_hbm.at[u])

    segments = lax.div(me.seq, PER_SEG) * PER_DEV

    def attend(u, h):
        scale = HEAD ** (-0.5)
        slope = slopes[h]
        segment, micro, _ = units_of(me.column, u)
        segment = jnp.minimum(segment, PER_DEV - 1) + segments
        edge = boundary[micro, segment]
        linked = links[micro, segment]
        key_at = lax.broadcasted_iota(jnp.int32, (1, KINDS * SEG), 1)
        kind_at = lax.div(key_at, SEG)
        bias = (key_at - 2 * SEG * kind_at).astype(F32) * (slope / SEG)
        key_x = lax.broadcasted_iota(jnp.int32, (QUERY_BLOCK, SEG), 1)
        per = QUERY_BLOCK // CHUNK

        @pl.loop(0, SEG // QUERY_BLOCK)
        def _(b):
            rows = pl.ds(pl.multiple_of(b * QUERY_BLOCK, QUERY_BLOCK), QUERY_BLOCK)
            raw = dot_second_t(q_ref[u, h, rows], k_ref[u, h]) * scale + bias
            at = b * QUERY_BLOCK + lax.broadcasted_iota(jnp.int32, (QUERY_BLOCK, SEG), 0)
            seen = jnp.logical_and(key_x <= at, jnp.logical_or(key_x >= edge, at < edge))
            near = jnp.where(seen, raw[:, :SEG], -1e30)
            open_row = jnp.logical_and(at[:, :1] < edge, linked == 1)
            far = jnp.where(open_row, raw[:, SEG:], -1e30)
            top = jnp.maximum(
                jnp.max(near, axis=-1, keepdims=True), jnp.max(far, axis=-1, keepdims=True)
            )
            near = jnp.exp(near - top)
            far = jnp.exp(far - top)
            whole = jnp.sum(near, axis=-1, keepdims=True) + jnp.sum(far, axis=-1, keepdims=True)
            lse_ref[u, h, rows] = jnp.broadcast_to(top + jnp.log(whole), (QUERY_BLOCK, HEAD))
            share = 1.0 / whole
            near = near * share
            far = far * share
            near_low = near.astype(BF)
            far_low = far.astype(BF)
            value_x, value_far = v_ref[u, h, :SEG], v_ref[u, h, SEG:]
            context = dot_plain(near_low, value_x) + dot_plain(far_low, value_far)
            near_rest = (near - near_low.astype(F32)).astype(BF)
            far_rest = (far - far_low.astype(F32)).astype(BF)
            rest = dot_plain(near_rest, value_x) + dot_plain(far_rest, value_far)
            ctxn_ref[u, h, rows] = context + rest
            ctx_ref[u, pl.ds(b * per, per), :, :, :, h * HEAD : (h + 1) * HEAD] = (
                context.astype(BF).reshape(per, 2, 2, PART, HEAD)
            )

    def my_columns(tp):
        return pl.ds(pl.multiple_of(tp * width, width), width)

    def ctx_copies(u):
        dst = all_ref.at[u, :, :, :, my_columns(me.tp)]
        same, other = ctx_ref.at[u, :, :, low], ctx_ref.at[u, :, :, 1 - low]
        return [
            remote(src, dst, ctx_send.at[u, i], ctx_recv.at[u, i], device)
            for i, (src, device) in enumerate(
                [(same, me.across()), (other, me.corner()), (other, me.mate())]
            )
        ]

    def ctx_start(u):
        for copy in ctx_copies(u):
            copy.start()
        all_ref[u, :, :, :, my_columns(me.tp)] = ctx_ref[u, :, :, low]
        save(ctx_ref.at[u], ctx_hbm.at[u])
        save(ctxn_ref.at[u], ctxn_hbm.at[u])

    def wo_rows(tp):
        return wo_ref.at[pl.ds(pl.multiple_of(tp * width, width), width)]

    across_tp = me.tp + 2 - 4 * high
    mate_tp = me.tp + 1 - 2 * low
    wo_copies = [
        remote(w_out, wo_rows(me.tp), wo_send.at[0], wo_recv.at[0], me.across()),
        remote(w_out, wo_rows(me.tp), wo_send.at[1], wo_recv.at[1], me.mate()),
        remote(
            wo_rows(across_tp), wo_rows(across_tp), wo_send.at[2], wo_recv.at[2], me.mate()
        ),
    ]

    def half_pass(ref, u, kind):
        here = ref.at[u, :, :, low]
        return remote(here, here, pass_send.at[kind, u], pass_recv.at[kind, u], me.mate())

    def hidden_norm(u):
        for copy in ctx_copies(u):
            copy.wait()

        @pl.loop(0, 2)
        def _(r):
            some = pl.ds(r * (PER_SEG // 2), PER_SEG // 2)
            rows = SEG // 4
            hidden = dot_plain(all_ref[u, some].reshape(rows, 4 * width), wo_ref[...])
            hidden += raw_ref[u, 0, some].reshape(rows, d).astype(F32)
            hid_ref[u, some] = hidden.reshape(PER_SEG // 2, 2, PART, d)
            scaled, _ = center_of(hidden)
            normed = (scaled * gain_1 + shift_1).astype(BF)
            nh_ref[u, some, :, low] = normed.reshape(PER_SEG // 2, 2, PART, d)

        half_pass(nh_ref, u, KINDS + 1).start()
        save(hid_ref.at[u, :, high], hid_hbm.at[u])

    def store_part(part, cols, tile):
        part[:, :, :, :, cols] = tile.astype(part.dtype).reshape(
            PER_SEG, 2, 2, PART, tile.shape[1]
        )

    def ffn_up(u):
        ff = wi_ref.shape[1]

        @pl.loop(0, ff // 256)
        def _(n):
            cols = pl.ds(pl.multiple_of(n * 256, 256), 256)
            for r in range(2):
                chunks = slice(r * PER_SEG // 2, (r + 1) * PER_SEG // 2)
                rows = slice(r * SEG // 2, (r + 1) * SEG // 2)
                upper = dot_plain(nh_ref[u, chunks].reshape(SEG // 2, d), wi_ref[:, cols])
                d_act = dot_second_t(cot_ref[u, chunks].reshape(SEG // 2, d), wd_ref[cols])
                square = upper * upper
                inner = GELU_IN * upper * (1.0 + 0.044715 * square)
                bend = jnp.tanh(inner)
                grown = 0.5 * (1.0 + bend)
                act_ref[u, rows, cols] = (upper * grown).astype(BF)
                slope = grown + 0.5 * upper * (1.0 - bend * bend) * (
                    GELU_IN * (1.0 + 3.0 * 0.044715 * square)
                )
                du_ref[u, rows, cols] = (d_act * slope).astype(BF)

    def ffn_out(u, part):
        @pl.loop(0, d // 256)
        def _(n):
            cols = pl.ds(pl.multiple_of(n * 256, 256), 256)
            store_part(part, cols, dot_plain(act_ref[u], wd_ref[:, cols]))

    def ffn_back(u, part):
        @pl.loop(0, d // 256)
        def _(n):
            cols = pl.ds(pl.multiple_of(n * 256, 256), 256)
            store_part(part, cols, dot_second_t(du_ref[u], wi_ref[cols]))

    def hidden_back(u, task):
        task.end()

        @pl.loop(0, PER_SEG, step=4)
        def _(at):
            k = pl.ds(at, 4)
            scaled, inverse = center_of(hid_ref[u, k, high])
            grad = task.total(k)
            cot = cot_ref[u, k, high, low].astype(F32)
            d_hidden = cot + norm_back(grad, scaled, inverse, gain_1)
            vec_ref[0] += eights(grad * scaled)
            vec_ref[1] += eights(grad)
            task.second[k] = d_hidden
            datt_ref[u, k, high, low] = d_hidden.astype(BF)

        datts[u].start()
        save(task.second, dhid_hbm.at[u])

    staged = []

    def weight_grads(first, left, right):
        for n in range(d // 256):
            cols = slice(n * 256, (n + 1) * 256)
            slot = len(staged) % 2
            if len(staged) >= 2:
                for copy in staged[-2]:
                    copy.wait()
            tile = dot_first_t(left(0, cols), right(0)) + dot_first_t(left(1, cols), right(1))
            chunks = tile.shape[1] // 256
            rows = pl.ds(slot * 256, 256)
            pool_ref[rows, : tile.shape[1]] = tile.astype(BF)
            copies = [
                pltpu.make_async_copy(
                    pool_ref.at[rows, pl.ds(c * 256, 256)],
                    gffn_hbm.at[first + c, cols],
                    stage_sem.at[slot, c],
                )
                for c in range(chunks)
            ]
            for copy in copies:
                copy.start()
            staged.append(copies)

    slots = cot_new.shape[1]
    rows_here = edge_rows * PART
    edges = [
        remote(
            mem_hbm.at[:, pl.ds(0, REACH // PART)],
            ext_ref.at[:, pl.ds(edge_rows, REACH // PART)],
            edge_send.at[0],
            edge_recv.at[0],
            me.before(),
        ),
        remote(cot_new, cot_prev, edge_send.at[1], edge_recv.at[1], me.after()),
    ]
    seq = SeqReduce(me, comp_ref, comp_total, landed, (seq_send, seq_recv), [[0, 1, 2]])
    win = TpReduce(me, win_part, win_first, win_second, (rs_send, rs_recv), 0)

    def local_rows(at, tap, is_lead):
        slot = slots * me.column + at - jnp.where(is_lead, LEAD, 0)
        used = at < jnp.where(is_lead, LEAD, slots)
        slot_seg = lax.div(slot, CSEG)
        place = 3 * (slot - slot_seg * CSEG) + tap
        there = jnp.logical_and(used, jnp.logical_and(slot >= 0, place < SEG))
        return jnp.where(there, slot_seg * SEG + place - rows_here * me.column, -1)

    lead_rows = 32
    own_rows = 3 * SLOT_PAD
    ext_rows = rows_here + REACH
    feats = w_comp.shape[2]

    def compress_masks():
        row = lax.broadcasted_iota(jnp.int32, (own_rows, 1), 0)
        tap = lax.div(row, SLOT_PAD)
        local = local_rows(row - tap * SLOT_PAD, tap, False)
        where_at = lax.broadcasted_iota(jnp.int32, (own_rows, ext_rows), 1)
        pick_ref[...] = jnp.where(local == where_at, 1.0, 0.0).astype(BF)
        col = lax.broadcasted_iota(jnp.int32, (1, own_rows + 3 * lead_rows), 1)
        is_lead = col >= own_rows
        col = jnp.where(is_lead, col - own_rows, col)
        per = jnp.where(is_lead, lead_rows, SLOT_PAD)
        tap = jnp.where(is_lead, lax.div(col, lead_rows), lax.div(col, SLOT_PAD))
        local = local_rows(col - tap * per, tap, is_lead)
        where_at = lax.broadcasted_iota(jnp.int32, spread_ref.shape, 0)
        spread_ref[...] = jnp.where(local == where_at, 1.0, 0.0).astype(BF)
        cot_pad[...] = jnp.zeros(cot_pad.shape, BF)
        lead_pad[...] = jnp.zeros(lead_pad.shape, BF)

    def compress():
        for load in loads[:3]:
            load.wait()
        for copy in edges:
            copy.wait()
        grads = [None] * 3
        for m in range(2):
            cot_pad[m, :slots] = cot_own[m]
            lead_pad[m, :LEAD] = cot_prev[m, slots - LEAD :]
            cot, cot_lead = cot_pad[m], lead_pad[m]
            fresh = None
            taken = dot_plain(pick_ref[...], ext_ref[m].reshape(ext_rows, d)).astype(BF)
            for tap in range(3):
                span = slice(tap * SLOT_PAD, (tap + 1) * SLOT_PAD)
                lead = slice(own_rows + tap * lead_rows, own_rows + (tap + 1) * lead_rows)
                term = dot_plain(taken[span], wc_ref[tap])
                fresh = term if fresh is None else fresh + term
                term = dot_first_t(taken[span], cot)
                grads[tap] = term if grads[tap] is None else grads[tap] + term
                pool_ref[span, :d] = dot_second_t(cot, wc_ref[tap]).astype(BF)
                pool_ref[lead, :d] = dot_second_t(cot_lead, wc_ref[tap]).astype(BF)
            fresh_ref[m] = fresh[:slots]
            for n in range(2):
                cols = slice(n * d // 2, (n + 1) * d // 2)
                tile = dot_plain(spread_ref[...], pool_ref[:, cols])
                win_part[m * PER_DEV : (m + 1) * PER_DEV, :, :, :, cols] = (
                    tile.astype(BF).reshape(PER_DEV, 2, 2, PART, d // 2)
                )
        for tap in range(3):
            split_store(me, comp_ref, 0, tap * (feats // 256), grads[tap])
        save(fresh_ref, fresh_hbm)

    def win_end():
        win.end()

        @pl.loop(0, 2 * PER_DEV, step=2)
        def _(at):
            k = pl.ds(at, 2)
            win_second[k] = win.total(k).astype(BF)

        save(win_second, win_hbm)

    rs = (rs_send, rs_recv)
    backs = [
        TpReduce(me, back_parts[u], back_firsts[u], back_quarters[u], rs, 1 + u) for u in range(2)
    ]
    datts = [TpGather(me, datt_ref.at[u], (ag_send, ag_recv), u) for u in range(2)]

    send_out(kinds, 0)
    for copy in edges:
        copy.start()
    for copy in wo_copies[:2]:
        copy.start()
    vec_ref[...] = jnp.zeros(vec_ref.shape, F32)

    @pl.when(jnp.logical_not(spans[1][2]))
    def _():
        raw_ref[1] = jnp.zeros(raw_ref.shape[1:], BF)
        cot_ref[1, :, :, low] = jnp.zeros((PER_SEG, 2, PART, d), BF)

    compress_masks()
    norm_own(0)
    norm_moved(0)
    send_out(kinds, 1)
    for load in loads[3:6]:
        load.wait()
    project(0)
    attend(0, 0)
    wo_copies[0].wait()
    wo_copies[2].start()
    norm_own(1)
    attend(0, 1)
    ctx_start(0)
    compress()
    win.start()
    norm_moved(1)
    send_out([KINDS], 0)
    send_out([KINDS], 1)
    seq.launch(0)
    win.middle()
    project(1)
    save(q_ref, q_hbm)
    save(k_ref, k_hbm)
    save(v_ref, v_hbm)
    save(raw_ref.at[:, :, :, high], own_hbm)
    loads[6].wait()
    for copy in wo_copies[1:]:
        copy.wait()
    hidden_norm(0)
    attend(1, 0)
    cot_pass(0)
    attend(1, 1)
    win_end()
    save(lse_ref, lse_hbm)
    ctx_start(1)
    cot_pass(1)
    loads[7].wait()
    loads[8].wait()
    half_pass(nh_ref, 0, KINDS + 1).wait()
    passing(KINDS, 0).wait()
    ffn_up(0)
    ffn_back(0, back_parts[0])
    backs[0].start()
    hidden_norm(1)
    backs[0].middle()
    seq.turn()
    ffn_out(0, parts[0])
    save(parts[0], outp_hbm.at[0])
    half_pass(nh_ref, 1, KINDS + 1).wait()
    passing(KINDS, 1).wait()
    ffn_up(1)
    ffn_back(1, back_parts[1])
    backs[1].start()
    ffn_out(1, parts[1])
    save(parts[1], outp_hbm.at[1])
    backs[1].middle()
    hidden_back(0, backs[0])
    seq.turn()
    ff = wi_ref.shape[1]
    weight_grads(
        0, lambda u, cols: nh_ref[u, :, :, :, :, cols].reshape(SEG, 256), lambda u: du_ref[u]
    )
    weight_grads(
        ff // 256, lambda u, cols: cot_ref[u, :, :, :, :, cols].reshape(SEG, 256), lambda u: act_ref[u]
    )
    seq.drain()
    save(comp_total, comp_hbm)
    hidden_back(1, backs[1])
    save(vec_ref, vec_hbm)
    datts[0].middle()
    datts[1].middle()
    datts[0].end()
    save(datt_ref.at[0], datt_hbm.at[0])
    datts[1].end()
    save(datt_ref.at[1], datt_hbm.at[1])
    for micro in range(2):
        sent(kinds + [KINDS], micro)
    for copies in staged[-2:]:
        for copy in copies:
            copy.wait()
    for copy in saves:
        copy.wait()


def forward_call(rows, cot, memory, cot_new, w_comp, boundary, links, slopes, gains, shifts, weights):
    count = lax.axis_size("seq")
    bits = count.bit_length() - 1
    d = cot.shape[-1]
    heads = weights[0].shape[1] // HEAD
    width = heads * HEAD
    ff = weights[4].shape[1]
    slots, feats = cot_new.shape[1:]
    split = (PER_SEG, 2, 2, PART, d)
    half = (PER_SEG, 2, PART, d)
    own = (PER_SEG, PART, d)
    keys = KINDS * SEG
    owned = 2 * PER_DEV
    shard = d // count
    any_space = pl.BlockSpec(memory_space=pl.ANY)
    smem = pl.BlockSpec(memory_space=pltpu.SMEM)
    vmem = pl.BlockSpec(memory_space=pltpu.VMEM)
    shapes = [
        ((2, KINDS) + split, BF),
        ((2, KINDS) + own, BF),
        ((2, heads, SEG, HEAD), BF),
        ((2, heads, keys, HEAD), BF),
        ((2, heads, keys, HEAD), BF),
        ((2, heads, SEG, HEAD), F32),
        ((2, PER_SEG, 2, 2, PART, width), BF),
        ((2, heads, SEG, HEAD), F32),
        ((2,) + split, BF),
        ((2,) + own, F32),
        ((2,) + own, F32),
        ((2,) + split, BF),
        ((2 * ff // 256, d, 256), BF),
        ((2, 8, d), F32),
        ((owned, PART, d), BF),
        ((2, slots, feats), F32),
        ((shard, 3 * feats), F32),
    ]
    dma = pltpu.SemaphoreType.DMA
    total_rows = 3 * (SLOT_PAD + 32)
    ext_rows = memory.shape[1] + REACH // PART
    scratch = [
        pltpu.VMEM((2, KINDS) + split, BF),
        pltpu.VMEM((2, KINDS) + half, BF),
        pltpu.VMEM((2,) + split, BF),
        pltpu.VMEM((2, heads, SEG, HEAD), BF),
        pltpu.VMEM((2, heads, keys, HEAD), BF),
        pltpu.VMEM((2, heads, keys, HEAD), BF),
        pltpu.VMEM((2, heads, SEG, HEAD), F32),
        pltpu.VMEM((2, PER_SEG, 2, 2, PART, width), BF),
        pltpu.VMEM((2, heads, SEG, HEAD), F32),
        pltpu.VMEM((2, PER_SEG, 2, PART, 4 * width), BF),
        pltpu.VMEM((d, 3 * width), BF),
        pltpu.VMEM((4 * width, d), BF),
        pltpu.VMEM((d, ff), BF),
        pltpu.VMEM((ff, d), BF),
        [pltpu.VMEM(split, BF) for _ in range(2)],
        [pltpu.VMEM(split, F32) for _ in range(2)],
        [pltpu.VMEM(half, F32) for _ in range(2)],
        [pltpu.VMEM(own, F32) for _ in range(2)],
        pltpu.VMEM((2,) + split, BF),
        pltpu.VMEM((2,) + split, BF),
        pltpu.VMEM((2, SEG, ff), BF),
        pltpu.VMEM((2, SEG, ff), BF),
        pltpu.VMEM((2,) + half, F32),
        pltpu.VMEM((2, 8, d), F32),
        pltpu.VMEM((2, ext_rows, PART, d), BF),
        pltpu.VMEM((2, slots, feats), BF),
        pltpu.VMEM((2, slots, feats), BF),
        pltpu.VMEM((2, SLOT_PAD, feats), BF),
        pltpu.VMEM((2, 32, feats), BF),
        pltpu.VMEM((3, d, feats), BF),
        pltpu.VMEM((3 * SLOT_PAD, ext_rows * PART), BF),
        pltpu.VMEM((memory.shape[1] * PART, total_rows), BF),
        pltpu.VMEM((total_rows, max(d, ff)), BF),
        pltpu.VMEM((owned, 2, 2, PART, d), BF),
        pltpu.VMEM((owned, 2, PART, d), BF),
        pltpu.VMEM((owned, PART, d), BF),
        pltpu.VMEM((2, slots, feats), F32),
        pltpu.VMEM((3 * feats // 256,) + (2,) * bits + (shard, 256), BF),
        pltpu.VMEM((shard, 3 * feats), F32),
        [
            pltpu.VMEM((3 * feats // 256,) + (2,) * (bits - 1 - i) + (shard, 256), BF)
            for i in range(bits)
        ],
        dma((9,)),
        dma((24,)),
        dma((2, ff // 256)),
        dma((KINDS + 1, 2, PER_SEG)),
        dma((KINDS + 1, 2, PER_DEV)),
        dma((KINDS + 1, 2, PER_SEG)),
        dma((KINDS + 3, 2)),
        dma((KINDS + 3, 2)),
        dma((2, 3)),
        dma((2, 3)),
        dma((3,)),
        dma((3,)),
        dma((2,)),
        dma((2,)),
        dma((3, 2)),
        dma((3, 2)),
        dma((2, 2)),
        dma((2, 2)),
        dma((bits, 3)),
        dma((bits, 3)),
    ]
    return pl.pallas_call(
        forward_kernel,
        out_shape=[jax.ShapeDtypeStruct(shape, kind) for shape, kind in shapes],
        in_specs=[[any_space] * KINDS]
        + [any_space] * 4
        + [smem] * 3
        + [vmem] * 2
        + [any_space] * 6,
        out_specs=[any_space] * len(shapes),
        scratch_shapes=scratch,
        compiler_params=pltpu.CompilerParams(
            collective_id=1, has_side_effects=True, vmem_limit_bytes=63 << 20
        ),
    )(rows, cot, memory, cot_new, w_comp, boundary, links, slopes, gains, shifts, *weights)


FINALS = 4


def backward_kernel(
    normed_hbm,
    own_hbm,
    q_hbm,
    k_hbm,
    v_hbm,
    lse_hbm,
    ctx_hbm,
    ctxn_hbm,
    outp_hbm,
    hid_hbm,
    dhid_hbm,
    datt_hbm,
    gffn_hbm,
    win_hbm,
    vec_in,
    boundary,
    links,
    slopes,
    gains,
    w_query,
    w_key,
    w_value,
    w_out,
    finals,
    total_hbm,
    small_hbm,
    normed_ref,
    own_ref,
    q_ref,
    kx_ref,
    v_ref,
    lse_ref,
    ctx_ref,
    ctxn_ref,
    dhid_ref,
    datt_ref,
    wqkv_ref,
    wo_ref,
    dctx_ref,
    ds_ref,
    prob_ref,
    dq_ref,
    dqkv_ref,
    parts,
    firsts,
    seconds,
    out_parts,
    hid_ref,
    out_ref,
    win_ref,
    home_ref,
    owner_ref,
    grads_ref,
    total_ref,
    landed,
    vec_ref,
    aux_ref,
    small_ref,
    small_came,
    load_sem,
    save_sem,
    rs_send,
    rs_recv,
    ag_send,
    ag_recv,
    ag_here,
    move_send,
    move_recv,
    seq_send,
    seq_recv,
    small_send,
    small_recv,
):
    me = Place()
    d = normed_ref.shape[-1]
    heads = q_ref.shape[1]
    width = heads * HEAD
    late = gffn_hbm.shape[0]
    heads_wide = width // 256

    load_pairs = {
        "gffn": (gffn_hbm, grads_ref.at[pl.ds(0, late)]),
        "outp0": (outp_hbm.at[0], out_parts[0]),
        "outp1": (outp_hbm.at[1], out_parts[1]),
        "datt": (datt_hbm, datt_ref),
        "wo": (w_out, wo_ref),
        "v": (v_hbm, v_ref),
        "ctxn": (ctxn_hbm, ctxn_ref),
        "lse": (lse_hbm, lse_ref),
        "k": (k_hbm, kx_ref.at[:, :, :, pl.ds(0, HEAD)]),
        "q": (q_hbm, q_ref),
        "wk": (w_key, wqkv_ref.at[:, pl.ds(0, width)]),
        "wv": (w_value, wqkv_ref.at[:, pl.ds(width, width)]),
        "wq": (w_query, wqkv_ref.at[:, pl.ds(2 * width, width)]),
        "hid": (hid_hbm, hid_ref),
        "own": (own_hbm, own_ref),
        "dhid": (dhid_hbm, dhid_ref),
        "win": (win_hbm, win_ref),
        "vec": (vec_in, vec_ref.at[pl.ds(2, 2)]),
        "normed": (normed_hbm, normed_ref),
        "ctx": (ctx_hbm, ctx_ref),
    }
    loads = {
        name: pltpu.make_async_copy(src, dst, load_sem.at[i])
        for i, (name, (src, dst)) in enumerate(load_pairs.items())
    }
    for load in loads.values():
        load.start()

    def ready(*names):
        for name in names:
            loads[name].wait()

    meet(
        me,
        [me.mate(), me.across(), me.after(), me.before()]
        + [me.flipped(b) for b in range(me.bits)],
    )

    gain_0 = gains[0:1]
    vec_ref[:2] = jnp.zeros((2,) + vec_ref.shape[1:], F32)
    aux_ref[...] = jnp.zeros(aux_ref.shape, F32)
    key_at = lax.broadcasted_iota(jnp.int32, (KINDS * SEG, HEAD), 0)
    lane = lax.broadcasted_iota(jnp.int32, (KINDS * SEG, HEAD), 1)
    kind_at = lax.div(key_at, SEG)
    in_kind = key_at - SEG * kind_at
    odd = lax.rem(in_kind, 2)
    marks = jnp.where(
        lane == 0,
        in_kind - odd,
        jnp.where(lane == 1, odd, jnp.where(lane == 2, kind_at, jnp.where(lane == 3, 1, 0))),
    )
    marks = marks.astype(F32).astype(BF)
    for u in range(2):
        for h in range(heads):
            kx_ref[u, h, :, HEAD:] = marks

    rs = (rs_send, rs_recv)
    sems = (seq_send, seq_recv)
    chunks = grads_ref.shape[0]
    n = chunks - 8

    def reducer(groups):
        return SeqReduce(me, grads_ref, total_ref, landed, sems, groups)

    seq = reducer([[i] for i in range(n)] + [[n, n + 1]])
    mid = reducer([[n + 2, n + 3, n + 4]])
    tail = reducer([[n + 5, n + 6, n + 7]])


    def to_owner(kind, slot):
        segment, micro, there = units_of(me.column, slot)

        @pl.loop(0, PER_SEG)
        def _(chunk):
            place = PER_SEG * segment + chunk
            holder = lax.div(place, PER_DEV)
            q = lax.rem(place, PER_DEV)
            src = out_ref.at[slot, chunk] if kind == KINDS else home_ref.at[kind, slot, chunk]
            dst = owner_ref.at[kind, micro, q]

            @pl.when(jnp.logical_and(there, holder == me.column))
            def _():
                pltpu.make_async_copy(src, dst, move_recv.at[kind, micro, q]).start()

            @pl.when(jnp.logical_and(there, holder != me.column))
            def _():
                remote(
                    src,
                    dst,
                    move_send.at[kind, slot, chunk],
                    move_recv.at[kind, micro, q],
                    me.beside(holder - me.column),
                ).start()

    def sent(kind, slot):
        segment, micro, there = units_of(me.column, slot)

        @pl.loop(0, PER_SEG)
        def _(chunk):
            holder = lax.div(PER_SEG * segment + chunk, PER_DEV)

            @pl.when(jnp.logical_and(there, holder != me.column))
            def _():
                src = home_ref.at[0, slot, chunk]
                remote(
                    src,
                    src,
                    move_send.at[kind, slot, chunk],
                    move_recv.at[kind, 0, 0],
                    me.mate(),
                ).wait_send()

    def collect(kind, micro):
        @pl.loop(0, PER_DEV)
        def _(q):
            segment = jnp.where(q < me.column, me.column - 1, me.column)
            home, slot = home_of(segment, micro)
            dst = owner_ref.at[kind, micro, q]

            @pl.when(home == me.column)
            def _():
                pltpu.make_async_copy(dst, dst, move_recv.at[kind, micro, q]).wait()

            @pl.when(home != me.column)
            def _():
                remote(
                    dst,
                    dst,
                    move_send.at[kind, 0, 0],
                    move_recv.at[kind, micro, q],
                    me.mate(),
                ).wait_recv()

    class Final:
        def __init__(self, kind, micro):
            self.own = owner_ref.at[kind, micro]
            whole = finals[kind].at[micro]
            self.mine = whole.at[:, me.high, me.low]
            self.here = pltpu.make_async_copy(self.own, self.mine, ag_here.at[kind, micro])
            self.one = remote(
                self.own,
                self.mine,
                ag_send.at[kind, micro, 0],
                ag_recv.at[kind, micro, 0],
                me.across(),
            )
            both = whole.at[:, :, me.low]
            self.two = remote(
                both, both, ag_send.at[kind, micro, 1], ag_recv.at[kind, micro, 1], me.mate()
            )

        def start(self):
            self.here.start()
            self.one.start()

        def middle(self):
            self.here.wait()
            self.one.wait()
            self.two.start()

        def end(self):
            self.two.wait()

    def context_back(u):
        datt = datt_ref[u].reshape(SEG, d)
        for h in range(heads):
            rows = slice(h * HEAD, (h + 1) * HEAD)
            dctx_ref[u, h] = dot_second_t(datt, wo_ref[rows]).astype(BF)

    segments = lax.div(me.seq, PER_SEG) * PER_DEV

    def attend_back(u, h, kind):
        scale = HEAD ** (-0.5)
        rows_at_once = 2 * QUERY_BLOCK
        keys = slice(kind * SEG, (kind + 1) * SEG)
        segment, micro, _ = units_of(me.column, u)
        segment = jnp.minimum(segment, PER_DEV - 1) + segments
        edge = boundary[micro, segment]
        linked = links[micro, segment]
        key_x = lax.broadcasted_iota(jnp.int32, (1, SEG), 1)
        bias = (key_x - SEG * kind).astype(F32) * (slopes[h] / SEG)

        @pl.loop(0, SEG // rows_at_once)
        def _(b):
            rows = pl.ds(pl.multiple_of(b * rows_at_once, rows_at_once), rows_at_once)
            scores = dot_second_t(q_ref[u, h, rows], kx_ref[u, h, keys, :HEAD]) * scale + bias
            at = b * rows_at_once + lax.broadcasted_iota(jnp.int32, (rows_at_once, 1), 0)
            if kind == 0:
                seen = jnp.logical_and(key_x <= at, jnp.logical_or(key_x >= edge, at < edge))
            else:
                seen = jnp.logical_and(at < edge, linked == 1)
            prob = jnp.exp(jnp.where(seen, scores - lse_ref[u, h, rows, :1], -1e30))
            prob_ref[rows] = prob.astype(BF)
            d_ctx = dctx_ref[u, h, rows]
            d_prob = dot_second_t(d_ctx, v_ref[u, h, keys])
            mean = jnp.sum(d_ctx.astype(F32) * ctxn_ref[u, h, rows], axis=-1, keepdims=True)
            d_scores = (prob * (d_prob - mean)).astype(BF)
            ds_ref[rows] = d_scores
            both = dot_plain(d_scores, kx_ref[u, h, keys])
            if kind < KINDS - 1:
                both += dq_ref[h, rows]
            if kind > 0:
                dq_ref[h, rows] = both
            else:
                cols = slice(2 * width + h * HEAD, 2 * width + (h + 1) * HEAD)
                dqkv_ref[u, 0, rows, cols] = (both[:, :HEAD] * scale).astype(BF)
                marked = both[:, HEAD:]
                at = b * rows_at_once + lax.broadcasted_iota(jnp.int32, marked.shape, 0)
                aux_ref[h, 0:1] += jnp.sum(marked, axis=0, keepdims=True)
                aux_ref[h, 1:2] += jnp.sum(marked * at.astype(F32), axis=0, keepdims=True)

        d_key = dot_first_t(ds_ref[...], q_ref[u, h]) * scale
        d_value = dot_first_t(prob_ref[...], dctx_ref[u, h])
        dqkv_ref[u, kind, :, h * HEAD : (h + 1) * HEAD] = d_key.astype(BF)
        dqkv_ref[u, kind, :, width + h * HEAD : width + (h + 1) * HEAD] = d_value.astype(BF)

    def project_back(u, kind, part):
        depth = (3 if kind == 0 else 2) * width

        @pl.loop(0, d // 256)
        def _(n):
            cols = pl.ds(pl.multiple_of(n * 256, 256), 256)
            tile = dot_second_t(dqkv_ref[u, kind, :, :depth], wqkv_ref[cols, :depth])
            part[:, :, :, :, cols] = tile.astype(BF).reshape(PER_SEG, 2, 2, PART, 256)

    def norm_end(u, kind, task):
        task.end()

        @pl.loop(0, PER_SEG, step=4)
        def _(at):
            k = pl.ds(at, 4)
            scaled, inverse = center_of(own_ref[u, kind, k].astype(F32))
            grad = task.total(k)
            vec_ref[0] += eights(grad * scaled)
            vec_ref[1] += eights(grad)
            result = norm_back(grad, scaled, inverse, gain_0)
            if kind == 0:
                result += dhid_ref[u, k]
            home_ref[kind, u, k] = result.astype(BF)

    def add_window(micro):
        @pl.loop(0, PER_DEV)
        def _(q):
            added = owner_ref[1, micro, q].astype(F32) + win_ref[micro * PER_DEV + q].astype(F32)
            owner_ref[1, micro, q] = added.astype(BF)

    def late_kv():
        for n in range(d // 256):
            cols = slice(n * 256, (n + 1) * 256)
            kv = None
            for u in range(2):
                for kind in range(KINDS):
                    left = normed_ref[u, kind, :, :, :, :, cols].reshape(SEG, 256)
                    term = dot_first_t(left, dqkv_ref[u, kind, :, : 2 * width])
                    kv = term if kv is None else kv + term
            split_store(me, grads_ref, n * 256, late + heads_wide, kv)

    def late_query():
        for n in range(d // 256):
            cols = slice(n * 256, (n + 1) * 256)
            query = None
            for u in range(2):
                left = normed_ref[u, 0, :, :, :, :, cols].reshape(SEG, 256)
                term = dot_first_t(left, dqkv_ref[u, 0, :, 2 * width :])
                query = term if query is None else query + term
            split_store(me, grads_ref, n * 256, late + 3 * heads_wide, query)

    def out_grad():
        for n in range(d // 256):
            cols = slice(n * 256, (n + 1) * 256)
            out = None
            for u in range(2):
                left = datt_ref[u, :, :, :, :, cols].reshape(SEG, 256)
                term = dot_first_t(left, ctx_ref[u].reshape(SEG, width))
                out = term if out is None else out + term
            split_store(me, grads_ref, n * 256, late, out)

    friends = [me.mate(), me.across()] + [me.flipped(b) for b in range(me.bits)]

    def small_copy(i):
        return remote(
            small_ref, small_came.at[i], small_send.at[i], small_recv.at[i], friends[i]
        )

    def small_start():
        lane = lax.broadcasted_iota(jnp.int32, (1, HEAD), 1)
        plain = jnp.where(lane < 2, 1.0, jnp.where(lane == 2, -float(SEG), 0.0))
        placed = jnp.where(lane == 3, 1.0, 0.0)
        small_ref[...] = jnp.zeros(small_ref.shape, F32)
        for i, at in enumerate((0, 2, 1, 3)):
            small_ref[i : i + 1] = jnp.sum(vec_ref[at], axis=0, keepdims=True)
        row = jnp.zeros((1, HEAD), F32)
        for h in range(heads):
            marked = aux_ref[h, 0:1] * plain - aux_ref[h, 1:2] * placed
            total = jnp.sum(marked, axis=-1, keepdims=True) / SEG
            row += jnp.where(lane == me.tp * heads + h, total, 0.0)
        small_ref[4:5, :HEAD] = row
        small_copy(0).start()

    def small_step(i):
        small_copy(i).wait()
        small_ref[...] += small_came[i]
        if i + 1 < len(friends):
            small_copy(i + 1).start()

    results = {}

    def final_start(kind, micro):
        collect(kind, micro)
        if kind == 1:
            add_window(micro)
        results[kind, micro] = Final(kind, micro)
        results[kind, micro].start()

    tasks = {
        (u, kind): TpReduce(
            me, parts[kind], firsts[u * KINDS + kind], seconds[u * KINDS + kind], rs, u * KINDS + kind
        )
        for u in range(2)
        for kind in range(KINDS)
    }

    def attend_kind(u, kind):
        for h in range(heads):
            attend_back(u, h, kind)

    def send_kind(u, kind):
        project_back(u, kind, parts[kind])
        tasks[u, kind].start()

    def end_kind(u, kind):
        norm_end(u, kind, tasks[u, kind])
        to_owner(kind, u)

    outs = [
        TpReduce(
            me, out_parts[u], firsts[2 * KINDS + u], seconds[2 * KINDS + u], rs, 2 * KINDS + u
        )
        for u in range(2)
    ]

    def out_end(u):
        outs[u].end()

        @pl.loop(0, PER_SEG, step=4)
        def _(at):
            k = pl.ds(at, 4)
            out_ref[u, k] = (hid_ref[u, k] + outs[u].total(k)).astype(BF)

        to_owner(KINDS, u)

    ready("outp0", "outp1")
    for u in range(2):
        outs[u].start()
    ready("gffn")
    for group in range(3):
        seq.launch(group)
    ready("datt", "wo")
    context_back(0)
    ready("v", "ctxn", "lse", "k", "q")
    for u in range(2):
        outs[u].middle()
    attend_kind(0, 2)
    ready("wk", "wv", "wq")
    send_kind(0, 2)
    seq.turn()
    seq.launch(3)
    attend_kind(0, 1)
    tasks[0, 2].middle()
    send_kind(0, 1)
    seq.turn()
    seq.launch(4)
    attend_kind(0, 0)
    tasks[0, 1].middle()
    send_kind(0, 0)
    ready("hid")
    out_end(0)
    out_end(1)
    seq.turn()
    context_back(1)
    ready("ctx")
    out_grad()
    mid.launch(0)
    tasks[0, 0].middle()
    ready("own", "dhid", "win", "vec")
    attend_kind(1, 2)
    end_kind(0, 2)
    send_kind(1, 2)
    seq.turn()
    final_start(KINDS, 0)
    final_start(KINDS, 1)
    attend_kind(1, 1)
    end_kind(0, 1)
    tasks[1, 2].middle()
    send_kind(1, 1)
    seq.turn()
    attend_kind(1, 0)
    end_kind(0, 0)
    tasks[1, 1].middle()
    send_kind(1, 0)
    mid.turn()
    seq.turn()
    final_start(2, 0)
    ready("normed")
    late_kv()
    tasks[1, 0].middle()
    late_query()
    tail.launch(0)
    results[KINDS, 0].middle()
    results[KINDS, 1].middle()
    final_start(1, 0)
    mid.turn()
    seq.turn()
    end_kind(1, 2)
    final_start(0, 0)
    end_kind(1, 1)
    results[2, 0].middle()
    mid.turn()
    end_kind(1, 0)
    small_start()
    tail.turn()
    final_start(2, 1)
    small_step(0)
    results[1, 0].middle()
    final_start(1, 1)
    results[0, 0].middle()
    tail.turn()
    final_start(0, 1)
    small_step(1)
    results[2, 1].middle()
    tail.turn()
    for i in range(2, len(friends)):
        small_step(i)
    results[1, 1].middle()
    seq.drain()
    mid.drain()
    tail.drain()
    results[0, 1].middle()
    saves = [
        pltpu.make_async_copy(total_ref, total_hbm, save_sem.at[0]),
        pltpu.make_async_copy(small_ref, small_hbm, save_sem.at[1]),
    ]
    for save in saves:
        save.start()
    for kind in range(FINALS):
        for at in range(2):
            results[kind, at].end()
            sent(kind, at)
    for save in saves:
        save.wait()


def backward_call(saved, boundary, links, slopes, gains, weights):
    normed, own, q, k, v, lse, ctx, ctxn, outp, hid, dhid, datt, gffn, vec, win = saved
    count = lax.axis_size("seq")
    bits = count.bit_length() - 1
    d = normed.shape[-1]
    heads = q.shape[1]
    keys = KINDS * SEG
    width = heads * HEAD
    chunks = gffn.shape[0] + 4 * width // 256
    columns = 256 * chunks
    view = (2,) * bits + (d // count, 256)
    split = (PER_SEG, 2, 2, PART, d)
    any_space = pl.BlockSpec(memory_space=pl.ANY)
    vmem = pl.BlockSpec(memory_space=pltpu.VMEM)
    smem = pl.BlockSpec(memory_space=pltpu.SMEM)
    dma = pltpu.SemaphoreType.DMA
    final = jax.ShapeDtypeStruct((2, PER_DEV, 2, 2, PART, d), BF)
    scratch = [
        pltpu.VMEM(normed.shape, BF),
        pltpu.VMEM(own.shape, BF),
        pltpu.VMEM(q.shape, BF),
        pltpu.VMEM((2, heads, keys, 2 * HEAD), BF),
        pltpu.VMEM(v.shape, BF),
        pltpu.VMEM(lse.shape, F32),
        pltpu.VMEM(ctx.shape, BF),
        pltpu.VMEM(ctxn.shape, F32),
        pltpu.VMEM(dhid.shape, F32),
        pltpu.VMEM(datt.shape, BF),
        pltpu.VMEM((d, 3 * width), BF),
        pltpu.VMEM((width, d), BF),
        pltpu.VMEM((2, heads, SEG, HEAD), BF),
        pltpu.VMEM((SEG, SEG), BF),
        pltpu.VMEM((SEG, SEG), BF),
        pltpu.VMEM((heads, SEG, 2 * HEAD), F32),
        pltpu.VMEM((2, KINDS, SEG, 3 * width), BF),
        [pltpu.VMEM(split, BF) for _ in range(KINDS)],
        [pltpu.VMEM((PER_SEG, 2, PART, d), BF) for _ in range(2 * KINDS + 2)],
        [pltpu.VMEM((PER_SEG, PART, d), BF) for _ in range(2 * KINDS + 2)],
        [pltpu.VMEM(split, BF) for _ in range(2)],
        pltpu.VMEM(hid.shape, F32),
        pltpu.VMEM(hid.shape, BF),
        pltpu.VMEM(win.shape, BF),
        pltpu.VMEM((KINDS, 2, PER_SEG, PART, d), BF),
        pltpu.VMEM((FINALS, 2, PER_DEV, PART, d), BF),
        pltpu.VMEM((chunks,) + view, BF),
        pltpu.VMEM((d // count, columns), F32),
        [pltpu.VMEM((chunks,) + view[i + 1 :], BF) for i in range(bits)],
        pltpu.VMEM((4, 8, d), F32),
        pltpu.VMEM((heads, 8, HEAD), F32),
        pltpu.VMEM((8, d), F32),
        pltpu.VMEM((bits + 2, 8, d), F32),
        dma((20,)),
        dma((2,)),
        dma((2 * KINDS + 2, 2)),
        dma((2 * KINDS + 2, 2)),
        dma((FINALS, 2, 2)),
        dma((FINALS, 2, 2)),
        dma((FINALS, 2)),
        dma((FINALS, 2, PER_SEG)),
        dma((FINALS, 2, PER_DEV)),
        dma((bits, chunks)),
        dma((bits, chunks)),
        dma((bits + 2,)),
        dma((bits + 2,)),
    ]
    return pl.pallas_call(
        backward_kernel,
        out_shape=[
            [final] * FINALS,
            jax.ShapeDtypeStruct((d // count, columns), F32),
            jax.ShapeDtypeStruct((8, d), F32),
        ],
        in_specs=[any_space] * 15 + [smem] * 3 + [vmem] + [any_space] * 4,
        out_specs=[[any_space] * FINALS] + [any_space] * 2,
        scratch_shapes=scratch,
        compiler_params=pltpu.CompilerParams(
            collective_id=2, has_side_effects=True, vmem_limit_bytes=63 << 20
        ),
    )(
        normed,
        own,
        q,
        k,
        v,
        lse,
        ctx,
        ctxn,
        outp,
        hid,
        dhid,
        datt,
        gffn.reshape((gffn.shape[0],) + view),
        win,
        vec,
        boundary,
        links,
        slopes,
        gains,
        *weights,
    )


def per_device(
    inputs,
    memory,
    compressed,
    boundary,
    links,
    gains,
    shifts,
    slopes,
    w_query,
    w_key,
    w_value,
    w_out,
    w_in,
    w_down,
    w_comp,
    cot_out,
    cot_new,
):
    d = inputs.shape[-1]
    rows = inputs.shape[1]
    heads = slopes.shape[0]
    width = heads * HEAD
    ff = w_in.shape[1]
    feats = w_comp.shape[2]
    count = lax.axis_size("seq")
    seq = lax.axis_index("seq")
    tp = lax.axis_index("tp")

    def chunked(array):
        return array.reshape(2, PER_DEV, 2, 2, PART, d)

    *saved, fresh, comp = forward_call(
        [chunked(inputs), chunked(memory), chunked(compressed)],
        chunked(cot_out),
        memory.reshape(2, rows // PART, PART, d),
        cot_new,
        w_comp,
        boundary,
        links,
        slopes,
        gains,
        shifts,
        (w_query, w_key, w_value, w_out, w_in, w_down),
    )
    finals, total, small = backward_call(
        saved, boundary, links, slopes, gains, (w_query, w_key, w_value, w_out)
    )
    vectors = lax.dynamic_slice(small, (0, seq * (d // count)), (4, d // count))
    grad_slopes = lax.dynamic_slice(small, (4, tp * heads), (1, heads))[0]

    def whole(array):
        return array.reshape(2, rows, d)

    pieces, at = [], 0
    for cut in [ff, ff] + [width] * 4:
        pieces.append(total[:, at : at + cut])
        at += cut
    g_in, g_down, g_out, g_key, g_value, g_query = pieces
    return (
        whole(finals[3]),
        whole(finals[0]).astype(F32),
        whole(finals[1]).astype(F32),
        whole(finals[2]).astype(F32),
        fresh,
        vectors[:2],
        vectors[2:],
        grad_slopes,
        g_query,
        g_key,
        g_value,
        g_out.T,
        g_in,
        g_down.T,
        jnp.stack([comp[:, i * feats : (i + 1) * feats] for i in range(3)]),
    )


def solution(mesh):
    in_specs = (
        P(None, "seq", None),
        P(None, "seq", None),
        P(None, "seq", None),
        P(),
        P(),
        P(),
        P(),
        P("tp"),
        P(None, "tp"),
        P(None, "tp"),
        P(None, "tp"),
        P("tp", None),
        P(None, "tp"),
        P("tp", None),
        P(None, None, "tp"),
        P(None, "seq", None),
        P(None, "seq", "tp"),
    )
    out_specs = (
        P(None, "seq", None),
        P(None, "seq", None),
        P(None, "seq", None),
        P(None, "seq", None),
        P(None, "seq", "tp"),
        P(None, "seq"),
        P(None, "seq"),
        P("tp"),
        P("seq", "tp"),
        P("seq", "tp"),
        P("seq", "tp"),
        P("tp", "seq"),
        P("seq", "tp"),
        P("tp", "seq"),
        P(None, "seq", "tp"),
    )
    return jax.shard_map(
        per_device, mesh=mesh, in_specs=in_specs, out_specs=out_specs, check_vma=False
    )
```
